256 devices in a mesh: ctx: 32 (over z, x), dp: 8 (over y, core).
Axes of the slice: x: 4, y: 4, z: 8, core: 2. Of those that a mesh axis runs over, the one named last changes fastest.
Arguments:
- query: bfloat16 [8, 32, 2, 64, 4096], P('dp', 'ctx'), may hold values from -42 to 42, as said below
- key: bfloat16 [8, 32, 2, 64, 1024], P('dp', 'ctx'), may hold values from -4 to 4, as said below
- value: bfloat16 [8, 32, 2, 64, 1024], P('dp', 'ctx'), may hold values from -6 to 6
- beacon_slot_state: bfloat16 [8, 32, 2, 8, 4096], P('dp', 'ctx'), may hold values from -6 to 6
- frozen_beacon_cache: bfloat16 [8, 32, 2, 8, 2048], P('dp', 'ctx'), may hold values from -6 to 6
- adapter_down_weight: bfloat16 [4096, 64], replicated, may hold values from -0.09375 to 0.09375
- adapter_up_weight: bfloat16 [64, 2048], replicated, may hold values from -0.75 to 0.75
- output_cotangent: bfloat16 [8, 32, 2, 64, 4096], P('dp', 'ctx'), may hold values from -6 to 6
- span_beacon_count: int32 [8, 32, 2], P('dp', 'ctx'), may hold values from 1 to 8, as said below
- span_document: int32 [8, 32, 2], P('dp', 'ctx'), may hold values from 0 to 4, as said below
- boundary: int32 [8, 32, 2], P('dp', 'ctx'), may hold values from 1 to 64, as said below
Outputs:
- attended: bfloat16 [8, 32, 2, 64, 4096], P('dp', 'ctx')
- grad_query: bfloat16 [8, 32, 2, 64, 4096], P('dp', 'ctx')
- grad_key: bfloat16 [8, 32, 2, 64, 1024], P('dp', 'ctx')
- grad_value: bfloat16 [8, 32, 2, 64, 1024], P('dp', 'ctx')
- beacon_cache_gradient: bfloat16 [8, 32, 2, 8, 2048], P('dp', 'ctx')
- adapter_gradient: float32 [64, 6144], replicated
The draws below stay inside these ranges and needn't reach their ends.
Inputs may be any that keep to these rules, and one draw needn't show every extreme that they name: `span_beacon_count`: the two spans of one pair index hold at most 12 beacons together; in every sequence one pair holds exactly 8 and 4. `span_document`: document numbers start at 0 in span 0 and rise by 0 or 1 from span c to span c + 1 in natural span order; every sequence reaches the largest. Every span that is not the last of its document has boundary 64. `query`: queries are real values. `key`: keys are real values.
All inputs are finite; a program needn't handle non-finite values.
Results may differ from the reference program's by a relative error of at most 0.02.
Values may be sent and summed in bfloat16 or wider, within the bound.
No kernel may reach another device: no remote copies, remote signals or barrier semaphores. Data moves between devices by JAX's collectives and lax.ppermute only.
A program may use at most 128 MiB of HBM per device.

```python
import jax
import jax.numpy as jnp
from jax import lax

MODEL_WIDTH = 4096
H = 32
KVH = 8
HD = 128
SPAN = 64
MAX_BEACONS = 8
UPDATE_RANK = 64
PAIRB = 12
GROUP = 4
QW = 4096
KEY_FEATURES = 1024
SPAN_PAIRS = 32
NCH = 64
BATCH = 8


def key_field(key):
    shape = (BATCH, SPAN_PAIRS, 2, SPAN, KEY_FEATURES)
    return jnp.clip(jax.random.normal(jax.random.fold_in(key, 11), shape, jnp.float32), -4.0, 4.0)


def draw_key(key, part):
    return key_field(key).astype(jnp.bfloat16)


def draw_query(key, part):
    shape = (BATCH, SPAN_PAIRS, 2, SPAN, H * HD)
    return jnp.clip(jax.random.normal(jax.random.fold_in(key, 12), shape, jnp.float32), -4.0, 4.0).astype(jnp.bfloat16)


def draw_span_beacon_count(key, part):
    first = jax.random.randint(jax.random.fold_in(key, 21), (BATCH, SPAN_PAIRS), 1, MAX_BEACONS + 1)
    second = jax.random.randint(jax.random.fold_in(key, 22), (BATCH, SPAN_PAIRS), 1, jnp.minimum(MAX_BEACONS, PAIRB - first) + 1)
    chosen = jax.random.randint(jax.random.fold_in(key, 23), (BATCH, 1), 0, SPAN_PAIRS)
    full_pair = jnp.arange(SPAN_PAIRS)[None, :] == chosen
    first = jnp.where(full_pair, MAX_BEACONS, first)
    second = jnp.where(full_pair, PAIRB - MAX_BEACONS, second)
    return jnp.stack([first, second], axis=-1).astype(jnp.int32)


def document_layout(key):
    start_count = max(1, NCH // 16)
    row_keys = jax.random.split(jax.random.fold_in(key, 31), BATCH)
    orders = jax.vmap(lambda row_key: jax.random.permutation(row_key, NCH - 2))(row_keys)
    picked = orders[:, :start_count] + 2
    span_ids = jnp.arange(NCH)
    starts = jnp.any(span_ids[None, None, :] == picked[:, :, None], axis=1)
    doc_ids = jnp.cumsum(starts.astype(jnp.int32), axis=1)
    ends_here = jnp.concatenate([starts[:, 1:], jnp.ones((BATCH, 1), jnp.bool_)], axis=1)
    tails = jax.random.randint(jax.random.fold_in(key, 32), (BATCH, NCH), 1, SPAN + 1)
    live_count = jnp.where(ends_here, tails, SPAN)
    pair_ids = jnp.arange(SPAN_PAIRS)
    folded = jnp.stack([pair_ids, NCH - 1 - pair_ids], axis=1)
    return (doc_ids[:, folded].astype(jnp.int32), live_count[:, folded].astype(jnp.int32))


def draw_span_document(key, part):
    return document_layout(key)[0]


def draw_boundary(key, part):
    return document_layout(key)[1]


def levels(key, extent, cuts, least, high):
    loudness, own = 1.0, jax.random.fold_in(key, 6)
    for dim, blocks in cuts:
        steps = jnp.exp(jax.random.uniform(jax.random.fold_in(own, dim), (blocks,), jnp.float32, least / len(cuts), high / len(cuts)))
        loudness = loudness * jnp.repeat(steps, extent[dim] // blocks).reshape([-1 if axis == dim else 1 for axis in range(len(extent))])
    return loudness


def centred(own_key, dims, scale, most, pieces=(), held_as=jnp.bfloat16):
    result = scale * jax.random.normal(own_key, dims, jnp.float32)
    if pieces:
        result = result * levels(own_key, dims, pieces, -0.22, 0.18)
    return jnp.clip(result, -most, most).astype(held_as)


def setup_inputs(seed: int = 0) -> dict:
    streams_of = jax.random.split(jax.random.key(seed), 12)
    query = draw_query(jax.random.fold_in(streams_of[11], 71), 0)
    key = draw_key(jax.random.fold_in(streams_of[11], 71), 0)
    value = centred(streams_of[2], (BATCH, SPAN_PAIRS, 2, SPAN, KEY_FEATURES), 1.0, 6.0, ((0, 8), (1, 32)))
    beacon_slot_state = centred(streams_of[3], (BATCH, SPAN_PAIRS, 2, MAX_BEACONS, MODEL_WIDTH), 1.0, 6.0, ((0, 8), (1, 32)))
    frozen_beacon_cache = centred(streams_of[4], (BATCH, SPAN_PAIRS, 2, MAX_BEACONS, 2 * KEY_FEATURES), 1.0, 6.0, ((0, 8), (1, 32)))
    adapter_down_weight = centred(streams_of[5], (MODEL_WIDTH, UPDATE_RANK), MODEL_WIDTH ** -0.5, 0.09375)
    adapter_up_weight = centred(streams_of[6], (UPDATE_RANK, 2 * KEY_FEATURES), UPDATE_RANK ** -0.5, 0.75)
    output_cotangent = centred(streams_of[7], (BATCH, SPAN_PAIRS, 2, SPAN, QW), 1.0, 6.0, ((0, 8), (1, 32)))
    span_beacon_count = draw_span_beacon_count(jax.random.fold_in(streams_of[11], 71), 0)
    span_document = draw_span_document(jax.random.fold_in(streams_of[11], 71), 0)
    boundary = draw_boundary(jax.random.fold_in(streams_of[11], 71), 0)
    return dict(query=query, key=key, value=value, beacon_slot_state=beacon_slot_state, frozen_beacon_cache=frozen_beacon_cache, adapter_down_weight=adapter_down_weight, adapter_up_weight=adapter_up_weight, output_cotangent=output_cotangent, span_beacon_count=span_beacon_count, span_document=span_document, boundary=boundary)


masked_score = -1e30


def rounded(values):
    return lax.optimization_barrier(values.astype(jnp.bfloat16)).astype(jnp.float32)


def attend(query, key, value, output_cotangent, beacon_states, own_span, own_doc, live_lengths, slot_span, slot_doc):
    score_scale = HD ** -0.5
    positions = jnp.arange(SPAN)
    live_rows = positions[None, :] < live_lengths[:, None]
    near_mask = (positions[None, None, :] <= positions[None, :, None]) & (live_rows[:, :, None] == live_rows[:, None, :])
    far_mask = live_rows[:, :, None] & (slot_span[None, None, :] < own_span[:, None, None]) & (slot_doc[None, None, :] == own_doc[:, None, None])
    visible = jnp.concatenate([near_mask, far_mask], axis=2)[:, None, None]
    query_heads = query.astype(jnp.float32).reshape(2, SPAN, KVH, GROUP, HD)
    key_heads = key.astype(jnp.float32).reshape(2, SPAN, KVH, HD)
    value_heads = value.astype(jnp.float32).reshape(2, SPAN, KVH, HD)
    grad_heads = output_cotangent.astype(jnp.float32).reshape(2, SPAN, KVH, GROUP, HD)
    beacon_keys = beacon_states[:, :KEY_FEATURES].astype(jnp.float32).reshape(-1, KVH, HD)
    beacon_values = beacon_states[:, KEY_FEATURES:].astype(jnp.float32).reshape(-1, KVH, HD)
    scores = jnp.concatenate([jnp.einsum('sqgmd,skgd->sgmqk', query_heads, key_heads), jnp.einsum('sqgmd,kgd->sgmqk', query_heads, beacon_keys)], axis=4) * score_scale
    scores = jnp.where(visible, scores, masked_score)
    row_max = jnp.max(scores, axis=4, keepdims=True)
    log_total = row_max + jnp.log(jnp.sum(jnp.exp(scores - row_max), axis=4, keepdims=True))
    probs_exact = jnp.exp(scores - log_total)
    probs = rounded(probs_exact)
    near_probs = probs[..., :SPAN]
    far_probs = probs[..., SPAN:]
    summed = jnp.einsum('sgmqk,skgd->sqgmd', near_probs, value_heads) + jnp.einsum('sgmqk,kgd->sqgmd', far_probs, beacon_values)
    attended = summed.astype(jnp.bfloat16)
    attended_heads = lax.optimization_barrier(attended).astype(jnp.float32)
    row_delta = jnp.transpose(jnp.sum(grad_heads * attended_heads, axis=4), (0, 2, 3, 1))[..., None]
    grad_probs = jnp.concatenate([jnp.einsum('sqgmd,skgd->sgmqk', grad_heads, value_heads), jnp.einsum('sqgmd,kgd->sgmqk', grad_heads, beacon_values)], axis=4)
    grad_scores = rounded(probs_exact * (grad_probs - row_delta))
    near_grads = grad_scores[..., :SPAN]
    far_grads = grad_scores[..., SPAN:]
    grad_query = (jnp.einsum('sgmqk,skgd->sqgmd', near_grads, key_heads) + jnp.einsum('sgmqk,kgd->sqgmd', far_grads, beacon_keys)) * score_scale
    grad_key = jnp.einsum('sgmqk,sqgmd->skgd', near_grads, query_heads) * score_scale
    grad_value = jnp.einsum('sgmqk,sqgmd->skgd', near_probs, grad_heads)
    slot_keys = jnp.einsum('sgmqk,sqgmd->kgd', far_grads, query_heads) * score_scale
    slot_values = jnp.einsum('sgmqk,sqgmd->kgd', far_probs, grad_heads)
    slot_term = jnp.concatenate([slot_keys.reshape(-1, KEY_FEATURES), slot_values.reshape(-1, KEY_FEATURES)], axis=1)
    return (attended.reshape(2, SPAN, QW), grad_query.astype(jnp.bfloat16).reshape(2, SPAN, QW), grad_key.astype(jnp.bfloat16).reshape(2, SPAN, KEY_FEATURES), grad_value.astype(jnp.bfloat16).reshape(2, SPAN, KEY_FEATURES), slot_term)


def reference(query, key, value, beacon_slot_state, frozen_beacon_cache, adapter_down_weight, adapter_up_weight, output_cotangent, span_beacon_count, span_document, boundary):
    pair_ids = jnp.arange(SPAN_PAIRS)
    own_spans = jnp.stack([pair_ids, NCH - 1 - pair_ids], axis=1).astype(jnp.int32)

    def sequence_results(adapter_gradient_sum, sequence_entries):
        seq_query, seq_key, seq_value, seq_hidden, seq_base, seq_grad, counts, doc_ids, live_lengths = sequence_entries
        flattened_state = seq_hidden.reshape(-1, MODEL_WIDTH)
        reduced_state = jnp.dot(flattened_state, adapter_down_weight, preferred_element_type=jnp.float32).astype(jnp.bfloat16)
        weight_update = jnp.dot(reduced_state, adapter_up_weight, preferred_element_type=jnp.float32)
        states = (seq_base.reshape(-1, 2 * KEY_FEATURES).astype(jnp.float32) + weight_update).astype(jnp.bfloat16)
        valid_slots = jnp.arange(MAX_BEACONS)[None, None, :] < counts[:, :, None]
        slot_span = jnp.broadcast_to(own_spans[:, :, None], (SPAN_PAIRS, 2, MAX_BEACONS)).reshape(-1).astype(jnp.int32)
        slot_doc = jnp.where(valid_slots, doc_ids[:, :, None], -1).reshape(-1).astype(jnp.int32)

        def per_device(running_sum, device_items):
            dev_query, dev_key, dev_value, dev_grad, dev_span, dev_doc, dev_live = device_items
            attended, grad_query, grad_key, grad_value, slot_term = attend(dev_query, dev_key, dev_value, dev_grad, states, dev_span, dev_doc, dev_live, slot_span, slot_doc)
            return running_sum + slot_term, (attended, grad_query, grad_key, grad_value)

        running_sum, result_list = lax.scan(per_device, jnp.zeros((SPAN_PAIRS * 2 * MAX_BEACONS, 2 * KEY_FEATURES), jnp.float32), (seq_query, seq_key, seq_value, seq_grad, own_spans, doc_ids, live_lengths))
        beacon_cache_gradient = running_sum.astype(jnp.bfloat16)
        reduced_gradient = jnp.dot(beacon_cache_gradient, adapter_up_weight.T, preferred_element_type=jnp.float32).astype(jnp.bfloat16)
        down_factor_term = jnp.dot(reduced_gradient.T, flattened_state, preferred_element_type=jnp.float32)
        up_factor_term = jnp.dot(reduced_state.T, beacon_cache_gradient, preferred_element_type=jnp.float32)
        adapter_gradient_sum = adapter_gradient_sum + jnp.concatenate([down_factor_term, up_factor_term], axis=1)
        return adapter_gradient_sum, result_list + (beacon_cache_gradient.reshape(SPAN_PAIRS, 2, MAX_BEACONS, 2 * KEY_FEATURES),)

    adapter_gradient, output_list = lax.scan(sequence_results, jnp.zeros((UPDATE_RANK, MODEL_WIDTH + 2 * KEY_FEATURES), jnp.float32), (query, key, value, beacon_slot_state, frozen_beacon_cache, output_cotangent, span_beacon_count, span_document, boundary))
    return (output_list[0], output_list[1], output_list[2], output_list[3], output_list[4], adapter_gradient)
```

```python
import functools

import jax
import jax.numpy as jnp
from jax import lax
from jax.experimental import pallas as pl
from jax.experimental.pallas import tpu as pltpu
from jax.sharding import Mesh, PartitionSpec as P

MODEL_WIDTH = 4096
KVH = 8
HD = 128
SPAN = 64
MAX_BEACONS = 8
UPDATE_RANK = 64
GROUP = 4
QW = 4096
KEY_FEATURES = 1024
NCH = 64
NZ, NX, NY, NC = 8, 4, 4, 2

bf16 = jnp.bfloat16
f32 = jnp.float32
ALL_AXES = ("z", "x", "y", "core")
WIDE = ("x", "y", "core")

TILES = 26
GRAD_TILES = 24
FAR = 384
NEAR = 128
KEYS = FAR + NEAR
ROWS = GROUP * 2 * SPAN
MASKED = -1e30
SCORE_SCALE = HD ** (-0.5)
LOG2E = 1.4426950408889634


def dot(a, b, dims=((1,), (0,))):
    return lax.dot_general(a, b, (dims, ((), ())), preferred_element_type=f32)


def selection(first, second):
    row = lax.broadcasted_iota(jnp.int32, (16, 16), 0)
    slot = lax.broadcasted_iota(jnp.int32, (16, 16), 1)
    source = jnp.where(row < first, row, row - first + MAX_BEACONS)
    return jnp.where((slot == source) & (row < first + second), 1.0, 0.0)


def project_kernel(info, state, down, up, frozen, out, low_out):
    first, second = info[0], info[1]
    low = dot(state[...], down[...]).astype(bf16)
    low_out[...] = low
    states = (frozen[...].astype(f32) + dot(low, up[...])).astype(bf16)
    pick = selection(first, second).astype(bf16)
    rows = dot(pick, states)
    low_rows = dot(pick, low).astype(bf16)
    sub = lax.broadcasted_iota(jnp.int32, (8, HD), 0)
    tiles = []
    for h in range(2 * KVH):
        tiles.append(rows[:8, h * HD : (h + 1) * HD])
    for h in range(KVH):
        keys = rows[8:, h * HD : (h + 1) * HD]
        values = rows[8:, (KVH + h) * HD : (KVH + h + 1) * HD]
        tiles.append(jnp.where(sub < 4, keys, pltpu.roll(values, 4, 0)))
    put_row = lax.broadcasted_iota(jnp.int32, (UPDATE_RANK, HD), 0)
    put_col = lax.broadcasted_iota(jnp.int32, (UPDATE_RANK, HD), 1)
    left = jnp.where(put_row == put_col, 1.0, 0.0).astype(bf16)
    right = jnp.where(put_row + UPDATE_RANK == put_col, 1.0, 0.0).astype(bf16)
    tiles.append((dot(low_rows, left)[:8] + dot(low_rows, right)[8:]))
    facts = jnp.zeros((8, HD), f32)
    for i in range(4):
        facts = jnp.where(sub == i, info[i].astype(f32), facts)
    tiles.append(facts)
    for t, tile in enumerate(tiles):
        packed = tile.astype(bf16)
        for z in range(NZ):
            out[z, t] = packed


def project(info, state, down, up, frozen):
    vmem = pl.BlockSpec(memory_space=pltpu.VMEM)
    return pl.pallas_call(
        project_kernel,
        in_specs=[pl.BlockSpec(memory_space=pltpu.SMEM)] + [vmem] * 4,
        out_specs=[vmem, vmem],
        out_shape=[
            jax.ShapeDtypeStruct((NZ, TILES, 8, HD), bf16),
            jax.ShapeDtypeStruct((16, UPDATE_RANK), bf16),
        ],
        name="project",
    )(info, state, down, up, frozen)


def fill_bias(info, boxes, bias):
    z_own, x_own = info[0], info[1]
    pair = z_own * NX + x_own
    lane = lax.broadcasted_iota(jnp.int32, (8, NEAR), 1)
    sub = lax.broadcasted_iota(jnp.int32, (8, NEAR), 0)
    side = lane // SPAN
    offset = lane % SPAN
    own_span = jnp.where(side == 0, pair, NCH - 1 - pair).astype(f32)
    own_doc = jnp.where(side == 0, info[2], info[3]).astype(f32)
    live = offset < jnp.where(side == 0, info[4], info[5])
    for block in range(NEAR // 8):
        key_side = block * 8 // SPAN
        key_offset = sub + (block * 8) % SPAN
        key_live = key_offset < info[4 + key_side]
        seen = (side == key_side) & (key_offset <= offset) & (key_live == live)
        bias[block * 8 : block * 8 + 8, :] = jnp.where(seen, 0.0, MASKED)

    def facts(box, z, slot):
        tile = boxes[box][z, 25].astype(f32)
        first, second = tile[0:1], tile[1:2]
        first_doc, second_doc = tile[2:3], tile[3:4]
        source = z * NX + lax.rem(x_own - box + NX, NX)
        low = slot < first
        high = slot < first + second
        span = jnp.where(low, source, NCH - 1 - source).astype(f32)
        doc = jnp.where(low, first_doc, second_doc)
        return jnp.where(high, span, 2.0 * NCH), doc

    def write(at, span, doc):
        seen = live & (span < own_span) & (doc == own_doc)
        bias[at : at + 8, :] = jnp.where(seen, 0.0, MASKED)

    slot = sub.astype(f32)
    for box in range(NX):
        for z in range(NZ):
            write(NEAR + box * 64 + z * 8, *facts(box, z, slot))
        for z in range(0, NZ, 2):
            span_a, doc_a = facts(box, z, slot + 8.0)
            span_b, doc_b = facts(box, z + 1, slot + 4.0)
            write(
                NEAR + 256 + box * 32 + z * 4,
                jnp.where(sub < 4, span_a, span_b),
                jnp.where(sub < 4, doc_a, doc_b),
            )


def attend_kernel(
    info, query, key, value, grad, box0, box1, box2, box3,
    attended, grad_query, grad_key, grad_value, out0, out1, out2, out3, bias,
):
    boxes = (box0, box1, box2, box3)
    outs = (out0, out1, out2, out3)
    g = pl.program_id(0)

    @pl.when(g == 0)
    def _():
        fill_bias(info, boxes, bias)

    sub = lax.broadcasted_iota(jnp.int32, (NZ // 2, 8, HD), 1)

    def stack(ref):
        whole = ref[...].reshape(2 * SPAN, GROUP * HD)
        return jnp.concatenate(
            [whole[:, m * HD : (m + 1) * HD] for m in range(GROUP)], axis=0
        )

    def far_rows(tile):
        return [box[:, tile].astype(f32).reshape(8 * NZ, HD) for box in boxes]

    extra_keys, extra_values = [], []
    for box in boxes:
        both = box[:, 16 + g].astype(f32).reshape(NZ // 2, 2, 8, HD)
        even, odd = both[:, 0], both[:, 1]
        extra_keys.append(jnp.where(sub < 4, even, pltpu.roll(odd, 4, 1)).reshape(4 * NZ, HD))
        extra_values.append(jnp.where(sub < 4, pltpu.roll(even, 4, 1), odd).reshape(4 * NZ, HD))
    keys = jnp.concatenate(
        [key[...].reshape(NEAR, HD).astype(f32)] + far_rows(g) + extra_keys, axis=0
    )
    values = jnp.concatenate(
        [value[...].reshape(NEAR, HD).astype(f32)] + far_rows(KVH + g) + extra_values, axis=0
    )
    keys_t = keys.T.astype(bf16)
    values_t = values.T.astype(bf16)
    keys = keys.astype(bf16)
    values = values.astype(bf16)
    queries = stack(query)
    grads = stack(grad)
    grads_t = grads.astype(f32).T

    scores = dot(keys, queries, ((1,), (1,))) * (SCORE_SCALE * LOG2E)
    scores = scores + jnp.tile(bias[...], (1, GROUP))
    top = jnp.max(scores, axis=0, keepdims=True)
    weights = jnp.exp2(scores - top)
    total = jnp.sum(weights, axis=0, keepdims=True)
    exact = weights * (1.0 / total)
    probs = exact.astype(bf16)
    summed_t = dot(values_t, probs)
    summed = summed_t.T.astype(bf16)
    rounded_t = summed_t.astype(bf16).astype(f32)
    delta = jnp.sum(grads_t * rounded_t, axis=0, keepdims=True)
    grad_probs = dot(values, grads_t.astype(bf16))
    grad_scores = (exact * (grad_probs - delta)).astype(bf16)
    query_grad = (dot(keys_t, grad_scores) * SCORE_SCALE).T.astype(bf16)
    key_grad = dot(grad_scores, queries) * SCORE_SCALE
    value_grad = dot(probs, grads)

    for m in range(GROUP):
        at = slice(m * 2 * SPAN, (m + 1) * 2 * SPAN)
        cols = slice(m * HD, (m + 1) * HD)
        attended[:, :, cols] = summed[at].reshape(2, SPAN, HD)
        grad_query[:, :, cols] = query_grad[at].reshape(2, SPAN, HD)
    grad_key[...] = key_grad[:NEAR].astype(bf16).reshape(2, SPAN, HD)
    grad_value[...] = value_grad[:NEAR].astype(bf16).reshape(2, SPAN, HD)
    for b, out in enumerate(outs):
        at = NEAR + b * 64
        out[:, 0, 0] = key_grad[at : at + 64].reshape(NZ, 8, HD).astype(bf16)
        out[:, 1, 0] = value_grad[at : at + 64].reshape(NZ, 8, HD).astype(bf16)
        at = NEAR + 256 + b * 32
        k = key_grad[at : at + 32].reshape(NZ // 2, 8, HD)
        v = value_grad[at : at + 32].reshape(NZ // 2, 8, HD)
        even = jnp.where(sub < 4, k, pltpu.roll(v, 4, 1)).astype(bf16)
        odd = jnp.where(sub < 4, pltpu.roll(k, 4, 1), v).astype(bf16)
        for i in range(NZ // 2):
            out[2 * i, 2, 0] = even[i]
            out[2 * i + 1, 2, 0] = odd[i]


def attend(info, query, key, value, grad, boxes):
    wide = pl.BlockSpec((2, SPAN, GROUP * HD), lambda g: (0, 0, g))
    narrow = pl.BlockSpec((2, SPAN, HD), lambda g: (0, 0, g))
    whole = pl.BlockSpec((NZ, TILES, 8, HD), lambda g: (0, 0, 0, 0))
    part = pl.BlockSpec((NZ, 3, 1, 8, HD), lambda g: (0, 0, g, 0, 0))
    wide_shape = jax.ShapeDtypeStruct((2, SPAN, QW), bf16)
    narrow_shape = jax.ShapeDtypeStruct((2, SPAN, KEY_FEATURES), bf16)
    part_shape = jax.ShapeDtypeStruct((NZ, 3, KVH, 8, HD), bf16)
    return pl.pallas_call(
        attend_kernel,
        grid=(KVH,),
        in_specs=[pl.BlockSpec(memory_space=pltpu.SMEM), wide, narrow, narrow, wide] + [whole] * NX,
        out_specs=[wide, wide, narrow, narrow] + [part] * NX,
        out_shape=[wide_shape, wide_shape, narrow_shape, narrow_shape] + [part_shape] * NX,
        scratch_shapes=[pltpu.VMEM((KEYS, NEAR), f32)],
        compiler_params=pltpu.CompilerParams(vmem_limit_bytes=48 * 1024 * 1024),
        name="attend",
    )(info, query, key, value, grad, *boxes)


def finish_kernel(info, parts, up, state, low, cache_out, pieces):
    pick = selection(info[0], info[1]).astype(bf16)
    total = jnp.sum(parts[...].astype(f32), axis=0)
    sub = lax.broadcasted_iota(jnp.int32, (8, HD), 0)
    tops = [total[h] for h in range(2 * KVH)]
    rest_keys, rest_values = [], []
    for h in range(KVH):
        both = total[16 + h]
        rest_keys.append(jnp.where(sub < 4, both, 0.0))
        rest_values.append(jnp.where(sub < 4, pltpu.roll(both, 4, 0), 0.0))
    compact = jnp.concatenate(
        [jnp.concatenate(tops, axis=1), jnp.concatenate(rest_keys + rest_values, axis=1)], axis=0
    ).astype(bf16)
    cache = dot(pick, compact, ((0,), (0,))).astype(bf16)
    cache_out[...] = cache
    low_grad = dot(cache, up[...], ((1,), (1,))).astype(bf16)
    down_piece = dot(low_grad, state[...], ((0,), (0,)))
    up_piece = dot(low[...], cache, ((0,), (0,)))
    per_row = (MODEL_WIDTH + 2 * KEY_FEATURES) // HD
    for t in range(8 * per_row):
        r, c = divmod(t, per_row)
        if c < MODEL_WIDTH // HD:
            tile = down_piece[r * 8 : r * 8 + 8, c * HD : (c + 1) * HD]
        else:
            c -= MODEL_WIDTH // HD
            tile = up_piece[r * 8 : r * 8 + 8, c * HD : (c + 1) * HD]
        pieces[t // 12, t % 12] = tile.astype(bf16)


def finish(info, parts, up, state, low):
    vmem = pl.BlockSpec(memory_space=pltpu.VMEM)
    return pl.pallas_call(
        finish_kernel,
        in_specs=[pl.BlockSpec(memory_space=pltpu.SMEM)] + [vmem] * 4,
        out_specs=[vmem, vmem],
        out_shape=[
            jax.ShapeDtypeStruct((16, 2 * KEY_FEATURES), bf16),
            jax.ShapeDtypeStruct((32, 12, 8, HD), bf16),
        ],
        name="finish",
    )(info, parts, up, state, low)


def add_kernel(copies, parts, out):
    total = jnp.sum(parts[...].astype(f32), axis=0).astype(bf16)
    for i in range(copies):
        out[i] = total


def add_and_copy(parts, copies, name):
    vmem = pl.BlockSpec(memory_space=pltpu.VMEM)
    return pl.pallas_call(
        functools.partial(add_kernel, copies),
        in_specs=[vmem],
        out_specs=vmem,
        out_shape=jax.ShapeDtypeStruct((copies,) + parts.shape[1:], bf16),
        name=name,
    )(parts)


def add_four_kernel(a, b, c, d, out):
    out[...] = (
        (a[...].astype(f32) + b[...].astype(f32)) + (c[...].astype(f32) + d[...].astype(f32))
    ).astype(bf16)


def add_four(parts):
    vmem = pl.BlockSpec(memory_space=pltpu.VMEM)
    return pl.pallas_call(
        add_four_kernel,
        in_specs=[vmem] * 4,
        out_specs=vmem,
        out_shape=jax.ShapeDtypeStruct(parts[0].shape, bf16),
        name="add_four",
    )(*parts)


def unpack_kernel(tiles, out):
    per_row = (MODEL_WIDTH + 2 * KEY_FEATURES) // HD
    for t in range(8 * per_row):
        r, c = divmod(t, per_row)
        out[r * 8 : r * 8 + 8, c * HD : (c + 1) * HD] = tiles[t // 12, t % 12].astype(f32)


def unpack(tiles):
    vmem = pl.BlockSpec(memory_space=pltpu.VMEM)
    return pl.pallas_call(
        unpack_kernel,
        in_specs=[vmem],
        out_specs=vmem,
        out_shape=jax.ShapeDtypeStruct((UPDATE_RANK, MODEL_WIDTH + 2 * KEY_FEATURES), f32),
        name="unpack",
    )(tiles)


def exchange(x, axes):
    return lax.all_to_all(x, axes, 0, 0, tiled=True)


def shift(x, by):
    return lax.ppermute(x, "x", [(i, (i + by) % NX) for i in range(NX)])


def local(
    query, key, value, beacon_slot_state, frozen_beacon_cache, adapter_down_weight,
    adapter_up_weight, output_cotangent, span_beacon_count, span_document, boundary,
):
    counts = span_beacon_count[0, 0]
    docs = span_document[0, 0]
    ends = boundary[0, 0]
    z_own = lax.axis_index("z").astype(jnp.int32)
    x_own = lax.axis_index("x").astype(jnp.int32)
    state = beacon_slot_state[0, 0].reshape(2 * MAX_BEACONS, MODEL_WIDTH)
    frozen = frozen_beacon_cache[0, 0].reshape(2 * MAX_BEACONS, 2 * KEY_FEATURES)
    pair_info = jnp.concatenate([counts, docs])
    place_info = jnp.concatenate([jnp.stack([z_own, x_own]), docs, ends])

    message, low = project(pair_info, state, adapter_down_weight, adapter_up_weight, frozen)
    column = exchange(message, "z")
    boxes = [column, shift(column, 1), shift(column, 2), shift(column, 3)]
    attended, grad_query, grad_key, grad_value, *parts = attend(
        place_info, query[0, 0], key[0, 0], value[0, 0], output_cotangent[0, 0], boxes
    )
    parts = [p.reshape(NZ, GRAD_TILES, 8, HD) for p in parts]
    mine = add_four([parts[0], shift(parts[1], -1), shift(parts[2], -2), shift(parts[3], -3)])
    cache_gradient, pieces = finish(
        pair_info, exchange(mine, "z"), adapter_up_weight, state, low
    )
    wide = add_and_copy(exchange(pieces, WIDE), NZ, "add_wide")
    full = add_and_copy(exchange(wide, "z"), 32, "add_z")
    adapter_gradient = unpack(exchange(full, WIDE))
    return (
        attended[None, None],
        grad_query[None, None],
        grad_key[None, None],
        grad_value[None, None],
        cache_gradient.reshape(1, 1, 2, MAX_BEACONS, 2 * KEY_FEATURES),
        adapter_gradient,
    )


def solution(mesh):
    chips = Mesh(mesh.devices.reshape(NZ, NX, NY, NC), ALL_AXES)
    dp, ctx = ("y", "core"), ("z", "x")
    array5 = P(dp, ctx, None, None, None)
    array3 = P(dp, ctx, None)
    return jax.shard_map(
        local,
        mesh=chips,
        in_specs=(array5, array5, array5, array5, array5, P(), P(), array5, array3, array3, array3),
        out_specs=(array5, array5, array5, array5, array5, P()),
        check_vma=False,
    )
```

```python
import jax
import jax.numpy as jnp
from jax import lax
from jax.experimental import pallas as pl
from jax.experimental.pallas import tpu as pltpu
from jax.sharding import Mesh, PartitionSpec as P

MODEL_WIDTH = 4096
KVH = 8
HD = 128
SPAN = 64
MAX_BEACONS = 8
UPDATE_RANK = 64
GROUP = 4
QW = 4096
KEY_FEATURES = 1024
NCH = 64
NZ, NX, NY, NC = 8, 4, 4, 2

bf16 = jnp.bfloat16
f32 = jnp.float32
ALL_AXES = ("z", "x", "y", "core")
WIDE = ("x", "y", "core")

TILES = 26
GRAD_TILES = 24
FAR = 384
NEAR = 128
KEYS = FAR + NEAR
ROWS = GROUP * 2 * SPAN
MASKED = -1e30
SCORE_SCALE = HD ** (-0.5)
LOG2E = 1.4426950408889634


def dot(a, b, dims=((1,), (0,))):
    return lax.dot_general(a, b, (dims, ((), ())), preferred_element_type=f32)


def selection(first, second):
    row = lax.broadcasted_iota(jnp.int32, (16, 16), 0)
    slot = lax.broadcasted_iota(jnp.int32, (16, 16), 1)
    source = jnp.where(row < first, row, row - first + MAX_BEACONS)
    return jnp.where((slot == source) & (row < first + second), 1.0, 0.0)


def project_kernel(counts, docs, state, down_t, up, frozen, out):
    first, second = counts[0, 0, 0], counts[0, 0, 1]
    low = dot(state[...], down_t[...], ((1,), (1,))).astype(bf16)
    states = (frozen[...].astype(f32) + dot(low, up[...])).astype(bf16)
    pick = selection(first, second).astype(bf16)
    rows = dot(pick, states)
    low_rows = dot(pick, low).astype(bf16)
    sub = lax.broadcasted_iota(jnp.int32, (8, HD), 0)
    tiles = []
    for h in range(2 * KVH):
        tiles.append(rows[:8, h * HD : (h + 1) * HD])
    for h in range(KVH):
        keys = rows[8:, h * HD : (h + 1) * HD]
        values = rows[8:, (KVH + h) * HD : (KVH + h + 1) * HD]
        tiles.append(jnp.where(sub < 4, keys, pltpu.roll(values, 4, 0)))
    put_row = lax.broadcasted_iota(jnp.int32, (UPDATE_RANK, HD), 0)
    put_col = lax.broadcasted_iota(jnp.int32, (UPDATE_RANK, HD), 1)
    left = jnp.where(put_row == put_col, 1.0, 0.0).astype(bf16)
    right = jnp.where(put_row + UPDATE_RANK == put_col, 1.0, 0.0).astype(bf16)
    tiles.append((dot(low_rows, left)[:8] + dot(low_rows, right)[8:]))
    facts = jnp.zeros((8, HD), f32)
    for i, fact in enumerate((first, second, docs[0, 0, 0], docs[0, 0, 1])):
        facts = jnp.where(sub == i, fact.astype(f32), facts)
    tiles.append(facts)
    for t, tile in enumerate(tiles):
        packed = tile.astype(bf16)
        for z in range(NZ):
            out[z, t] = packed


VMEM = pl.BlockSpec(memory_space=pltpu.VMEM)
SMEM = pl.BlockSpec(memory_space=pltpu.SMEM)


def project(counts, docs, state, down_t, up, frozen):
    return pl.pallas_call(
        project_kernel,
        in_specs=[SMEM] * 2 + [VMEM] * 4,
        out_specs=VMEM,
        out_shape=jax.ShapeDtypeStruct((NZ, TILES, 8, HD), bf16),
        name="project",
    )(counts, docs, state, down_t, up, frozen)


def fill_bias(place, docs, ends, boxes, bias):
    z_own, x_own = place[0], place[1]
    pair = z_own * NX + x_own
    lane = lax.broadcasted_iota(jnp.int32, (8, NEAR), 1)
    sub = lax.broadcasted_iota(jnp.int32, (8, NEAR), 0)
    side = lane // SPAN
    offset = lane % SPAN
    own_span = jnp.where(side == 0, pair, NCH - 1 - pair).astype(f32)
    own_doc = jnp.where(side == 0, docs[0, 0, 0], docs[0, 0, 1]).astype(f32)
    live = offset < jnp.where(side == 0, ends[0, 0, 0], ends[0, 0, 1])
    for block in range(NEAR // 8):
        key_side = block * 8 // SPAN
        key_offset = sub + (block * 8) % SPAN
        key_live = key_offset < ends[0, 0, key_side]
        seen = (side == key_side) & (key_offset <= offset) & (key_live == live)
        bias[block * 8 : block * 8 + 8, :] = jnp.where(seen, 0.0, MASKED)

    def facts(box, z, slot):
        tile = boxes[box][z, 25].astype(f32)
        first, second = tile[0:1], tile[1:2]
        first_doc, second_doc = tile[2:3], tile[3:4]
        source = z * NX + lax.rem(x_own - box + NX, NX)
        low = slot < first
        high = slot < first + second
        span = jnp.where(low, source, NCH - 1 - source).astype(f32)
        doc = jnp.where(low, first_doc, second_doc)
        return jnp.where(high, span, 2.0 * NCH), doc

    def write(at, span, doc):
        seen = live & (span < own_span) & (doc == own_doc)
        bias[at : at + 8, :] = jnp.where(seen, 0.0, MASKED)

    slot = sub.astype(f32)
    for box in range(NX):
        for z in range(NZ):
            write(NEAR + box * 64 + z * 8, *facts(box, z, slot))
        for z in range(0, NZ, 2):
            span_a, doc_a = facts(box, z, slot + 8.0)
            span_b, doc_b = facts(box, z + 1, slot + 4.0)
            write(
                NEAR + 256 + box * 32 + z * 4,
                jnp.where(sub < 4, span_a, span_b),
                jnp.where(sub < 4, doc_a, doc_b),
            )


def gather_low(boxes, low_all):
    lane = lax.broadcasted_iota(jnp.int32, (NZ, 8, HD), 2)
    sub = lax.broadcasted_iota(jnp.int32, (NZ // 2, 8, HD), 1)
    for b, box in enumerate(boxes):
        tile = box[:, 24].astype(f32)
        head = jnp.where(lane < UPDATE_RANK, tile, 0.0)
        low_all[b * 64 : b * 64 + 64, :] = head.reshape(64, HD).astype(bf16)
        tail = jnp.where(lane < UPDATE_RANK, pltpu.roll(tile, UPDATE_RANK, 2), 0.0)
        tail = tail.reshape(NZ // 2, 2, 8, HD)
        tail = jnp.where(sub < 4, tail[:, 0], pltpu.roll(tail[:, 1], 4, 1))
        at = 256 + b * 32
        low_all[at : at + 32, :] = tail.reshape(32, HD).astype(bf16)


def attend_kernel(
    place, docs, ends, query, key, value, grad, up_key, up_value, box0, box1, box2, box3,
    attended, grad_query, grad_key, grad_value, out0, out1, out2, out3, up_key_part,
    up_value_part, low_part, bias, low_all, low_total,
):
    boxes = (box0, box1, box2, box3)
    outs = (out0, out1, out2, out3)
    g = pl.program_id(0)

    @pl.when(g == 0)
    def _():
        fill_bias(place, docs, ends, boxes, bias)
        gather_low(boxes, low_all)
        low_total[...] = jnp.zeros_like(low_total)

    sub = lax.broadcasted_iota(jnp.int32, (NZ // 2, 8, HD), 1)

    def stack(ref):
        whole = ref[...].reshape(2 * SPAN, GROUP * HD)
        return jnp.concatenate(
            [whole[:, m * HD : (m + 1) * HD] for m in range(GROUP)], axis=0
        )

    def far_rows(tile):
        return [box[:, tile].astype(f32).reshape(8 * NZ, HD) for box in boxes]

    extra_keys, extra_values = [], []
    for box in boxes:
        both = box[:, 16 + g].astype(f32).reshape(NZ // 2, 2, 8, HD)
        even, odd = both[:, 0], both[:, 1]
        extra_keys.append(jnp.where(sub < 4, even, pltpu.roll(odd, 4, 1)).reshape(4 * NZ, HD))
        extra_values.append(jnp.where(sub < 4, pltpu.roll(even, 4, 1), odd).reshape(4 * NZ, HD))
    keys = jnp.concatenate(
        [key[...].reshape(NEAR, HD).astype(f32)] + far_rows(g) + extra_keys, axis=0
    )
    values = jnp.concatenate(
        [value[...].reshape(NEAR, HD).astype(f32)] + far_rows(KVH + g) + extra_values, axis=0
    )
    keys_t = keys.T.astype(bf16)
    values_t = values.T.astype(bf16)
    keys = keys.astype(bf16)
    values = values.astype(bf16)
    queries = stack(query)
    grads = stack(grad)
    grads_t = grads.astype(f32).T

    scores = dot(keys, queries, ((1,), (1,))) * (SCORE_SCALE * LOG2E)
    scores = scores + jnp.tile(bias[...], (1, GROUP))
    top = jnp.max(scores, axis=0, keepdims=True)
    weights = jnp.exp2(scores - top)
    total = jnp.sum(weights, axis=0, keepdims=True)
    exact = weights * (1.0 / total)
    probs = exact.astype(bf16)
    summed_t = dot(values_t, probs)
    summed = summed_t.T.astype(bf16)
    rounded_t = summed_t.astype(bf16).astype(f32)
    delta = jnp.sum(grads_t * rounded_t, axis=0, keepdims=True)
    grad_probs = dot(values, grads_t.astype(bf16))
    grad_scores = (exact * (grad_probs - delta)).astype(bf16)
    query_grad = (dot(keys_t, grad_scores) * SCORE_SCALE).T.astype(bf16)
    key_grad = dot(grad_scores, queries) * SCORE_SCALE
    value_grad = dot(probs, grads)

    for m in range(GROUP):
        at = slice(m * 2 * SPAN, (m + 1) * 2 * SPAN)
        cols = slice(m * HD, (m + 1) * HD)
        attended[:, :, cols] = summed[at].reshape(2, SPAN, HD)
        grad_query[:, :, cols] = query_grad[at].reshape(2, SPAN, HD)
    grad_key[...] = key_grad[:NEAR].astype(bf16).reshape(2, SPAN, HD)
    grad_value[...] = value_grad[:NEAR].astype(bf16).reshape(2, SPAN, HD)
    for b, out in enumerate(outs):
        at = NEAR + b * 64
        out[:, 0, 0] = key_grad[at : at + 64].reshape(NZ, 8, HD).astype(bf16)
        out[:, 1, 0] = value_grad[at : at + 64].reshape(NZ, 8, HD).astype(bf16)
        at = NEAR + 256 + b * 32
        k = key_grad[at : at + 32].reshape(NZ // 2, 8, HD)
        v = value_grad[at : at + 32].reshape(NZ // 2, 8, HD)
        even = jnp.where(sub < 4, k, pltpu.roll(v, 4, 1)).astype(bf16)
        odd = jnp.where(sub < 4, pltpu.roll(k, 4, 1), v).astype(bf16)
        for i in range(NZ // 2):
            out[2 * i, 2, 0] = even[i]
            out[2 * i + 1, 2, 0] = odd[i]

    far_keys = key_grad[NEAR:].astype(bf16)
    far_values = value_grad[NEAR:].astype(bf16)
    up_key_part[...] = dot(low_all[...], far_keys, ((0,), (0,)))[:UPDATE_RANK]
    up_value_part[...] = dot(low_all[...], far_values, ((0,), (0,)))[:UPDATE_RANK]

    def twice(ref):
        return jnp.concatenate([ref[...], ref[...]], axis=0)

    low_total[...] += dot(far_keys, twice(up_key), ((1,), (1,)))
    low_total[...] += dot(far_values, twice(up_value), ((1,), (1,)))

    @pl.when(g == KVH - 1)
    def _():
        lane = lax.broadcasted_iota(jnp.int32, (8, HD), 1)
        for b in range(NX):
            x = lax.rem(place[1] - b + NX, NX)
            for z in range(NZ):
                at = b * 64 + z * 8
                head = low_total[at : at + 8, :]
                at = 256 + b * 32 + z // 2 * 8
                tail = low_total[at : at + 8, :]
                if z % 2:
                    tail = pltpu.roll(tail, 4, 0)
                low_part[z, x] = jnp.where(lane < UPDATE_RANK, head, tail).astype(bf16)


def attend(place, docs, ends, query, key, value, grad, up, boxes):
    wide = pl.BlockSpec((2, SPAN, GROUP * HD), lambda g: (0, 0, g))
    narrow = pl.BlockSpec((2, SPAN, HD), lambda g: (0, 0, g))
    whole = pl.BlockSpec((NZ, TILES, 8, HD), lambda g: (0, 0, 0, 0))
    part = pl.BlockSpec((NZ, 3, 1, 8, HD), lambda g: (0, 0, g, 0, 0))
    up_key = pl.BlockSpec((UPDATE_RANK, HD), lambda g: (0, g))
    up_value = pl.BlockSpec((UPDATE_RANK, HD), lambda g: (0, KVH + g))
    low_part = pl.BlockSpec((NZ, NX, 8, HD), lambda g: (0, 0, 0, 0))
    wide_shape = jax.ShapeDtypeStruct((2, SPAN, QW), bf16)
    narrow_shape = jax.ShapeDtypeStruct((2, SPAN, KEY_FEATURES), bf16)
    part_shape = jax.ShapeDtypeStruct((NZ, 3, KVH, 8, HD), bf16)
    up_shape = jax.ShapeDtypeStruct((UPDATE_RANK, KEY_FEATURES), f32)
    return pl.pallas_call(
        attend_kernel,
        grid=(KVH,),
        in_specs=[SMEM] * 3 + [wide, narrow, narrow, wide, up_key, up_value] + [whole] * NX,
        out_specs=[wide, wide, narrow, narrow] + [part] * NX + [up_key, up_key, low_part],
        out_shape=[wide_shape, wide_shape, narrow_shape, narrow_shape]
        + [part_shape] * NX
        + [up_shape, up_shape, jax.ShapeDtypeStruct((NZ, NX, 8, HD), bf16)],
        scratch_shapes=[
            pltpu.VMEM((KEYS, NEAR), f32),
            pltpu.VMEM((FAR, HD), bf16),
            pltpu.VMEM((FAR, HD), f32),
        ],
        compiler_params=pltpu.CompilerParams(vmem_limit_bytes=48 * 1024 * 1024),
        name="attend",
    )(place, docs, ends, query, key, value, grad, up, up, *boxes)


PER_ROW = (MODEL_WIDTH + 2 * KEY_FEATURES) // HD
CHUNK = 12
CHUNKS = 8 * PER_ROW // CHUNK


def factor_kernel(counts, low_parts, state, up_key, up_value, pieces):
    pick = selection(counts[0, 0, 0], counts[0, 0, 1])
    total = jnp.sum(low_parts[...].astype(f32), axis=0)
    compact = jnp.concatenate([total, pltpu.roll(total, UPDATE_RANK, 1)], axis=0).astype(bf16)
    low_grad = dot(pick.astype(bf16), compact, ((0,), (0,))).astype(bf16)
    down_piece = dot(low_grad, state[...], ((0,), (0,)))
    wide = MODEL_WIDTH // HD
    for t in range(8 * PER_ROW):
        r, c = divmod(t, PER_ROW)
        rows = slice(r * 8, r * 8 + 8)
        if c < wide:
            tile = down_piece[rows, c * HD : (c + 1) * HD]
        elif c < wide + KVH:
            c -= wide
            tile = up_key[rows, c * HD : (c + 1) * HD]
        else:
            c -= wide + KVH
            tile = up_value[rows, c * HD : (c + 1) * HD]
        pieces[t // CHUNK, t % CHUNK] = tile.astype(bf16)


def factor(counts, low_parts, state, up_key, up_value):
    return pl.pallas_call(
        factor_kernel,
        in_specs=[SMEM] + [VMEM] * 4,
        out_specs=VMEM,
        out_shape=jax.ShapeDtypeStruct((CHUNKS, CHUNK, 8, HD), bf16),
        name="factor",
    )(counts, low_parts, state, up_key, up_value)


def middle_kernel(pieces, a, b, c, d, out):
    chunk = jnp.sum(pieces[...].astype(f32), axis=0).astype(bf16)
    for z in range(NZ):
        out[z, :CHUNK] = chunk
        out[z, CHUNK:] = (
            (a[z].astype(f32) + b[z].astype(f32)) + (c[z].astype(f32) + d[z].astype(f32))
        ).astype(bf16)


def middle(pieces, parts):
    return pl.pallas_call(
        middle_kernel,
        in_specs=[VMEM] * 5,
        out_specs=VMEM,
        out_shape=jax.ShapeDtypeStruct((NZ, CHUNK + GRAD_TILES, 8, HD), bf16),
        name="middle",
    )(pieces, *parts)


def close_kernel(counts, parts, cache_out, out):
    pick = selection(counts[0, 0, 0], counts[0, 0, 1]).astype(bf16)
    total = jnp.sum(parts[...].astype(f32), axis=0)
    chunk = total[:CHUNK].astype(bf16)
    for i in range(CHUNKS):
        out[i] = chunk
    total = total[CHUNK:]
    sub = lax.broadcasted_iota(jnp.int32, (8, HD), 0)
    tops = [total[h] for h in range(2 * KVH)]
    rest_keys, rest_values = [], []
    for h in range(KVH):
        both = total[16 + h]
        rest_keys.append(jnp.where(sub < 4, both, 0.0))
        rest_values.append(jnp.where(sub < 4, pltpu.roll(both, 4, 0), 0.0))
    compact = jnp.concatenate(
        [jnp.concatenate(tops, axis=1), jnp.concatenate(rest_keys + rest_values, axis=1)], axis=0
    ).astype(bf16)
    cache_out[...] = dot(pick, compact, ((0,), (0,))).astype(bf16)


def close(counts, parts):
    return pl.pallas_call(
        close_kernel,
        in_specs=[SMEM, VMEM],
        out_specs=[VMEM, VMEM],
        out_shape=[
            jax.ShapeDtypeStruct((16, 2 * KEY_FEATURES), bf16),
            jax.ShapeDtypeStruct((CHUNKS, CHUNK, 8, HD), bf16),
        ],
        name="close",
    )(counts, parts)


def unpack_kernel(tiles, out):
    for t in range(8 * PER_ROW):
        r, c = divmod(t, PER_ROW)
        out[r * 8 : r * 8 + 8, c * HD : (c + 1) * HD] = tiles[t // CHUNK, t % CHUNK].astype(f32)


def unpack(tiles):
    return pl.pallas_call(
        unpack_kernel,
        in_specs=[VMEM],
        out_specs=VMEM,
        out_shape=jax.ShapeDtypeStruct((UPDATE_RANK, MODEL_WIDTH + 2 * KEY_FEATURES), f32),
        name="unpack",
    )(tiles)


def exchange(x, axes):
    return lax.all_to_all(x, axes, 0, 0, tiled=True)


def shift(x, by):
    return lax.ppermute(x, "x", [(i, (i + by) % NX) for i in range(NX)])


def local(
    query, key, value, beacon_slot_state, frozen_beacon_cache, adapter_down_weight,
    adapter_up_weight, output_cotangent, span_beacon_count, span_document, boundary,
):
    place = jnp.stack([lax.axis_index("z"), lax.axis_index("x")]).astype(jnp.int32)
    state = beacon_slot_state[0, 0].reshape(2 * MAX_BEACONS, MODEL_WIDTH)
    frozen = frozen_beacon_cache[0, 0].reshape(2 * MAX_BEACONS, 2 * KEY_FEATURES)

    message = project(
        span_beacon_count, span_document, state, adapter_down_weight.T, adapter_up_weight, frozen
    )
    column = exchange(message, "z")
    boxes = [column, shift(column, 1), shift(column, 2), shift(column, 3)]
    attended, grad_query, grad_key, grad_value, *rest = attend(
        place, span_document, boundary, query[0, 0], key[0, 0], value[0, 0],
        output_cotangent[0, 0], adapter_up_weight, boxes,
    )
    parts = [p.reshape(NZ, GRAD_TILES, 8, HD) for p in rest[:NX]]
    up_key, up_value, low_part = rest[NX:]
    parts = [parts[0], shift(parts[1], -1), shift(parts[2], -2), shift(parts[3], -3)]
    low_parts = exchange(low_part.reshape(NZ * NX, 8, HD), ("z", "x"))
    pieces = factor(span_beacon_count, low_parts, state, up_key, up_value)
    both = exchange(middle(exchange(pieces, WIDE), parts), "z")
    cache_gradient, chunk = close(span_beacon_count, both)
    adapter_gradient = unpack(exchange(chunk, WIDE))
    return (
        attended[None, None],
        grad_query[None, None],
        grad_key[None, None],
        grad_value[None, None],
        cache_gradient.reshape(1, 1, 2, MAX_BEACONS, 2 * KEY_FEATURES),
        adapter_gradient,
    )


def solution(mesh):
    chips = Mesh(mesh.devices.reshape(NZ, NX, NY, NC), ALL_AXES)
    dp, ctx = ("y", "core"), ("z", "x")
    array5 = P(dp, ctx, None, None, None)
    array3 = P(dp, ctx, None)
    return jax.shard_map(
        local,
        mesh=chips,
        in_specs=(array5, array5, array5, array5, array5, P(), P(), array5, array3, array3, array3),
        out_specs=(array5, array5, array5, array5, array5, P()),
        check_vma=False,
    )
```

```python
import jax
import jax.numpy as jnp
from jax import lax
from jax.experimental import pallas as pl
from jax.experimental.pallas import tpu as pltpu
from jax.sharding import Mesh, PartitionSpec as P

MODEL_WIDTH = 4096
KVH = 8
HD = 128
SPAN = 64
MAX_BEACONS = 8
UPDATE_RANK = 64
GROUP = 4
QW = 4096
KEY_FEATURES = 1024
NCH = 64
NZ, NX, NY, NC = 8, 4, 4, 2

bf16 = jnp.bfloat16
f32 = jnp.float32
ALL_AXES = ("z", "x", "y", "core")
WIDE = ("x", "y", "core")

HEADS = 4
HALF_TILES = 3 * HEADS
LOW_TILE = HALF_TILES
FACT_TILE = HALF_TILES + 1
FAR = 384
NEAR = 128
KEYS = FAR + NEAR
ROWS = GROUP * 2 * SPAN
MASKED = -1e30
SCORE_SCALE = HD ** (-0.5)
LOG2E = 1.4426950408889634


def dot(a, b, dims=((1,), (0,))):
    return lax.dot_general(a, b, (dims, ((), ())), preferred_element_type=f32)


def selection(first, second):
    row = lax.broadcasted_iota(jnp.int32, (16, 16), 0)
    slot = lax.broadcasted_iota(jnp.int32, (16, 16), 1)
    source = jnp.where(row < first, row, row - first + MAX_BEACONS)
    return jnp.where((slot == source) & (row < first + second), 1.0, 0.0)


def project_kernel(counts, docs, state, down_t, up, frozen, out_a, out_b):
    first, second = counts[0, 0, 0], counts[0, 0, 1]
    low = dot(state[...], down_t[...], ((1,), (1,))).astype(bf16)
    states = (frozen[...].astype(f32) + dot(low, up[...])).astype(bf16)
    pick = selection(first, second).astype(bf16)
    rows = dot(pick, states)
    low_rows = dot(pick, low).astype(bf16)
    sub = lax.broadcasted_iota(jnp.int32, (8, HD), 0)
    halves = []
    for heads in (range(HEADS), range(HEADS, KVH)):
        tiles = [rows[:8, h * HD : (h + 1) * HD] for h in heads]
        tiles += [rows[:8, (KVH + h) * HD : (KVH + h + 1) * HD] for h in heads]
        for h in heads:
            keys = rows[8:, h * HD : (h + 1) * HD]
            values = rows[8:, (KVH + h) * HD : (KVH + h + 1) * HD]
            tiles.append(jnp.where(sub < 4, keys, pltpu.roll(values, 4, 0)))
        halves.append(tiles)
    put_row = lax.broadcasted_iota(jnp.int32, (UPDATE_RANK, HD), 0)
    put_col = lax.broadcasted_iota(jnp.int32, (UPDATE_RANK, HD), 1)
    left = jnp.where(put_row == put_col, 1.0, 0.0).astype(bf16)
    right = jnp.where(put_row + UPDATE_RANK == put_col, 1.0, 0.0).astype(bf16)
    halves[0].append(dot(low_rows, left)[:8] + dot(low_rows, right)[8:])
    facts = jnp.zeros((8, HD), f32)
    for i, fact in enumerate((first, second, docs[0, 0, 0], docs[0, 0, 1])):
        facts = jnp.where(sub == i, fact.astype(f32), facts)
    halves[0].append(facts)
    for out, tiles in zip((out_a, out_b), halves):
        for t, tile in enumerate(tiles):
            packed = tile.astype(bf16)
            for z in range(NZ):
                out[z, t] = packed


VMEM = pl.BlockSpec(memory_space=pltpu.VMEM)
SMEM = pl.BlockSpec(memory_space=pltpu.SMEM)


def project(counts, docs, state, down_t, up, frozen):
    return pl.pallas_call(
        project_kernel,
        in_specs=[SMEM] * 2 + [VMEM] * 4,
        out_specs=[VMEM] * 2,
        out_shape=[
            jax.ShapeDtypeStruct((NZ, FACT_TILE + 1, 8, HD), bf16),
            jax.ShapeDtypeStruct((NZ, HALF_TILES, 8, HD), bf16),
        ],
        name="project",
    )(counts, docs, state, down_t, up, frozen)


def fill_bias(place, docs, ends, boxes, bias):
    z_own, x_own = place[0], place[1]
    pair = z_own * NX + x_own
    lane = lax.broadcasted_iota(jnp.int32, (8, NEAR), 1)
    sub = lax.broadcasted_iota(jnp.int32, (8, NEAR), 0)
    side = lane // SPAN
    offset = lane % SPAN
    own_span = jnp.where(side == 0, pair, NCH - 1 - pair).astype(f32)
    own_doc = jnp.where(side == 0, docs[0, 0, 0], docs[0, 0, 1]).astype(f32)
    live = offset < jnp.where(side == 0, ends[0, 0, 0], ends[0, 0, 1])
    for block in range(NEAR // 8):
        key_side = block * 8 // SPAN
        key_offset = sub + (block * 8) % SPAN
        key_live = key_offset < ends[0, 0, key_side]
        seen = (side == key_side) & (key_offset <= offset) & (key_live == live)
        bias[block * 8 : block * 8 + 8, :] = jnp.where(seen, 0.0, MASKED)

    def facts(box, z, slot):
        tile = boxes[box][z, FACT_TILE].astype(f32)
        first, second = tile[0:1], tile[1:2]
        first_doc, second_doc = tile[2:3], tile[3:4]
        source = z * NX + lax.rem(x_own - box + NX, NX)
        low = slot < first
        high = slot < first + second
        span = jnp.where(low, source, NCH - 1 - source).astype(f32)
        doc = jnp.where(low, first_doc, second_doc)
        return jnp.where(high, span, 2.0 * NCH), doc

    def write(at, span, doc):
        seen = live & (span < own_span) & (doc == own_doc)
        bias[at : at + 8, :] = jnp.where(seen, 0.0, MASKED)

    slot = sub.astype(f32)
    for box in range(NX):
        for z in range(NZ):
            write(NEAR + box * 64 + z * 8, *facts(box, z, slot))
        for z in range(0, NZ, 2):
            span_a, doc_a = facts(box, z, slot + 8.0)
            span_b, doc_b = facts(box, z + 1, slot + 4.0)
            write(
                NEAR + 256 + box * 32 + z * 4,
                jnp.where(sub < 4, span_a, span_b),
                jnp.where(sub < 4, doc_a, doc_b),
            )


def gather_low(boxes, low_all):
    lane = lax.broadcasted_iota(jnp.int32, (NZ, 8, HD), 2)
    sub = lax.broadcasted_iota(jnp.int32, (NZ // 2, 8, HD), 1)
    for b, box in enumerate(boxes):
        tile = box[:, LOW_TILE].astype(f32)
        head = jnp.where(lane < UPDATE_RANK, tile, 0.0)
        low_all[b * 64 : b * 64 + 64, :] = head.reshape(64, HD).astype(bf16)
        tail = jnp.where(lane < UPDATE_RANK, pltpu.roll(tile, UPDATE_RANK, 2), 0.0)
        tail = tail.reshape(NZ // 2, 2, 8, HD)
        tail = jnp.where(sub < 4, tail[:, 0], pltpu.roll(tail[:, 1], 4, 1))
        at = 256 + b * 32
        low_all[at : at + 32, :] = tail.reshape(32, HD).astype(bf16)


def attend_kernel(
    place, docs, ends, query, key, value, grad, up_key, up_value, box0, box1, box2, box3,
    bias, low_all, low_before,
    attended, grad_query, grad_key, grad_value, out0, out1, out2, out3, up_key_part,
    up_value_part, low_part, low_total, last,
):
    boxes = (box0, box1, box2, box3)
    outs = (out0, out1, out2, out3)
    g = pl.program_id(0)

    @pl.when(g == 0)
    def _():
        if low_before is None:
            fill_bias(place, docs, ends, boxes, bias)
            gather_low(boxes, low_all)
            low_total[...] = jnp.zeros_like(low_total)
        else:
            low_total[...] = low_before[...]

    sub = lax.broadcasted_iota(jnp.int32, (NZ // 2, 8, HD), 1)

    def stack(ref):
        whole = ref[...].reshape(2 * SPAN, GROUP * HD)
        return jnp.concatenate(
            [whole[:, m * HD : (m + 1) * HD] for m in range(GROUP)], axis=0
        )

    def far_rows(tile):
        return [box[:, tile].astype(f32).reshape(8 * NZ, HD) for box in boxes]

    extra_keys, extra_values = [], []
    for box in boxes:
        both = box[:, 2 * HEADS + g].astype(f32).reshape(NZ // 2, 2, 8, HD)
        even, odd = both[:, 0], both[:, 1]
        extra_keys.append(jnp.where(sub < 4, even, pltpu.roll(odd, 4, 1)).reshape(4 * NZ, HD))
        extra_values.append(jnp.where(sub < 4, pltpu.roll(even, 4, 1), odd).reshape(4 * NZ, HD))
    keys = jnp.concatenate(
        [key[...].reshape(NEAR, HD).astype(f32)] + far_rows(g) + extra_keys, axis=0
    )
    values = jnp.concatenate(
        [value[...].reshape(NEAR, HD).astype(f32)] + far_rows(HEADS + g) + extra_values, axis=0
    )
    keys_t = keys.T.astype(bf16)
    values_t = values.T.astype(bf16)
    keys = keys.astype(bf16)
    values = values.astype(bf16)
    queries = stack(query)
    grads = stack(grad)
    grads_t = grads.astype(f32).T

    scores = dot(keys, queries, ((1,), (1,))) * (SCORE_SCALE * LOG2E)
    scores = scores + jnp.tile(bias[...], (1, GROUP))
    top = jnp.max(scores, axis=0, keepdims=True)
    weights = jnp.exp2(scores - top)
    total = jnp.sum(weights, axis=0, keepdims=True)
    exact = weights * (1.0 / total)
    probs = exact.astype(bf16)
    summed_t = dot(values_t, probs)
    summed = summed_t.T.astype(bf16)
    rounded_t = summed_t.astype(bf16).astype(f32)
    delta = jnp.sum(grads_t * rounded_t, axis=0, keepdims=True)
    grad_probs = dot(values, grads_t.astype(bf16))
    grad_scores = (exact * (grad_probs - delta)).astype(bf16)
    query_grad = (dot(keys_t, grad_scores) * SCORE_SCALE).T.astype(bf16)
    key_grad = dot(grad_scores, queries) * SCORE_SCALE
    value_grad = dot(probs, grads)

    for m in range(GROUP):
        at = slice(m * 2 * SPAN, (m + 1) * 2 * SPAN)
        cols = slice(m * HD, (m + 1) * HD)
        attended[:, :, cols] = summed[at].reshape(2, SPAN, HD)
        grad_query[:, :, cols] = query_grad[at].reshape(2, SPAN, HD)
    grad_key[...] = key_grad[:NEAR].astype(bf16).reshape(2, SPAN, HD)
    grad_value[...] = value_grad[:NEAR].astype(bf16).reshape(2, SPAN, HD)
    for b, out in enumerate(outs):
        at = NEAR + b * 64
        out[:, 0, 0] = key_grad[at : at + 64].reshape(NZ, 8, HD).astype(bf16)
        out[:, 1, 0] = value_grad[at : at + 64].reshape(NZ, 8, HD).astype(bf16)
        at = NEAR + 256 + b * 32
        k = key_grad[at : at + 32].reshape(NZ // 2, 8, HD)
        v = value_grad[at : at + 32].reshape(NZ // 2, 8, HD)
        even = jnp.where(sub < 4, k, pltpu.roll(v, 4, 1)).astype(bf16)
        odd = jnp.where(sub < 4, pltpu.roll(k, 4, 1), v).astype(bf16)
        for i in range(NZ // 2):
            out[2 * i, 2, 0] = even[i]
            out[2 * i + 1, 2, 0] = odd[i]

    far_keys = key_grad[NEAR:].astype(bf16)
    far_values = value_grad[NEAR:].astype(bf16)
    up_key_part[...] = dot(low_all[...], far_keys, ((0,), (0,)))[:UPDATE_RANK]
    up_value_part[...] = dot(low_all[...], far_values, ((0,), (0,)))[:UPDATE_RANK]

    def twice(ref):
        return jnp.concatenate([ref[...], ref[...]], axis=0)

    low_total[...] += dot(far_keys, twice(up_key), ((1,), (1,)))
    low_total[...] += dot(far_values, twice(up_value), ((1,), (1,)))

    if not last:
        return

    @pl.when(g == HEADS - 1)
    def _():
        lane = lax.broadcasted_iota(jnp.int32, (8, HD), 1)
        for b in range(NX):
            x = lax.rem(place[1] - b + NX, NX)
            for z in range(NZ):
                at = b * 64 + z * 8
                head = low_total[at : at + 8, :]
                at = 256 + b * 32 + z // 2 * 8
                tail = low_total[at : at + 8, :]
                if z % 2:
                    tail = pltpu.roll(tail, 4, 0)
                low_part[z, x] = jnp.where(lane < UPDATE_RANK, head, tail).astype(bf16)


def first_kernel(*refs):
    (place, docs, ends, query, key, value, grad, up_key, up_value, *boxes) = refs[:13]
    (attended, grad_query, grad_key, grad_value, *rest) = refs[13:]
    outs, (up_k, up_v, low_total, bias, low_all) = rest[:4], rest[4:]
    attend_kernel(
        place, docs, ends, query, key, value, grad, up_key, up_value, *boxes,
        bias, low_all, None,
        attended, grad_query, grad_key, grad_value, *outs, up_k, up_v, None, low_total, False,
    )


def second_kernel(*refs):
    (place, query, key, value, grad, up_key, up_value, *boxes) = refs[:11]
    bias, low_all, low_before = refs[11:14]
    (attended, grad_query, grad_key, grad_value, *rest) = refs[18:]
    outs, (up_k, up_v, low_part, low_total) = rest[:4], rest[4:]
    attend_kernel(
        place, None, None, query, key, value, grad, up_key, up_value, *boxes,
        bias, low_all, low_before,
        attended, grad_query, grad_key, grad_value, *outs, up_k, up_v, low_part, low_total, True,
    )


def attend(half, small, query, key, value, grad, up, boxes, carried=(), filled=()):
    at = half * HEADS
    wide = pl.BlockSpec((2, SPAN, GROUP * HD), lambda g: (0, 0, g + at))
    narrow = pl.BlockSpec((2, SPAN, HD), lambda g: (0, 0, g + at))
    whole = pl.BlockSpec(boxes[0].shape, lambda g: (0, 0, 0, 0))
    part = pl.BlockSpec((NZ, 3, 1, 8, HD), lambda g: (0, 0, g, 0, 0))
    up_key = pl.BlockSpec((UPDATE_RANK, HD), lambda g: (0, g + at))
    up_value = pl.BlockSpec((UPDATE_RANK, HD), lambda g: (0, KVH + g + at))
    up_part = pl.BlockSpec((UPDATE_RANK, HD), lambda g: (0, g))
    low_part = pl.BlockSpec((NZ, NX, 8, HD), lambda g: (0, 0, 0, 0))
    wide_shape = jax.ShapeDtypeStruct((2, SPAN, QW), bf16)
    narrow_shape = jax.ShapeDtypeStruct((2, SPAN, KEY_FEATURES), bf16)
    part_shape = jax.ShapeDtypeStruct((NZ, 3, HEADS, 8, HD), bf16)
    up_shape = jax.ShapeDtypeStruct((UPDATE_RANK, HEADS * HD), f32)
    kept = [
        jax.ShapeDtypeStruct((FAR, HD), f32),
        jax.ShapeDtypeStruct((KEYS, NEAR), f32),
        jax.ShapeDtypeStruct((FAR, HD), bf16),
    ]
    kept_specs = [pl.BlockSpec(k.shape, lambda g: (0, 0)) for k in kept]
    in_specs = [SMEM] * len(small) + [wide, narrow, narrow, wide, up_key, up_value] + [whole] * NX
    out_specs = [wide, wide, narrow, narrow] + [part] * NX + [up_part] * 2
    out_shape = [wide_shape] * 2 + [narrow_shape] * 2 + [part_shape] * NX + [up_shape] * 2
    scratch, aliases = [], {}
    if half == 0:
        out_specs += kept_specs
        out_shape += kept
    else:
        in_specs += kept_specs[1:] + kept_specs[:1] + [pl.BlockSpec(memory_space=pl.ANY)] * 4
        out_specs.append(low_part)
        out_shape.append(jax.ShapeDtypeStruct((NZ, NX, 8, HD), bf16))
        scratch = [pltpu.VMEM((FAR, HD), f32)]
        aliases = {len(in_specs) - 4 + i: i for i in range(4)}
    return pl.pallas_call(
        (first_kernel, second_kernel)[half],
        grid=(HEADS,),
        in_specs=in_specs,
        out_specs=out_specs,
        out_shape=out_shape,
        scratch_shapes=scratch,
        input_output_aliases=aliases,
        compiler_params=pltpu.CompilerParams(vmem_limit_bytes=20 * 1024 * 1024),
        cost_estimate=pl.CostEstimate(
            flops=6 * 10**9, bytes_accessed=4 * 2**20, transcendentals=HEADS * KEYS * ROWS
        ),
        name=("attend_first", "attend_second")[half],
    )(*small, query, key, value, grad, up, up, *boxes, *carried, *filled)


PER_ROW = (MODEL_WIDTH + 2 * KEY_FEATURES) // HD
CHUNK = 12
CHUNKS = 8 * PER_ROW // CHUNK


def factor_kernel(counts, low_parts, state, key_a, value_a, key_b, value_b, pieces):
    pick = selection(counts[0, 0, 0], counts[0, 0, 1])
    total = jnp.sum(low_parts[...].astype(f32), axis=0)
    compact = jnp.concatenate([total, pltpu.roll(total, UPDATE_RANK, 1)], axis=0).astype(bf16)
    low_grad = dot(pick.astype(bf16), compact, ((0,), (0,))).astype(bf16)
    down_piece = dot(low_grad, state[...], ((0,), (0,)))
    wide = MODEL_WIDTH // HD
    ups = (key_a, key_b, value_a, value_b)
    for t in range(8 * PER_ROW):
        r, c = divmod(t, PER_ROW)
        rows = slice(r * 8, r * 8 + 8)
        if c < wide:
            tile = down_piece[rows, c * HD : (c + 1) * HD]
        else:
            which, c = divmod(c - wide, HEADS)
            tile = ups[which][rows, c * HD : (c + 1) * HD]
        pieces[t // CHUNK, t % CHUNK] = tile.astype(bf16)


def factor(counts, low_parts, state, ups):
    return pl.pallas_call(
        factor_kernel,
        in_specs=[SMEM] + [VMEM] * 6,
        out_specs=VMEM,
        out_shape=jax.ShapeDtypeStruct((CHUNKS, CHUNK, 8, HD), bf16),
        name="factor",
    )(counts, low_parts, state, *ups)


def middle_kernel(pieces, *refs):
    out = refs[-1]
    chunk = jnp.sum(pieces[...].astype(f32), axis=0).astype(bf16)
    for z in range(NZ):
        out[z, :CHUNK] = chunk
        for half in range(2):
            a, b, c, d = refs[half * NX : half * NX + NX]
            at = CHUNK + half * HALF_TILES
            out[z, at : at + HALF_TILES] = (
                (a[z].astype(f32) + b[z].astype(f32)) + (c[z].astype(f32) + d[z].astype(f32))
            ).astype(bf16)


def middle(pieces, parts):
    return pl.pallas_call(
        middle_kernel,
        in_specs=[VMEM] * (1 + len(parts)),
        out_specs=VMEM,
        out_shape=jax.ShapeDtypeStruct((NZ, CHUNK + 2 * HALF_TILES, 8, HD), bf16),
        name="middle",
    )(pieces, *parts)


def close_kernel(counts, parts, cache_out, out):
    pick = selection(counts[0, 0, 0], counts[0, 0, 1]).astype(bf16)
    total = jnp.sum(parts[...].astype(f32), axis=0)
    chunk = total[:CHUNK].astype(bf16)
    for i in range(CHUNKS):
        out[i] = chunk
    sub = lax.broadcasted_iota(jnp.int32, (8, HD), 0)
    top_keys, top_values, rest_keys, rest_values = [], [], [], []
    for h in range(KVH):
        at = CHUNK + h // HEADS * HALF_TILES + h % HEADS
        top_keys.append(total[at])
        top_values.append(total[at + HEADS])
        both = total[at + 2 * HEADS]
        rest_keys.append(jnp.where(sub < 4, both, 0.0))
        rest_values.append(jnp.where(sub < 4, pltpu.roll(both, 4, 0), 0.0))
    compact = jnp.concatenate(
        [
            jnp.concatenate(top_keys + top_values, axis=1),
            jnp.concatenate(rest_keys + rest_values, axis=1),
        ],
        axis=0,
    ).astype(bf16)
    cache_out[...] = dot(pick, compact, ((0,), (0,))).astype(bf16)


def close(counts, parts):
    return pl.pallas_call(
        close_kernel,
        in_specs=[SMEM, VMEM],
        out_specs=[VMEM, VMEM],
        out_shape=[
            jax.ShapeDtypeStruct((16, 2 * KEY_FEATURES), bf16),
            jax.ShapeDtypeStruct((CHUNKS, CHUNK, 8, HD), bf16),
        ],
        name="close",
    )(counts, parts)


def unpack_kernel(tiles, out):
    for t in range(8 * PER_ROW):
        r, c = divmod(t, PER_ROW)
        out[r * 8 : r * 8 + 8, c * HD : (c + 1) * HD] = tiles[t // CHUNK, t % CHUNK].astype(f32)


def unpack(tiles):
    return pl.pallas_call(
        unpack_kernel,
        in_specs=[VMEM],
        out_specs=VMEM,
        out_shape=jax.ShapeDtypeStruct((UPDATE_RANK, MODEL_WIDTH + 2 * KEY_FEATURES), f32),
        name="unpack",
    )(tiles)


def exchange(x, axes):
    return lax.all_to_all(x, axes, 0, 0, tiled=True)


def shift(x, by):
    return lax.ppermute(x, "x", [(i, (i + by) % NX) for i in range(NX)])


def spread(column):
    return [column, shift(column, 1), shift(column, 2), shift(column, 3)]


def collect(parts):
    parts = [p.reshape(NZ, HALF_TILES, 8, HD) for p in parts]
    return [parts[0], shift(parts[1], -1), shift(parts[2], -2), shift(parts[3], -3)]


def local(
    query, key, value, beacon_slot_state, frozen_beacon_cache, adapter_down_weight,
    adapter_up_weight, output_cotangent, span_beacon_count, span_document, boundary,
):
    place = jnp.stack([lax.axis_index("z"), lax.axis_index("x")]).astype(jnp.int32)
    state = beacon_slot_state[0, 0].reshape(2 * MAX_BEACONS, MODEL_WIDTH)
    frozen = frozen_beacon_cache[0, 0].reshape(2 * MAX_BEACONS, 2 * KEY_FEATURES)

    message_a, message_b = project(
        span_beacon_count, span_document, state, adapter_down_weight.T, adapter_up_weight, frozen
    )
    arrays = (query[0, 0], key[0, 0], value[0, 0], output_cotangent[0, 0], adapter_up_weight)
    boxes_a = spread(exchange(message_a, "z"))
    boxes_b = spread(exchange(message_b, "z"))
    first = attend(0, (place, span_document, boundary), *arrays, boxes_a)
    low_total, bias, low_all = first[10:]
    parts_a = collect(first[4:8])
    second = attend(1, (place,), *arrays, boxes_b, (bias, low_all, low_total), first[:4])
    parts_b = collect(second[4:8])
    attended, grad_query, grad_key, grad_value = second[:4]
    low_part, parts_a = lax.optimization_barrier((second[10], parts_a))
    low_parts = exchange(low_part.reshape(NZ * NX, 8, HD), ("z", "x"))
    low_parts, parts_b = lax.optimization_barrier((low_parts, parts_b))
    pieces = factor(span_beacon_count, low_parts, state, first[8:10] + second[8:10])
    both = exchange(middle(exchange(pieces, WIDE), parts_a + parts_b), "z")
    cache_gradient, chunk = close(span_beacon_count, both)
    adapter_gradient = unpack(exchange(chunk, WIDE))
    return (
        attended[None, None],
        grad_query[None, None],
        grad_key[None, None],
        grad_value[None, None],
        cache_gradient.reshape(1, 1, 2, MAX_BEACONS, 2 * KEY_FEATURES),
        adapter_gradient,
    )


def solution(mesh):
    chips = Mesh(mesh.devices.reshape(NZ, NX, NY, NC), ALL_AXES)
    dp, ctx = ("y", "core"), ("z", "x")
    array5 = P(dp, ctx, None, None, None)
    array3 = P(dp, ctx, None)
    return jax.shard_map(
        local,
        mesh=chips,
        in_specs=(array5, array5, array5, array5, array5, P(), P(), array5, array3, array3, array3),
        out_specs=(array5, array5, array5, array5, array5, P()),
        check_vma=False,
    )
```

```python
import jax
import jax.numpy as jnp
from jax import lax
from jax.experimental import pallas as pl
from jax.experimental.pallas import tpu as pltpu
from jax.sharding import Mesh, PartitionSpec as P

MODEL_WIDTH = 4096
KVH = 8
HD = 128
SPAN = 64
MAX_BEACONS = 8
UPDATE_RANK = 64
GROUP = 4
QW = 4096
KEY_FEATURES = 1024
NCH = 64
NZ, NX, NY, NC = 8, 4, 4, 2

bf16 = jnp.bfloat16
f32 = jnp.float32
ALL_AXES = ("z", "x", "y", "core")
PLANE = ("x", "y")

HEADS = 4
HALF_TILES = 3 * HEADS
LOW_TILE = HALF_TILES
FACT_TILE = HALF_TILES + 1
FAR = 384
NEAR = 128
KEYS = FAR + NEAR
ROWS = GROUP * 2 * SPAN
MASKED = -1e30
SCORE_SCALE = HD ** (-0.5)
LOG2E = 1.4426950408889634


def dot(a, b, dims=((1,), (0,))):
    return lax.dot_general(a, b, (dims, ((), ())), preferred_element_type=f32)


def selection(first, second):
    row = lax.broadcasted_iota(jnp.int32, (16, 16), 0)
    slot = lax.broadcasted_iota(jnp.int32, (16, 16), 1)
    source = jnp.where(row < first, row, row - first + MAX_BEACONS)
    return jnp.where((slot == source) & (row < first + second), 1.0, 0.0)


def project_kernel(counts, docs, state, down_t, up, frozen, out):
    first, second = counts[0, 0, 0], counts[0, 0, 1]
    low = dot(state[...], down_t[...], ((1,), (1,))).astype(bf16)
    states = (frozen[...].astype(f32) + dot(low, up[...])).astype(bf16)
    pick = selection(first, second).astype(bf16)
    rows = dot(pick, states)
    low_rows = dot(pick, low).astype(bf16)
    sub = lax.broadcasted_iota(jnp.int32, (8, HD), 0)
    halves = []
    for heads in (range(HEADS), range(HEADS, KVH)):
        tiles = [rows[:8, h * HD : (h + 1) * HD] for h in heads]
        tiles += [rows[:8, (KVH + h) * HD : (KVH + h + 1) * HD] for h in heads]
        for h in heads:
            keys = rows[8:, h * HD : (h + 1) * HD]
            values = rows[8:, (KVH + h) * HD : (KVH + h + 1) * HD]
            tiles.append(jnp.where(sub < 4, keys, pltpu.roll(values, 4, 0)))
        halves.append(tiles)
    put_row = lax.broadcasted_iota(jnp.int32, (UPDATE_RANK, HD), 0)
    put_col = lax.broadcasted_iota(jnp.int32, (UPDATE_RANK, HD), 1)
    left = jnp.where(put_row == put_col, 1.0, 0.0).astype(bf16)
    right = jnp.where(put_row + UPDATE_RANK == put_col, 1.0, 0.0).astype(bf16)
    halves[0].append(dot(low_rows, left)[:8] + dot(low_rows, right)[8:])
    facts = jnp.zeros((8, HD), f32)
    for i, fact in enumerate((first, second, docs[0, 0, 0], docs[0, 0, 1])):
        facts = jnp.where(sub == i, fact.astype(f32), facts)
    halves[0].append(facts)
    for t, tile in enumerate(halves[0] + halves[1]):
        packed = tile.astype(bf16)
        for z in range(NZ):
            out[z, t] = packed


VMEM = pl.BlockSpec(memory_space=pltpu.VMEM)
SMEM = pl.BlockSpec(memory_space=pltpu.SMEM)
SMALL = pltpu.CompilerParams(vmem_limit_bytes=8 * 1024 * 1024)


def project(counts, docs, state, down_t, up, frozen):
    return pl.pallas_call(
        project_kernel,
        in_specs=[SMEM] * 2 + [VMEM] * 4,
        out_specs=VMEM,
        out_shape=jax.ShapeDtypeStruct((NZ, FACT_TILE + 1 + HALF_TILES, 8, HD), bf16),
        compiler_params=SMALL,
        name="project",
    )(counts, docs, state, down_t, up, frozen)


def fill_bias(place, docs, ends, boxes, bias):
    z_own, x_own = place[0], place[1]
    pair = z_own * NX + x_own
    lane = lax.broadcasted_iota(jnp.int32, (8, NEAR), 1)
    sub = lax.broadcasted_iota(jnp.int32, (8, NEAR), 0)
    side = lane // SPAN
    offset = lane % SPAN
    own_span = jnp.where(side == 0, pair, NCH - 1 - pair).astype(f32)
    own_doc = jnp.where(side == 0, docs[0, 0, 0], docs[0, 0, 1]).astype(f32)
    live = offset < jnp.where(side == 0, ends[0, 0, 0], ends[0, 0, 1])
    for block in range(NEAR // 8):
        key_side = block * 8 // SPAN
        key_offset = sub + (block * 8) % SPAN
        key_live = key_offset < ends[0, 0, key_side]
        seen = (side == key_side) & (key_offset <= offset) & (key_live == live)
        bias[block * 8 : block * 8 + 8, :] = jnp.where(seen, 0.0, MASKED)

    def facts(box, z, slot):
        tile = boxes[box][z, FACT_TILE].astype(f32)
        first, second = tile[0:1], tile[1:2]
        first_doc, second_doc = tile[2:3], tile[3:4]
        source = z * NX + lax.rem(x_own - box + NX, NX)
        low = slot < first
        high = slot < first + second
        span = jnp.where(low, source, NCH - 1 - source).astype(f32)
        doc = jnp.where(low, first_doc, second_doc)
        return jnp.where(high, span, 2.0 * NCH), doc

    def write(at, span, doc):
        seen = live & (span < own_span) & (doc == own_doc)
        bias[at : at + 8, :] = jnp.where(seen, 0.0, MASKED)

    slot = sub.astype(f32)
    for box in range(NX):
        for z in range(NZ):
            write(NEAR + box * 64 + z * 8, *facts(box, z, slot))
        for z in range(0, NZ, 2):
            span_a, doc_a = facts(box, z, slot + 8.0)
            span_b, doc_b = facts(box, z + 1, slot + 4.0)
            write(
                NEAR + 256 + box * 32 + z * 4,
                jnp.where(sub < 4, span_a, span_b),
                jnp.where(sub < 4, doc_a, doc_b),
            )


def gather_low(boxes, low_all):
    lane = lax.broadcasted_iota(jnp.int32, (NZ, 8, HD), 2)
    sub = lax.broadcasted_iota(jnp.int32, (NZ // 2, 8, HD), 1)
    for b, box in enumerate(boxes):
        tile = box[:, LOW_TILE].astype(f32)
        head = jnp.where(lane < UPDATE_RANK, tile, 0.0)
        low_all[b * 64 : b * 64 + 64, :] = head.reshape(64, HD).astype(bf16)
        tail = jnp.where(lane < UPDATE_RANK, pltpu.roll(tile, UPDATE_RANK, 2), 0.0)
        tail = tail.reshape(NZ // 2, 2, 8, HD)
        tail = jnp.where(sub < 4, tail[:, 0], pltpu.roll(tail[:, 1], 4, 1))
        at = 256 + b * 32
        low_all[at : at + 32, :] = tail.reshape(32, HD).astype(bf16)


def attend_kernel(
    place, docs, ends, query, key, value, grad, up_key, up_value, box0, box1, box2, box3,
    bias, low_all, low_before,
    attended, grad_query, grad_key, grad_value, out0, out1, out2, out3, up_key_part,
    up_value_part, low_part, low_total, last,
):
    boxes = (box0, box1, box2, box3)
    outs = (out0, out1, out2, out3)
    g = pl.program_id(0)

    @pl.when(g == 0)
    def _():
        if low_before is None:
            fill_bias(place, docs, ends, boxes, bias)
            gather_low(boxes, low_all)
            low_total[...] = jnp.zeros_like(low_total)
        else:
            low_total[...] = low_before[...]

    sub = lax.broadcasted_iota(jnp.int32, (NZ // 2, 8, HD), 1)

    def stack(ref):
        whole = ref[...].reshape(2 * SPAN, GROUP * HD)
        return jnp.concatenate(
            [whole[:, m * HD : (m + 1) * HD] for m in range(GROUP)], axis=0
        )

    def far_rows(tile):
        return [box[:, tile].astype(f32).reshape(8 * NZ, HD) for box in boxes]

    extra_keys, extra_values = [], []
    for box in boxes:
        both = box[:, 2 * HEADS + g].astype(f32).reshape(NZ // 2, 2, 8, HD)
        even, odd = both[:, 0], both[:, 1]
        extra_keys.append(jnp.where(sub < 4, even, pltpu.roll(odd, 4, 1)).reshape(4 * NZ, HD))
        extra_values.append(jnp.where(sub < 4, pltpu.roll(even, 4, 1), odd).reshape(4 * NZ, HD))
    keys = jnp.concatenate(
        [key[...].reshape(NEAR, HD).astype(f32)] + far_rows(g) + extra_keys, axis=0
    )
    values = jnp.concatenate(
        [value[...].reshape(NEAR, HD).astype(f32)] + far_rows(HEADS + g) + extra_values, axis=0
    )
    keys_t = keys.T.astype(bf16)
    values_t = values.T.astype(bf16)
    keys = keys.astype(bf16)
    values = values.astype(bf16)
    queries = stack(query)
    grads = stack(grad)
    grads_t = grads.astype(f32).T

    scores = dot(keys, queries, ((1,), (1,))) * (SCORE_SCALE * LOG2E)
    scores = scores + jnp.tile(bias[...], (1, GROUP))
    top = jnp.max(scores, axis=0, keepdims=True)
    weights = jnp.exp2(scores - top)
    total = jnp.sum(weights, axis=0, keepdims=True)
    exact = weights * (1.0 / total)
    probs = exact.astype(bf16)
    summed_t = dot(values_t, probs)
    summed = summed_t.T.astype(bf16)
    rounded_t = summed_t.astype(bf16).astype(f32)
    delta = jnp.sum(grads_t * rounded_t, axis=0, keepdims=True)
    grad_probs = dot(values, grads_t.astype(bf16))
    grad_scores = (exact * (grad_probs - delta)).astype(bf16)
    query_grad = (dot(keys_t, grad_scores) * SCORE_SCALE).T.astype(bf16)
    key_grad = dot(grad_scores, queries) * SCORE_SCALE
    value_grad = dot(probs, grads)

    for m in range(GROUP):
        at = slice(m * 2 * SPAN, (m + 1) * 2 * SPAN)
        cols = slice(m * HD, (m + 1) * HD)
        attended[:, :, cols] = summed[at].reshape(2, SPAN, HD)
        grad_query[:, :, cols] = query_grad[at].reshape(2, SPAN, HD)
    grad_key[...] = key_grad[:NEAR].astype(bf16).reshape(2, SPAN, HD)
    grad_value[...] = value_grad[:NEAR].astype(bf16).reshape(2, SPAN, HD)
    for b, out in enumerate(outs):
        at = NEAR + b * 64
        out[:, 0, 0] = key_grad[at : at + 64].reshape(NZ, 8, HD).astype(bf16)
        out[:, 1, 0] = value_grad[at : at + 64].reshape(NZ, 8, HD).astype(bf16)
        at = NEAR + 256 + b * 32
        k = key_grad[at : at + 32].reshape(NZ // 2, 8, HD)
        v = value_grad[at : at + 32].reshape(NZ // 2, 8, HD)
        even = jnp.where(sub < 4, k, pltpu.roll(v, 4, 1)).astype(bf16)
        odd = jnp.where(sub < 4, pltpu.roll(k, 4, 1), v).astype(bf16)
        for i in range(NZ // 2):
            out[2 * i, 2, 0] = even[i]
            out[2 * i + 1, 2, 0] = odd[i]

    far_keys = key_grad[NEAR:].astype(bf16)
    far_values = value_grad[NEAR:].astype(bf16)
    up_key_part[...] = dot(low_all[...], far_keys, ((0,), (0,)))[:UPDATE_RANK]
    up_value_part[...] = dot(low_all[...], far_values, ((0,), (0,)))[:UPDATE_RANK]

    def twice(ref):
        return jnp.concatenate([ref[...], ref[...]], axis=0)

    low_total[...] += dot(far_keys, twice(up_key), ((1,), (1,)))
    low_total[...] += dot(far_values, twice(up_value), ((1,), (1,)))

    if not last:
        return

    @pl.when(g == HEADS - 1)
    def _():
        lane = lax.broadcasted_iota(jnp.int32, (8, HD), 1)
        for b in range(NX):
            x = lax.rem(place[1] - b + NX, NX)
            for z in range(NZ):
                at = b * 64 + z * 8
                head = low_total[at : at + 8, :]
                at = 256 + b * 32 + z // 2 * 8
                tail = low_total[at : at + 8, :]
                if z % 2:
                    tail = pltpu.roll(tail, 4, 0)
                low_part[z, x] = jnp.where(lane < UPDATE_RANK, head, tail).astype(bf16)


def first_kernel(*refs):
    (place, docs, ends, query, key, value, grad, up_key, up_value, *boxes) = refs[:13]
    (attended, grad_query, grad_key, grad_value, *rest) = refs[13:]
    outs, (up_k, up_v, low_total, bias, low_all) = rest[:4], rest[4:]
    attend_kernel(
        place, docs, ends, query, key, value, grad, up_key, up_value, *boxes,
        bias, low_all, None,
        attended, grad_query, grad_key, grad_value, *outs, up_k, up_v, None, low_total, False,
    )


def second_kernel(*refs):
    (place, query, key, value, grad, up_key, up_value, *boxes) = refs[:11]
    bias, low_all, low_before = refs[11:14]
    (attended, grad_query, grad_key, grad_value, *rest) = refs[18:]
    outs, (up_k, up_v, low_part, low_total) = rest[:4], rest[4:]
    attend_kernel(
        place, None, None, query, key, value, grad, up_key, up_value, *boxes,
        bias, low_all, low_before,
        attended, grad_query, grad_key, grad_value, *outs, up_k, up_v, low_part, low_total, True,
    )


def attend(half, small, query, key, value, grad, up, boxes, carried=(), filled=()):
    at = half * HEADS
    wide = pl.BlockSpec((2, SPAN, GROUP * HD), lambda g: (0, 0, g + at))
    narrow = pl.BlockSpec((2, SPAN, HD), lambda g: (0, 0, g + at))
    whole = pl.BlockSpec(boxes[0].shape, lambda g: (0, 0, 0, 0))
    part = pl.BlockSpec((NZ, 3, 1, 8, HD), lambda g: (0, 0, g, 0, 0))
    up_key = pl.BlockSpec((UPDATE_RANK, HD), lambda g: (0, g + at))
    up_value = pl.BlockSpec((UPDATE_RANK, HD), lambda g: (0, KVH + g + at))
    up_part = pl.BlockSpec((UPDATE_RANK, HD), lambda g: (0, g))
    low_part = pl.BlockSpec((NZ, NX, 8, HD), lambda g: (0, 0, 0, 0))
    wide_shape = jax.ShapeDtypeStruct((2, SPAN, QW), bf16)
    narrow_shape = jax.ShapeDtypeStruct((2, SPAN, KEY_FEATURES), bf16)
    part_shape = jax.ShapeDtypeStruct((NZ, 3, HEADS, 8, HD), bf16)
    up_shape = jax.ShapeDtypeStruct((UPDATE_RANK, HEADS * HD), f32)
    kept = [
        jax.ShapeDtypeStruct((FAR, HD), f32),
        jax.ShapeDtypeStruct((KEYS, NEAR), f32),
        jax.ShapeDtypeStruct((FAR, HD), bf16),
    ]
    kept_specs = [pl.BlockSpec(k.shape, lambda g: (0, 0)) for k in kept]
    in_specs = [SMEM] * len(small) + [wide, narrow, narrow, wide, up_key, up_value] + [whole] * NX
    out_specs = [wide, wide, narrow, narrow] + [part] * NX + [up_part] * 2
    out_shape = [wide_shape] * 2 + [narrow_shape] * 2
    out_shape += [pltpu.HBM(part_shape.shape, bf16)] + [part_shape] * (NX - 1)
    out_shape += [pltpu.HBM(up_shape.shape, f32)] * 2
    scratch, aliases = [], {}
    if half == 0:
        out_specs += kept_specs
        out_shape += kept
    else:
        in_specs += kept_specs[1:] + kept_specs[:1] + [pl.BlockSpec(memory_space=pl.ANY)] * 4
        out_specs.append(low_part)
        out_shape.append(jax.ShapeDtypeStruct((NZ, NX, 8, HD), bf16))
        scratch = [pltpu.VMEM((FAR, HD), f32)]
        aliases = {len(in_specs) - 4 + i: i for i in range(4)}
    return pl.pallas_call(
        (first_kernel, second_kernel)[half],
        grid=(HEADS,),
        in_specs=in_specs,
        out_specs=out_specs,
        out_shape=out_shape,
        scratch_shapes=scratch,
        input_output_aliases=aliases,
        compiler_params=pltpu.CompilerParams(vmem_limit_bytes=20 * 1024 * 1024),
        cost_estimate=pl.CostEstimate(
            flops=6 * 10**9, bytes_accessed=4 * 2**20, transcendentals=HEADS * KEYS * ROWS
        ),
        name=("attend_first", "attend_second")[half],
    )(*small, query, key, value, grad, up, up, *boxes, *carried, *filled)


PER_ROW = (MODEL_WIDTH + 2 * KEY_FEATURES) // HD
CHUNK = 12
CHUNKS = NX * NY
HALF = CHUNKS * CHUNK


def factor_kernel(place, counts, low_parts, state, key_a, value_a, key_b, value_b, keep, send):
    pick = selection(counts[0, 0, 0], counts[0, 0, 1])
    total = jnp.sum(low_parts[...].astype(f32), axis=0)
    compact = jnp.concatenate([total, pltpu.roll(total, UPDATE_RANK, 1)], axis=0).astype(bf16)
    low_grad = dot(pick.astype(bf16), compact, ((0,), (0,))).astype(bf16)
    down_piece = dot(low_grad, state[...], ((0,), (0,)))
    wide = MODEL_WIDTH // HD
    ups = (key_a, key_b, value_a, value_b)

    def tile(t):
        r, c = divmod(t, PER_ROW)
        rows = slice(r * 8, r * 8 + 8)
        if c < wide:
            return down_piece[rows, c * HD : (c + 1) * HD]
        which, c = divmod(c - wide, HEADS)
        return ups[which][rows, c * HD : (c + 1) * HD]

    lower = place[2] == 0
    for t in range(HALF):
        a, b = tile(t), tile(HALF + t)
        keep[t // CHUNK, t % CHUNK] = jnp.where(lower, a, b).astype(bf16)
        send[t // CHUNK, t % CHUNK] = jnp.where(lower, b, a).astype(bf16)


def factor(place, counts, low_parts, state, ups):
    return pl.pallas_call(
        factor_kernel,
        in_specs=[SMEM] * 2 + [VMEM] * 6,
        out_specs=[VMEM] * 2,
        out_shape=[jax.ShapeDtypeStruct((CHUNKS, CHUNK, 8, HD), bf16)] * 2,
        compiler_params=SMALL,
        name="factor",
    )(place, counts, low_parts, state, *ups)


def middle_kernel(pieces, *refs):
    out = refs[-1]
    chunk = jnp.sum(pieces[...].astype(f32), axis=0).astype(bf16)
    for z in range(NZ):
        out[z, :CHUNK] = chunk
        for half in range(2):
            a, b, c, d = refs[half * NX : half * NX + NX]
            at = CHUNK + half * HALF_TILES
            out[z, at : at + HALF_TILES] = (
                (a[z].astype(f32) + b[z].astype(f32)) + (c[z].astype(f32) + d[z].astype(f32))
            ).astype(bf16)


def middle(pieces, parts):
    return pl.pallas_call(
        middle_kernel,
        in_specs=[VMEM] * (1 + len(parts)),
        out_specs=VMEM,
        out_shape=jax.ShapeDtypeStruct((NZ, CHUNK + 2 * HALF_TILES, 8, HD), bf16),
        compiler_params=SMALL,
        name="middle",
    )(pieces, *parts)


def close_kernel(counts, parts, cache_out, out):
    pick = selection(counts[0, 0, 0], counts[0, 0, 1]).astype(bf16)
    total = jnp.sum(parts[...].astype(f32), axis=0)
    chunk = total[:CHUNK].astype(bf16)
    for i in range(CHUNKS):
        out[i] = chunk
    sub = lax.broadcasted_iota(jnp.int32, (8, HD), 0)
    top_keys, top_values, rest_keys, rest_values = [], [], [], []
    for h in range(KVH):
        at = CHUNK + h // HEADS * HALF_TILES + h % HEADS
        top_keys.append(total[at])
        top_values.append(total[at + HEADS])
        both = total[at + 2 * HEADS]
        rest_keys.append(jnp.where(sub < 4, both, 0.0))
        rest_values.append(jnp.where(sub < 4, pltpu.roll(both, 4, 0), 0.0))
    compact = jnp.concatenate(
        [
            jnp.concatenate(top_keys + top_values, axis=1),
            jnp.concatenate(rest_keys + rest_values, axis=1),
        ],
        axis=0,
    ).astype(bf16)
    cache_out[...] = dot(pick, compact, ((0,), (0,))).astype(bf16)


def close(counts, parts):
    return pl.pallas_call(
        close_kernel,
        in_specs=[SMEM, VMEM],
        out_specs=[VMEM, VMEM],
        out_shape=[
            jax.ShapeDtypeStruct((16, 2 * KEY_FEATURES), bf16),
            jax.ShapeDtypeStruct((CHUNKS, CHUNK, 8, HD), bf16),
        ],
        compiler_params=SMALL,
        name="close",
    )(counts, parts)


def unpack_kernel(place, mine, other, out):
    lower = place[2] == 0
    for t in range(HALF):
        a = mine[t // CHUNK, t % CHUNK].astype(f32)
        b = other[t // CHUNK, t % CHUNK].astype(f32)
        for at, tile in ((t, jnp.where(lower, a, b)), (t + HALF, jnp.where(lower, b, a))):
            r, c = divmod(at, PER_ROW)
            out[r * 8 : r * 8 + 8, c * HD : (c + 1) * HD] = tile


def unpack(place, mine, other):
    return pl.pallas_call(
        unpack_kernel,
        in_specs=[SMEM] + [VMEM] * 2,
        out_specs=VMEM,
        out_shape=jax.ShapeDtypeStruct((UPDATE_RANK, MODEL_WIDTH + 2 * KEY_FEATURES), f32),
        compiler_params=SMALL,
        name="unpack",
    )(place, mine, other)


def exchange(x, axes):
    return lax.all_to_all(x, axes, 0, 0, tiled=True)


def shift(x, by):
    return lax.ppermute(x, "x", [(i, (i + by) % NX) for i in range(NX)])


def swap(x):
    return lax.ppermute(x, "core", [(0, 1), (1, 0)])


def spread(column):
    return [column, shift(column, 1), shift(column, 2), shift(column, 3)]


def collect(parts):
    parts = [p.reshape(NZ, HALF_TILES, 8, HD) for p in parts]
    return [parts[0], shift(parts[1], -1), shift(parts[2], -2), shift(parts[3], -3)]


def local(
    query, key, value, beacon_slot_state, frozen_beacon_cache, adapter_down_weight,
    adapter_up_weight, output_cotangent, span_beacon_count, span_document, boundary,
):
    place = jnp.stack([lax.axis_index(axis) for axis in ("z", "x", "core")]).astype(jnp.int32)
    state = beacon_slot_state[0, 0].reshape(2 * MAX_BEACONS, MODEL_WIDTH)
    frozen = frozen_beacon_cache[0, 0].reshape(2 * MAX_BEACONS, 2 * KEY_FEATURES)

    message = project(
        span_beacon_count, span_document, state, adapter_down_weight.T, adapter_up_weight, frozen
    )
    arrays = (query[0, 0], key[0, 0], value[0, 0], output_cotangent[0, 0], adapter_up_weight)
    column = exchange(message, "z")
    boxes_a = spread(column[:, : FACT_TILE + 1])
    boxes_b = spread(column[:, FACT_TILE + 1 :])
    first = attend(0, (place, span_document, boundary), *arrays, boxes_a)
    low_total, bias, low_all = first[10:]
    parts_a = collect(first[4:8])
    second = attend(1, (place,), *arrays, boxes_b, (bias, low_all, low_total), first[:4])
    parts_b = collect(second[4:8])
    attended, grad_query, grad_key, grad_value = second[:4]
    low_part, parts_a = lax.optimization_barrier((second[10], parts_a))
    low_parts = exchange(low_part.reshape(NZ * NX, 8, HD), ("z", "x"))
    low_parts, parts_b = lax.optimization_barrier((low_parts, parts_b))
    keep, send = factor(place, span_beacon_count, low_parts, state, first[8:10] + second[8:10])
    pieces = (keep.astype(f32) + swap(send).astype(f32)).astype(bf16)
    both = exchange(middle(exchange(pieces, PLANE), parts_a + parts_b), "z")
    cache_gradient, chunk = close(span_beacon_count, both)
    mine = exchange(chunk, PLANE)
    adapter_gradient = unpack(place, mine, swap(mine))
    return (
        attended[None, None],
        grad_query[None, None],
        grad_key[None, None],
        grad_value[None, None],
        cache_gradient.reshape(1, 1, 2, MAX_BEACONS, 2 * KEY_FEATURES),
        adapter_gradient,
    )


def solution(mesh):
    chips = Mesh(mesh.devices.reshape(NZ, NX, NY, NC), ALL_AXES)
    dp, ctx = ("y", "core"), ("z", "x")
    array5 = P(dp, ctx, None, None, None)
    array3 = P(dp, ctx, None)
    return jax.shard_map(
        local,
        mesh=chips,
        in_specs=(array5, array5, array5, array5, array5, P(), P(), array5, array3, array3, array3),
        out_specs=(array5, array5, array5, array5, array5, P()),
        check_vma=False,
    )
```

```python
import jax
import jax.numpy as jnp
from jax import lax
from jax.experimental import pallas as pl
from jax.experimental.pallas import tpu as pltpu
from jax.sharding import Mesh, PartitionSpec as P

MODEL_WIDTH = 4096
KVH = 8
HD = 128
SPAN = 64
MAX_BEACONS = 8
UPDATE_RANK = 64
GROUP = 4
QW = 4096
KEY_FEATURES = 1024
NCH = 64
NZ, NX, NY, NC = 8, 4, 4, 2

bf16 = jnp.bfloat16
f32 = jnp.float32
ALL_AXES = ("z", "x", "y", "core")
PLANE = ("x", "y")

HEADS = 4
HALF_TILES = 3 * HEADS
LOW_TILE = HALF_TILES
FAR = 384
NEAR = 128
KEYS = FAR + NEAR
ROWS = GROUP * 2 * SPAN
MASKED = -1e30
SCORE_SCALE = HD ** (-0.5)
LOG2E = 1.4426950408889634


def dot(a, b, dims=((1,), (0,))):
    return lax.dot_general(a, b, (dims, ((), ())), preferred_element_type=f32)


def selection(first, second):
    row = lax.broadcasted_iota(jnp.int32, (16, 16), 0)
    slot = lax.broadcasted_iota(jnp.int32, (16, 16), 1)
    source = jnp.where(row < first, row, row - first + MAX_BEACONS)
    return jnp.where((slot == source) & (row < first + second), 1.0, 0.0)


def project_kernel(counts, docs, state, down_t, up, frozen, out):
    first, second = counts[0, 0, 0], counts[0, 0, 1]
    low = dot(state[...], down_t[...], ((1,), (1,))).astype(bf16)
    states = (frozen[...].astype(f32) + dot(low, up[...])).astype(bf16)
    pick = selection(first, second).astype(bf16)
    rows = dot(pick, states)
    low_rows = dot(pick, low).astype(bf16)
    sub = lax.broadcasted_iota(jnp.int32, (8, HD), 0)
    halves = []
    for heads in (range(HEADS), range(HEADS, KVH)):
        tiles = [rows[:8, h * HD : (h + 1) * HD] for h in heads]
        tiles += [rows[:8, (KVH + h) * HD : (KVH + h + 1) * HD] for h in heads]
        for h in heads:
            keys = rows[8:, h * HD : (h + 1) * HD]
            values = rows[8:, (KVH + h) * HD : (KVH + h + 1) * HD]
            tiles.append(jnp.where(sub < 4, keys, pltpu.roll(values, 4, 0)))
        halves.append(tiles)
    put_row = lax.broadcasted_iota(jnp.int32, (UPDATE_RANK, HD), 0)
    put_col = lax.broadcasted_iota(jnp.int32, (UPDATE_RANK, HD), 1)
    left = jnp.where(put_row == put_col, 1.0, 0.0).astype(bf16)
    right = jnp.where(put_row + UPDATE_RANK == put_col, 1.0, 0.0).astype(bf16)
    extra = dot(low_rows, left)[:8] + dot(low_rows, right)[8:]
    side = lax.broadcasted_iota(jnp.int32, (8, HD), 1) >= UPDATE_RANK
    for i, fact in enumerate((first, second, docs[0, 0, 0], docs[0, 0, 1])):
        extra = jnp.where(side & (sub == 4 + i), fact.astype(f32), extra)
    halves[0].append(extra)
    for t, tile in enumerate(halves[0] + halves[1]):
        packed = tile.astype(bf16)
        for z in range(NZ):
            out[z, t] = packed


VMEM = pl.BlockSpec(memory_space=pltpu.VMEM)
SMEM = pl.BlockSpec(memory_space=pltpu.SMEM)
SMALL = pltpu.CompilerParams(vmem_limit_bytes=8 * 1024 * 1024)


def project(counts, docs, state, down_t, up, frozen):
    return pl.pallas_call(
        project_kernel,
        in_specs=[SMEM] * 2 + [VMEM] * 4,
        out_specs=VMEM,
        out_shape=jax.ShapeDtypeStruct((NZ, LOW_TILE + 1 + HALF_TILES, 8, HD), bf16),
        name="project",
    )(counts, docs, state, down_t, up, frozen)


def fill_bias(place, docs, ends, boxes, bias):
    z_own, x_own = place[0], place[1]
    pair = z_own * NX + x_own
    lane = lax.broadcasted_iota(jnp.int32, (8, NEAR), 1)
    sub = lax.broadcasted_iota(jnp.int32, (8, NEAR), 0)
    side = lane // SPAN
    offset = lane % SPAN
    own_span = jnp.where(side == 0, pair, NCH - 1 - pair).astype(f32)
    own_doc = jnp.where(side == 0, docs[0, 0, 0], docs[0, 0, 1]).astype(f32)
    live = offset < jnp.where(side == 0, ends[0, 0, 0], ends[0, 0, 1])
    for block in range(NEAR // 8):
        key_side = block * 8 // SPAN
        key_offset = sub + (block * 8) % SPAN
        key_live = key_offset < ends[0, 0, key_side]
        seen = (side == key_side) & (key_offset <= offset) & (key_live == live)
        bias[block * 8 : block * 8 + 8, :] = jnp.where(seen, 0.0, MASKED)

    def facts(box, z, slot):
        tile = boxes[box][z, LOW_TILE].astype(f32)
        tile = jnp.where(lane < UPDATE_RANK, pltpu.roll(tile, UPDATE_RANK, 1), tile)
        first, second = tile[4:5], tile[5:6]
        first_doc, second_doc = tile[6:7], tile[7:8]
        source = z * NX + lax.rem(x_own - box + NX, NX)
        low = slot < first
        high = slot < first + second
        span = jnp.where(low, source, NCH - 1 - source).astype(f32)
        doc = jnp.where(low, first_doc, second_doc)
        return jnp.where(high, span, 2.0 * NCH), doc

    def write(at, span, doc):
        seen = live & (span < own_span) & (doc == own_doc)
        bias[at : at + 8, :] = jnp.where(seen, 0.0, MASKED)

    slot = sub.astype(f32)
    for box in range(NX):
        for z in range(NZ):
            write(NEAR + box * 64 + z * 8, *facts(box, z, slot))
        for z in range(0, NZ, 2):
            span_a, doc_a = facts(box, z, slot + 8.0)
            span_b, doc_b = facts(box, z + 1, slot + 4.0)
            write(
                NEAR + 256 + box * 32 + z * 4,
                jnp.where(sub < 4, span_a, span_b),
                jnp.where(sub < 4, doc_a, doc_b),
            )


def gather_low(boxes, low_all):
    rows = [None] * (2 * NX)
    lane = lax.broadcasted_iota(jnp.int32, (NZ, 8, HD), 2)
    sub = lax.broadcasted_iota(jnp.int32, (NZ // 2, 8, HD), 1)
    for b, box in enumerate(boxes):
        tile = box[:, LOW_TILE].astype(f32)
        head = jnp.where(lane < UPDATE_RANK, tile, 0.0)
        rows[b] = head.reshape(64, HD)
        tail = jnp.where(lane < UPDATE_RANK, pltpu.roll(tile, UPDATE_RANK, 2), 0.0)
        tail = tail.reshape(NZ // 2, 2, 8, HD)
        tail = jnp.where(sub < 4, tail[:, 0], pltpu.roll(tail[:, 1], 4, 1))
        rows[NX + b] = tail.reshape(32, HD)
    low_all[...] = jnp.concatenate(rows, axis=0).T[:UPDATE_RANK].astype(bf16)


def attend_kernel(
    place, docs, ends, query, key, value, grad, up_key, up_value, box0, box1, box2, box3,
    bias, low_all, low_before,
    attended, grad_query, grad_key, grad_value, out0, out1, out2, out3, up_key_part,
    up_value_part, low_part, low_total, last,
):
    boxes = (box0, box1, box2, box3)
    outs = (out0, out1, out2, out3)
    g = pl.program_id(0)

    @pl.when(g == 0)
    def _():
        if low_before is None:
            fill_bias(place, docs, ends, boxes, bias)
            gather_low(boxes, low_all)
            low_total[...] = jnp.zeros_like(low_total)
        else:
            low_total[...] = low_before[...]

    sub = lax.broadcasted_iota(jnp.int32, (NZ // 2, 8, HD), 1)

    def stack(ref):
        whole = ref[...].reshape(2 * SPAN, GROUP * HD)
        return jnp.concatenate(
            [whole[:, m * HD : (m + 1) * HD] for m in range(GROUP)], axis=0
        )

    def far_rows(tile):
        return [box[:, tile].astype(f32).reshape(8 * NZ, HD) for box in boxes]

    extra_keys, extra_values = [], []
    for box in boxes:
        both = box[:, 2 * HEADS + g].astype(f32).reshape(NZ // 2, 2, 8, HD)
        even, odd = both[:, 0], both[:, 1]
        extra_keys.append(jnp.where(sub < 4, even, pltpu.roll(odd, 4, 1)).reshape(4 * NZ, HD))
        extra_values.append(jnp.where(sub < 4, pltpu.roll(even, 4, 1), odd).reshape(4 * NZ, HD))
    keys = jnp.concatenate(
        [key[...].reshape(NEAR, HD).astype(f32)] + far_rows(g) + extra_keys, axis=0
    )
    values = jnp.concatenate(
        [value[...].reshape(NEAR, HD).astype(f32)] + far_rows(HEADS + g) + extra_values, axis=0
    )
    keys = keys.astype(bf16)
    values = values.astype(bf16)
    keys_t = keys.T
    values_t = values.T
    queries = stack(query)
    grads = stack(grad)
    grads_t = grads.T

    scores = dot(keys, queries, ((1,), (1,))) * (SCORE_SCALE * LOG2E)
    scores = scores + jnp.tile(bias[...], (1, GROUP))
    top = jnp.max(scores, axis=0, keepdims=True)
    weights = jnp.exp2(scores - top)
    total = jnp.sum(weights, axis=0, keepdims=True)
    exact = weights * (1.0 / total)
    probs = exact.astype(bf16)
    summed_t = dot(values_t, probs)
    rounded_t = summed_t.astype(bf16)
    summed = rounded_t.T
    delta = jnp.sum(grads_t.astype(f32) * rounded_t.astype(f32), axis=0, keepdims=True)
    grad_probs = dot(values, grads_t)
    grad_scores = (exact * (grad_probs - delta)).astype(bf16)
    query_grad = (dot(keys_t, grad_scores) * SCORE_SCALE).astype(bf16).T
    key_grad = dot(grad_scores, queries) * SCORE_SCALE
    value_grad = dot(probs, grads)

    for m in range(GROUP):
        at = slice(m * 2 * SPAN, (m + 1) * 2 * SPAN)
        cols = slice(m * HD, (m + 1) * HD)
        attended[:, :, cols] = summed[at].reshape(2, SPAN, HD)
        grad_query[:, :, cols] = query_grad[at].reshape(2, SPAN, HD)
    grad_key[...] = key_grad[:NEAR].astype(bf16).reshape(2, SPAN, HD)
    grad_value[...] = value_grad[:NEAR].astype(bf16).reshape(2, SPAN, HD)
    for b, out in enumerate(outs):
        at = NEAR + b * 64
        out[:, 0, 0] = key_grad[at : at + 64].reshape(NZ, 8, HD).astype(bf16)
        out[:, 1, 0] = value_grad[at : at + 64].reshape(NZ, 8, HD).astype(bf16)
        at = NEAR + 256 + b * 32
        k = key_grad[at : at + 32].reshape(NZ // 2, 8, HD)
        v = value_grad[at : at + 32].reshape(NZ // 2, 8, HD)
        even = jnp.where(sub < 4, k, pltpu.roll(v, 4, 1)).astype(bf16)
        odd = jnp.where(sub < 4, pltpu.roll(k, 4, 1), v).astype(bf16)
        for i in range(NZ // 2):
            out[2 * i, 2, 0] = even[i]
            out[2 * i + 1, 2, 0] = odd[i]

    far_keys = key_grad[NEAR:].astype(bf16)
    far_values = value_grad[NEAR:].astype(bf16)
    far = jnp.concatenate([far_keys, far_values], axis=1)
    up_part = dot(low_all[...], far)
    up_key_part[...] = up_part[:, :HD]
    up_value_part[...] = up_part[:, HD:]
    up_both = jnp.concatenate([up_key[...], up_value[...]], axis=1)
    low_total[...] += dot(far, jnp.concatenate([up_both, up_both], axis=0), ((1,), (1,)))

    if not last:
        return

    @pl.when(g == HEADS - 1)
    def _():
        lane = lax.broadcasted_iota(jnp.int32, (8, HD), 1)
        for b in range(NX):
            x = lax.rem(place[1] - b + NX, NX)
            for z in range(NZ):
                at = b * 64 + z * 8
                head = low_total[at : at + 8, :]
                at = 256 + b * 32 + z // 2 * 8
                tail = low_total[at : at + 8, :]
                if z % 2:
                    tail = pltpu.roll(tail, 4, 0)
                low_part[z, x] = jnp.where(lane < UPDATE_RANK, head, tail).astype(bf16)


def first_kernel(*refs):
    (place, docs, ends, query, key, value, grad, up_key, up_value, *boxes) = refs[:13]
    (attended, grad_query, grad_key, grad_value, *rest) = refs[13:]
    outs, (up_k, up_v, low_total, bias, low_all) = rest[:4], rest[4:]
    attend_kernel(
        place, docs, ends, query, key, value, grad, up_key, up_value, *boxes,
        bias, low_all, None,
        attended, grad_query, grad_key, grad_value, *outs, up_k, up_v, None, low_total, False,
    )


def second_kernel(*refs):
    (place, query, key, value, grad, up_key, up_value, *boxes) = refs[:11]
    bias, low_all, low_before = refs[11:14]
    (attended, grad_query, grad_key, grad_value, *rest) = refs[18:]
    outs, (up_k, up_v, low_part, low_total) = rest[:4], rest[4:]
    attend_kernel(
        place, None, None, query, key, value, grad, up_key, up_value, *boxes,
        bias, low_all, low_before,
        attended, grad_query, grad_key, grad_value, *outs, up_k, up_v, low_part, low_total, True,
    )


def attend(half, small, query, key, value, grad, up, boxes, carried=(), filled=()):
    at = half * HEADS
    wide = pl.BlockSpec((2, SPAN, GROUP * HD), lambda g: (0, 0, g + at))
    narrow = pl.BlockSpec((2, SPAN, HD), lambda g: (0, 0, g + at))
    whole = pl.BlockSpec(boxes[0].shape, lambda g: (0, 0, 0, 0))
    part = pl.BlockSpec((NZ, 3, 1, 8, HD), lambda g: (0, 0, g, 0, 0))
    up_key = pl.BlockSpec((UPDATE_RANK, HD), lambda g: (0, g + at))
    up_value = pl.BlockSpec((UPDATE_RANK, HD), lambda g: (0, KVH + g + at))
    up_part = pl.BlockSpec((UPDATE_RANK, HD), lambda g: (0, g))
    low_part = pl.BlockSpec((NZ, NX, 8, HD), lambda g: (0, 0, 0, 0))
    wide_shape = jax.ShapeDtypeStruct((2, SPAN, QW), bf16)
    narrow_shape = jax.ShapeDtypeStruct((2, SPAN, KEY_FEATURES), bf16)
    part_shape = jax.ShapeDtypeStruct((NZ, 3, HEADS, 8, HD), bf16)
    up_shape = jax.ShapeDtypeStruct((UPDATE_RANK, HEADS * HD), f32)
    kept = [
        jax.ShapeDtypeStruct((FAR, HD), f32),
        jax.ShapeDtypeStruct((KEYS, NEAR), f32),
        jax.ShapeDtypeStruct((UPDATE_RANK, FAR), bf16),
    ]
    kept_specs = [pl.BlockSpec(k.shape, lambda g: (0, 0)) for k in kept]
    in_specs = [SMEM] * len(small) + [wide, narrow, narrow, wide, up_key, up_value] + [whole] * NX
    out_specs = [wide, wide, narrow, narrow] + [part] * NX + [up_part] * 2
    out_shape = [wide_shape] * 2 + [narrow_shape] * 2
    out_shape += [part_shape] * NX + [up_shape] * 2
    scratch, aliases = [], {}
    if half == 0:
        out_specs += kept_specs
        out_shape += kept
    else:
        in_specs += kept_specs[1:] + kept_specs[:1] + [pl.BlockSpec(memory_space=pl.ANY)] * 4
        out_specs.append(low_part)
        out_shape.append(jax.ShapeDtypeStruct((NZ, NX, 8, HD), bf16))
        scratch = [pltpu.VMEM((FAR, HD), f32)]
        aliases = {len(in_specs) - 4 + i: i for i in range(4)}
    return pl.pallas_call(
        (first_kernel, second_kernel)[half],
        grid=(HEADS,),
        in_specs=in_specs,
        out_specs=out_specs,
        out_shape=out_shape,
        scratch_shapes=scratch,
        input_output_aliases=aliases,
        compiler_params=pltpu.CompilerParams(vmem_limit_bytes=20 * 1024 * 1024),
        cost_estimate=pl.CostEstimate(
            flops=6 * 10**9, bytes_accessed=4 * 2**20, transcendentals=HEADS * KEYS * ROWS
        ),
        name=("attend_first", "attend_second")[half],
    )(*small, query, key, value, grad, up, up, *boxes, *carried, *filled)


PER_ROW = (MODEL_WIDTH + 2 * KEY_FEATURES) // HD
CHUNK = 12
CHUNKS = NX * NY
HALF = CHUNKS * CHUNK


def factor_kernel(place, counts, low_parts, state, key_a, value_a, key_b, value_b, keep, send):
    pick = selection(counts[0, 0, 0], counts[0, 0, 1])
    total = jnp.sum(low_parts[...].astype(f32), axis=0)
    compact = jnp.concatenate([total, pltpu.roll(total, UPDATE_RANK, 1)], axis=0).astype(bf16)
    low_grad = dot(pick.astype(bf16), compact, ((0,), (0,))).astype(bf16)
    down_piece = dot(low_grad, state[...], ((0,), (0,)))
    wide = MODEL_WIDTH // HD
    ups = (key_a, key_b, value_a, value_b)

    def tile(t):
        r, c = divmod(t, PER_ROW)
        rows = slice(r * 8, r * 8 + 8)
        if c < wide:
            return down_piece[rows, c * HD : (c + 1) * HD]
        which, c = divmod(c - wide, HEADS)
        return ups[which][rows, c * HD : (c + 1) * HD]

    lower = place[2] == 0
    for t in range(HALF):
        a, b = tile(t), tile(HALF + t)
        keep[t // CHUNK, t % CHUNK] = jnp.where(lower, a, b).astype(bf16)
        send[t // CHUNK, t % CHUNK] = jnp.where(lower, b, a).astype(bf16)


def factor(place, counts, low_parts, state, ups):
    return pl.pallas_call(
        factor_kernel,
        in_specs=[SMEM] * 2 + [VMEM] * 6,
        out_specs=[VMEM] * 2,
        out_shape=[jax.ShapeDtypeStruct((CHUNKS, CHUNK, 8, HD), bf16)] * 2,
        compiler_params=SMALL,
        name="factor",
    )(place, counts, low_parts, state, *ups)


def middle_kernel(pieces, *refs):
    out = refs[-1]
    chunk = jnp.sum(pieces[...].astype(f32), axis=0).astype(bf16)
    for z in range(NZ):
        out[z, :CHUNK] = chunk
        for half in range(2):
            a, b, c, d = refs[half * NX : half * NX + NX]
            at = CHUNK + half * HALF_TILES
            out[z, at : at + HALF_TILES] = (
                (a[z].astype(f32) + b[z].astype(f32)) + (c[z].astype(f32) + d[z].astype(f32))
            ).astype(bf16)


def middle(pieces, parts):
    return pl.pallas_call(
        middle_kernel,
        in_specs=[VMEM] * (1 + len(parts)),
        out_specs=VMEM,
        out_shape=jax.ShapeDtypeStruct((NZ, CHUNK + 2 * HALF_TILES, 8, HD), bf16),
        compiler_params=SMALL,
        name="middle",
    )(pieces, *parts)


def close_kernel(counts, parts, cache_out, out):
    pick = selection(counts[0, 0, 0], counts[0, 0, 1]).astype(bf16)
    total = jnp.sum(parts[...].astype(f32), axis=0)
    chunk = total[:CHUNK].astype(bf16)
    for i in range(CHUNKS):
        out[i] = chunk
    sub = lax.broadcasted_iota(jnp.int32, (8, HD), 0)
    top_keys, top_values, rest_keys, rest_values = [], [], [], []
    for h in range(KVH):
        at = CHUNK + h // HEADS * HALF_TILES + h % HEADS
        top_keys.append(total[at])
        top_values.append(total[at + HEADS])
        both = total[at + 2 * HEADS]
        rest_keys.append(jnp.where(sub < 4, both, 0.0))
        rest_values.append(jnp.where(sub < 4, pltpu.roll(both, 4, 0), 0.0))
    compact = jnp.concatenate(
        [
            jnp.concatenate(top_keys + top_values, axis=1),
            jnp.concatenate(rest_keys + rest_values, axis=1),
        ],
        axis=0,
    ).astype(bf16)
    cache_out[...] = dot(pick, compact, ((0,), (0,))).astype(bf16)


def close(counts, parts):
    return pl.pallas_call(
        close_kernel,
        in_specs=[SMEM, VMEM],
        out_specs=[VMEM, VMEM],
        out_shape=[
            jax.ShapeDtypeStruct((16, 2 * KEY_FEATURES), bf16),
            jax.ShapeDtypeStruct((CHUNKS, CHUNK, 8, HD), bf16),
        ],
        compiler_params=SMALL,
        name="close",
    )(counts, parts)


def unpack_kernel(place, mine, other, out):
    lower = place[2] == 0
    for t in range(HALF):
        a = mine[t // CHUNK, t % CHUNK].astype(f32)
        b = other[t // CHUNK, t % CHUNK].astype(f32)
        for at, tile in ((t, jnp.where(lower, a, b)), (t + HALF, jnp.where(lower, b, a))):
            r, c = divmod(at, PER_ROW)
            out[r * 8 : r * 8 + 8, c * HD : (c + 1) * HD] = tile


def unpack(place, mine, other):
    return pl.pallas_call(
        unpack_kernel,
        in_specs=[SMEM] + [VMEM] * 2,
        out_specs=VMEM,
        out_shape=jax.ShapeDtypeStruct((UPDATE_RANK, MODEL_WIDTH + 2 * KEY_FEATURES), f32),
        compiler_params=SMALL,
        name="unpack",
    )(place, mine, other)


def exchange(x, axes):
    return lax.all_to_all(x, axes, 0, 0, tiled=True)


def shift(x, by):
    return lax.ppermute(x, "x", [(i, (i + by) % NX) for i in range(NX)])


def swap(x):
    return lax.ppermute(x, "core", [(0, 1), (1, 0)])


def spread(column):
    return [column, shift(column, 1), shift(column, 2), shift(column, 3)]


def collect(parts):
    parts = [p.reshape(NZ, HALF_TILES, 8, HD) for p in parts]
    return [parts[0], shift(parts[1], -1), shift(parts[2], -2), shift(parts[3], -3)]


def local(
    query, key, value, beacon_slot_state, frozen_beacon_cache, adapter_down_weight,
    adapter_up_weight, output_cotangent, span_beacon_count, span_document, boundary,
):
    place = jnp.stack([lax.axis_index(axis) for axis in ("z", "x", "core")]).astype(jnp.int32)
    state = beacon_slot_state[0, 0].reshape(2 * MAX_BEACONS, MODEL_WIDTH)
    frozen = frozen_beacon_cache[0, 0].reshape(2 * MAX_BEACONS, 2 * KEY_FEATURES)

    message = project(
        span_beacon_count, span_document, state, adapter_down_weight.T, adapter_up_weight, frozen
    )
    arrays = (query[0, 0], key[0, 0], value[0, 0], output_cotangent[0, 0], adapter_up_weight)
    column = exchange(message, "z")
    boxes_a = spread(column[:, : LOW_TILE + 1])
    boxes_b = spread(column[:, LOW_TILE + 1 :])
    first = attend(0, (place, span_document, boundary), *arrays, boxes_a)
    low_total, bias, low_all = first[10:]
    parts_a = collect(first[4:8])
    second = attend(1, (place,), *arrays, boxes_b, (bias, low_all, low_total), first[:4])
    parts_b = collect(second[4:8])
    attended, grad_query, grad_key, grad_value = second[:4]
    low_part, parts_a = lax.optimization_barrier((second[10], parts_a))
    low_parts = exchange(low_part.reshape(NZ * NX, 8, HD), ("z", "x"))
    low_parts, parts_b = lax.optimization_barrier((low_parts, parts_b))
    keep, send = factor(place, span_beacon_count, low_parts, state, first[8:10] + second[8:10])
    pieces = (keep.astype(f32) + swap(send).astype(f32)).astype(bf16)
    both = exchange(middle(exchange(pieces, PLANE), parts_a + parts_b), "z")
    cache_gradient, chunk = close(span_beacon_count, both)
    mine = exchange(chunk, PLANE)
    adapter_gradient = unpack(place, mine, swap(mine))
    return (
        attended[None, None],
        grad_query[None, None],
        grad_key[None, None],
        grad_value[None, None],
        cache_gradient.reshape(1, 1, 2, MAX_BEACONS, 2 * KEY_FEATURES),
        adapter_gradient,
    )


def solution(mesh):
    chips = Mesh(mesh.devices.reshape(NZ, NX, NY, NC), ALL_AXES)
    dp, ctx = ("y", "core"), ("z", "x")
    array5 = P(dp, ctx, None, None, None)
    array3 = P(dp, ctx, None)
    return jax.shard_map(
        local,
        mesh=chips,
        in_specs=(array5, array5, array5, array5, array5, P(), P(), array5, array3, array3, array3),
        out_specs=(array5, array5, array5, array5, array5, P()),
        check_vma=False,
    )
```

```python
import jax
import jax.numpy as jnp
from jax import lax
from jax.experimental import pallas as pl
from jax.experimental.pallas import tpu as pltpu
from jax.sharding import Mesh, PartitionSpec as P

MODEL_WIDTH = 4096
KVH = 8
HD = 128
SPAN = 64
MAX_BEACONS = 8
UPDATE_RANK = 64
GROUP = 4
QW = 4096
KEY_FEATURES = 1024
NCH = 64
NZ, NX, NY, NC = 8, 4, 4, 2

bf16 = jnp.bfloat16
f32 = jnp.float32
ALL_AXES = ("z", "x", "y", "core")
PLANE = ("x", "y")

HEADS = 4
HALF_TILES = 3 * HEADS
LOW_TILE = HALF_TILES
STATE_TILES = 6
FAR = 384
NEAR = 128
KEYS = FAR + NEAR
ROWS = GROUP * 2 * SPAN
MASKED = -1e30
SCORE_SCALE = HD ** (-0.5)
LOG2E = 1.4426950408889634


def dot(a, b, dims=((1,), (0,))):
    return lax.dot_general(a, b, (dims, ((), ())), preferred_element_type=f32)


def selection(first, second):
    row = lax.broadcasted_iota(jnp.int32, (16, 16), 0)
    slot = lax.broadcasted_iota(jnp.int32, (16, 16), 1)
    source = jnp.where(row < first, row, row - first + MAX_BEACONS)
    return jnp.where((slot == source) & (row < first + second), 1.0, 0.0)


def project_kernel(counts, docs, state, down_t, up, frozen, out, state_out):
    first, second = counts[0, 0, 0], counts[0, 0, 1]
    low = dot(state[...], down_t[...], ((1,), (1,))).astype(bf16)
    states = (frozen[...].astype(f32) + dot(low, up[...])).astype(bf16)
    pick = selection(first, second).astype(bf16)
    rows = dot(pick, states)
    low_rows = dot(pick, low).astype(bf16)
    sub = lax.broadcasted_iota(jnp.int32, (8, HD), 0)
    halves = []
    for heads in (range(HEADS), range(HEADS, KVH)):
        tiles = [rows[:8, h * HD : (h + 1) * HD] for h in heads]
        tiles += [rows[:8, (KVH + h) * HD : (KVH + h + 1) * HD] for h in heads]
        for h in heads:
            keys = rows[8:, h * HD : (h + 1) * HD]
            values = rows[8:, (KVH + h) * HD : (KVH + h + 1) * HD]
            tiles.append(jnp.where(sub < 4, keys, pltpu.roll(values, 4, 0)))
        halves.append(tiles)
    put_row = lax.broadcasted_iota(jnp.int32, (UPDATE_RANK, HD), 0)
    put_col = lax.broadcasted_iota(jnp.int32, (UPDATE_RANK, HD), 1)
    left = jnp.where(put_row == put_col, 1.0, 0.0).astype(bf16)
    right = jnp.where(put_row + UPDATE_RANK == put_col, 1.0, 0.0).astype(bf16)
    extra = dot(low_rows, left)[:8] + dot(low_rows, right)[8:]
    side = lax.broadcasted_iota(jnp.int32, (8, HD), 1) >= UPDATE_RANK
    for i, fact in enumerate((first, second, docs[0, 0, 0], docs[0, 0, 1])):
        extra = jnp.where(side & (sub == 4 + i), fact.astype(f32), extra)
    halves[0].append(extra)
    state_rows = dot(pick, state[...])
    half = MODEL_WIDTH // HD // 2
    blocks = [state_rows[:, c * HD : (c + 1) * HD] for c in range(2 * half)]
    tiles = [block[:8] for block in blocks]
    for c in range(half):
        a, b = blocks[c][8:], blocks[half + c][8:]
        tiles.append(jnp.where(sub < 4, a, pltpu.roll(b, 4, 0)))
    for t, tile in enumerate(tiles):
        state_out[t // STATE_TILES, t % STATE_TILES] = tile.astype(bf16)
    for t, tile in enumerate(halves[0] + halves[1]):
        packed = tile.astype(bf16)
        for z in range(NZ):
            out[z, t] = packed


VMEM = pl.BlockSpec(memory_space=pltpu.VMEM)
SMEM = pl.BlockSpec(memory_space=pltpu.SMEM)
SMALL = pltpu.CompilerParams(vmem_limit_bytes=8 * 1024 * 1024)


def project(counts, docs, state, down_t, up, frozen):
    return pl.pallas_call(
        project_kernel,
        in_specs=[SMEM] * 2 + [VMEM] * 4,
        out_specs=[VMEM] * 2,
        out_shape=[
            jax.ShapeDtypeStruct((NZ, LOW_TILE + 1 + HALF_TILES, 8, HD), bf16),
            jax.ShapeDtypeStruct((NZ, STATE_TILES, 8, HD), bf16),
        ],
        name="project",
    )(counts, docs, state, down_t, up, frozen)


def fill_bias(place, docs, ends, boxes, bias):
    z_own, x_own = place[0], place[1]
    pair = z_own * NX + x_own
    lane = lax.broadcasted_iota(jnp.int32, (8, NEAR), 1)
    sub = lax.broadcasted_iota(jnp.int32, (8, NEAR), 0)
    side = lane // SPAN
    offset = lane % SPAN
    own_span = jnp.where(side == 0, pair, NCH - 1 - pair).astype(f32)
    own_doc = jnp.where(side == 0, docs[0, 0, 0], docs[0, 0, 1]).astype(f32)
    live = offset < jnp.where(side == 0, ends[0, 0, 0], ends[0, 0, 1])
    for block in range(NEAR // 8):
        key_side = block * 8 // SPAN
        key_offset = sub + (block * 8) % SPAN
        key_live = key_offset < ends[0, 0, key_side]
        seen = (side == key_side) & (key_offset <= offset) & (key_live == live)
        bias[block * 8 : block * 8 + 8, :] = jnp.where(seen, 0.0, MASKED)

    def facts(box, z, slot):
        tile = boxes[box][z, LOW_TILE].astype(f32)
        tile = jnp.where(lane < UPDATE_RANK, pltpu.roll(tile, UPDATE_RANK, 1), tile)
        first, second = tile[4:5], tile[5:6]
        first_doc, second_doc = tile[6:7], tile[7:8]
        source = z * NX + lax.rem(x_own - box + NX, NX)
        low = slot < first
        high = slot < first + second
        span = jnp.where(low, source, NCH - 1 - source).astype(f32)
        doc = jnp.where(low, first_doc, second_doc)
        return jnp.where(high, span, 2.0 * NCH), doc

    def write(at, span, doc):
        seen = live & (span < own_span) & (doc == own_doc)
        bias[at : at + 8, :] = jnp.where(seen, 0.0, MASKED)

    slot = sub.astype(f32)
    for box in range(NX):
        for z in range(NZ):
            write(NEAR + box * 64 + z * 8, *facts(box, z, slot))
        for z in range(0, NZ, 2):
            span_a, doc_a = facts(box, z, slot + 8.0)
            span_b, doc_b = facts(box, z + 1, slot + 4.0)
            write(
                NEAR + 256 + box * 32 + z * 4,
                jnp.where(sub < 4, span_a, span_b),
                jnp.where(sub < 4, doc_a, doc_b),
            )


def gather_low(boxes, low_all):
    rows = [None] * (2 * NX)
    lane = lax.broadcasted_iota(jnp.int32, (NZ, 8, HD), 2)
    sub = lax.broadcasted_iota(jnp.int32, (NZ // 2, 8, HD), 1)
    for b, box in enumerate(boxes):
        tile = box[:, LOW_TILE].astype(f32)
        head = jnp.where(lane < UPDATE_RANK, tile, 0.0)
        rows[b] = head.reshape(64, HD)
        tail = jnp.where(lane < UPDATE_RANK, pltpu.roll(tile, UPDATE_RANK, 2), 0.0)
        tail = tail.reshape(NZ // 2, 2, 8, HD)
        tail = jnp.where(sub < 4, tail[:, 0], pltpu.roll(tail[:, 1], 4, 1))
        rows[NX + b] = tail.reshape(32, HD)
    low_all[...] = jnp.concatenate(rows, axis=0).T[:UPDATE_RANK].astype(bf16)


def attend_kernel(
    place, docs, ends, query, key, value, grad, up_key, up_value, box0, box1, box2, box3,
    bias, low_all, low_before,
    attended, grad_query, grad_key, grad_value, out0, out1, out2, out3, up_key_part,
    up_value_part, low_part, low_total, last,
):
    boxes = (box0, box1, box2, box3)
    outs = (out0, out1, out2, out3)
    g = pl.program_id(0)

    @pl.when(g == 0)
    def _():
        if low_before is None:
            fill_bias(place, docs, ends, boxes, bias)
            gather_low(boxes, low_all)
            low_total[...] = jnp.zeros_like(low_total)
        else:
            low_total[...] = low_before[...]

    sub = lax.broadcasted_iota(jnp.int32, (NZ // 2, 8, HD), 1)

    def stack(ref):
        whole = ref[...].reshape(2 * SPAN, GROUP * HD)
        return jnp.concatenate(
            [whole[:, m * HD : (m + 1) * HD] for m in range(GROUP)], axis=0
        )

    def far_rows(tile):
        return [box[:, tile].astype(f32).reshape(8 * NZ, HD) for box in boxes]

    extra_keys, extra_values = [], []
    for box in boxes:
        both = box[:, 2 * HEADS + g].astype(f32).reshape(NZ // 2, 2, 8, HD)
        even, odd = both[:, 0], both[:, 1]
        extra_keys.append(jnp.where(sub < 4, even, pltpu.roll(odd, 4, 1)).reshape(4 * NZ, HD))
        extra_values.append(jnp.where(sub < 4, pltpu.roll(even, 4, 1), odd).reshape(4 * NZ, HD))
    keys = jnp.concatenate(
        [key[...].reshape(NEAR, HD).astype(f32)] + far_rows(g) + extra_keys, axis=0
    )
    values = jnp.concatenate(
        [value[...].reshape(NEAR, HD).astype(f32)] + far_rows(HEADS + g) + extra_values, axis=0
    )
    keys = keys.astype(bf16)
    values = values.astype(bf16)
    keys_t = keys.T
    values_t = values.T
    queries = stack(query)
    grads = stack(grad)
    grads_t = grads.T

    scores = dot(keys, queries, ((1,), (1,))) * (SCORE_SCALE * LOG2E)
    scores = scores + jnp.tile(bias[...], (1, GROUP))
    top = jnp.max(scores, axis=0, keepdims=True)
    weights = jnp.exp2(scores - top)
    total = jnp.sum(weights, axis=0, keepdims=True)
    exact = weights * (1.0 / total)
    probs = exact.astype(bf16)
    summed_t = dot(values_t, probs)
    rounded_t = summed_t.astype(bf16)
    summed = rounded_t.T
    delta = jnp.sum(grads_t.astype(f32) * rounded_t.astype(f32), axis=0, keepdims=True)
    grad_probs = dot(values, grads_t)
    grad_scores = (exact * (grad_probs - delta)).astype(bf16)
    query_grad = (dot(keys_t, grad_scores) * SCORE_SCALE).astype(bf16).T
    key_grad = dot(grad_scores, queries) * SCORE_SCALE
    value_grad = dot(probs, grads)

    for m in range(GROUP):
        at = slice(m * 2 * SPAN, (m + 1) * 2 * SPAN)
        cols = slice(m * HD, (m + 1) * HD)
        attended[:, :, cols] = summed[at].reshape(2, SPAN, HD)
        grad_query[:, :, cols] = query_grad[at].reshape(2, SPAN, HD)
    grad_key[...] = key_grad[:NEAR].astype(bf16).reshape(2, SPAN, HD)
    grad_value[...] = value_grad[:NEAR].astype(bf16).reshape(2, SPAN, HD)
    for b, out in enumerate(outs):
        at = NEAR + b * 64
        out[:, 0, 0] = key_grad[at : at + 64].reshape(NZ, 8, HD).astype(bf16)
        out[:, 1, 0] = value_grad[at : at + 64].reshape(NZ, 8, HD).astype(bf16)
        at = NEAR + 256 + b * 32
        k = key_grad[at : at + 32].reshape(NZ // 2, 8, HD)
        v = value_grad[at : at + 32].reshape(NZ // 2, 8, HD)
        even = jnp.where(sub < 4, k, pltpu.roll(v, 4, 1)).astype(bf16)
        odd = jnp.where(sub < 4, pltpu.roll(k, 4, 1), v).astype(bf16)
        for i in range(NZ // 2):
            out[2 * i, 2, 0] = even[i]
            out[2 * i + 1, 2, 0] = odd[i]

    far_keys = key_grad[NEAR:].astype(bf16)
    far_values = value_grad[NEAR:].astype(bf16)
    far = jnp.concatenate([far_keys, far_values], axis=1)
    up_part = dot(low_all[...], far)
    up_key_part[...] = up_part[:, :HD]
    up_value_part[...] = up_part[:, HD:]
    up_both = jnp.concatenate([up_key[...], up_value[...]], axis=1)
    low_total[...] += dot(far, jnp.concatenate([up_both, up_both], axis=0), ((1,), (1,)))

    if not last:
        return

    @pl.when(g == HEADS - 1)
    def _():
        lane = lax.broadcasted_iota(jnp.int32, (8, HD), 1)
        for b in range(NX):
            for z in range(NZ):
                at = b * 64 + z * 8
                head = low_total[at : at + 8, :]
                at = 256 + b * 32 + z // 2 * 8
                tail = low_total[at : at + 8, :]
                if z % 2:
                    tail = pltpu.roll(tail, 4, 0)
                low_part[z, b] = jnp.where(lane < UPDATE_RANK, head, tail).astype(bf16)


def first_kernel(*refs):
    (place, docs, ends, query, key, value, grad, up_key, up_value, *boxes) = refs[:13]
    (attended, grad_query, grad_key, grad_value, *rest) = refs[13:]
    outs, (up_k, up_v, low_total, bias, low_all) = rest[:4], rest[4:]
    attend_kernel(
        place, docs, ends, query, key, value, grad, up_key, up_value, *boxes,
        bias, low_all, None,
        attended, grad_query, grad_key, grad_value, *outs, up_k, up_v, None, low_total, False,
    )


def second_kernel(*refs):
    (place, query, key, value, grad, up_key, up_value, *boxes) = refs[:11]
    bias, low_all, low_before = refs[11:14]
    (attended, grad_query, grad_key, grad_value, *rest) = refs[22:]
    outs, (up_k, up_v, low_part, low_total) = rest[:4], rest[4:]
    attend_kernel(
        place, None, None, query, key, value, grad, up_key, up_value, *boxes,
        bias, low_all, low_before,
        attended, grad_query, grad_key, grad_value, *outs, up_k, up_v, low_part, low_total, True,
    )


def attend(half, small, query, key, value, grad, up, boxes, carried=(), filled=()):
    at = half * HEADS
    wide = pl.BlockSpec((2, SPAN, GROUP * HD), lambda g: (0, 0, g + at))
    narrow = pl.BlockSpec((2, SPAN, HD), lambda g: (0, 0, g + at))
    whole = pl.BlockSpec(boxes[0].shape, lambda g: (0, 0, 0, 0))
    part = pl.BlockSpec((NZ, 3, 1, 8, HD), lambda g: (0, half, g, 0, 0))
    up_key = pl.BlockSpec((UPDATE_RANK, HD), lambda g: (0, g + at))
    up_value = pl.BlockSpec((UPDATE_RANK, HD), lambda g: (0, KVH + g + at))
    up_part = pl.BlockSpec((UPDATE_RANK, HD), lambda g: (0, g))
    low_part = pl.BlockSpec((NZ, NX, 8, HD), lambda g: (0, 0, 0, 0))
    wide_shape = jax.ShapeDtypeStruct((2, SPAN, QW), bf16)
    narrow_shape = jax.ShapeDtypeStruct((2, SPAN, KEY_FEATURES), bf16)
    part_shape = jax.ShapeDtypeStruct((NZ, 2 * 3, HEADS, 8, HD), bf16)
    up_shape = jax.ShapeDtypeStruct((UPDATE_RANK, HEADS * HD), f32)
    kept = [
        jax.ShapeDtypeStruct((FAR, HD), f32),
        jax.ShapeDtypeStruct((KEYS, NEAR), f32),
        jax.ShapeDtypeStruct((UPDATE_RANK, FAR), bf16),
    ]
    kept_specs = [pl.BlockSpec(k.shape, lambda g: (0, 0)) for k in kept]
    in_specs = [SMEM] * len(small) + [wide, narrow, narrow, wide, up_key, up_value] + [whole] * NX
    out_specs = [wide, wide, narrow, narrow] + [part] * NX + [up_part] * 2
    out_shape = [wide_shape] * 2 + [narrow_shape] * 2
    out_shape += [part_shape] * NX + [up_shape] * 2
    scratch, aliases = [], {}
    if half == 0:
        out_specs += kept_specs
        out_shape += kept
    else:
        in_specs += kept_specs[1:] + kept_specs[:1] + [pl.BlockSpec(memory_space=pl.ANY)] * 8
        out_specs.append(low_part)
        out_shape.append(jax.ShapeDtypeStruct((NZ, NX, 8, HD), bf16))
        scratch = [pltpu.VMEM((FAR, HD), f32)]
        aliases = {len(in_specs) - 8 + i: i for i in range(8)}
    return pl.pallas_call(
        (first_kernel, second_kernel)[half],
        grid=(HEADS,),
        in_specs=in_specs,
        out_specs=out_specs,
        out_shape=out_shape,
        scratch_shapes=scratch,
        input_output_aliases=aliases,
        compiler_params=pltpu.CompilerParams(vmem_limit_bytes=20 * 1024 * 1024),
        cost_estimate=pl.CostEstimate(
            flops=6 * 10**9, bytes_accessed=4 * 2**20, transcendentals=HEADS * KEYS * ROWS
        ),
        name=("attend_first", "attend_second")[half],
    )(*small, query, key, value, grad, up, up, *boxes, *carried, *filled)


PER_ROW = (MODEL_WIDTH + 2 * KEY_FEATURES) // HD
CHUNK = 12
CHUNKS = NX * NY
HALF = CHUNKS * CHUNK


def factor_kernel(
    place, low_parts, box0, box1, box2, box3, key_a, value_a, key_b, value_b, keep, send
):
    total = jnp.sum(low_parts[...].astype(f32), axis=0)
    sub = lax.broadcasted_iota(jnp.int32, (8, HD), 0)
    half = MODEL_WIDTH // HD // 2
    lows, states = [], []
    for b, box in enumerate((box0, box1, box2, box3)):
        tiles = [
            box[t // STATE_TILES, HALF_TILES + t % STATE_TILES].astype(f32) for t in range(3 * half)
        ]
        lows += [total[b], jnp.where(sub < 4, pltpu.roll(total[b], UPDATE_RANK, 1), 0.0)]
        states.append(jnp.concatenate(tiles[: 2 * half], axis=1))
        tails = tiles[2 * half :]
        states.append(jnp.concatenate(tails + [pltpu.roll(t, 4, 0) for t in tails], axis=1))
    low_grad = jnp.concatenate(lows, axis=0).astype(bf16)
    down_piece = dot(low_grad, jnp.concatenate(states, axis=0).astype(bf16), ((0,), (0,)))
    wide = MODEL_WIDTH // HD
    ups = (key_a, key_b, value_a, value_b)

    def tile(t):
        r, c = divmod(t, PER_ROW)
        rows = slice(r * 8, r * 8 + 8)
        if c < wide:
            return down_piece[rows, c * HD : (c + 1) * HD]
        which, c = divmod(c - wide, HEADS)
        return ups[which][rows, c * HD : (c + 1) * HD]

    lower = place[2] == 0
    for t in range(HALF):
        a, b = tile(t), tile(HALF + t)
        keep[t // CHUNK, t % CHUNK] = jnp.where(lower, a, b).astype(bf16)
        send[t // CHUNK, t % CHUNK] = jnp.where(lower, b, a).astype(bf16)


def factor(place, low_parts, boxes, ups):
    return pl.pallas_call(
        factor_kernel,
        in_specs=[SMEM] + [VMEM] * 9,
        out_specs=[VMEM] * 2,
        out_shape=[jax.ShapeDtypeStruct((CHUNKS, CHUNK, 8, HD), bf16)] * 2,
        compiler_params=SMALL,
        name="factor",
    )(place, low_parts, *boxes, *ups)


def middle_kernel(pieces, *refs):
    out = refs[-1]
    chunk = jnp.sum(pieces[...].astype(f32), axis=0).astype(bf16)
    a, b, c, d = refs[:-1]
    for z in range(NZ):
        out[z, :CHUNK] = chunk
        out[z, CHUNK:] = (
            (a[z].astype(f32) + b[z].astype(f32)) + (c[z].astype(f32) + d[z].astype(f32))
        ).astype(bf16)


def middle(pieces, parts):
    return pl.pallas_call(
        middle_kernel,
        in_specs=[VMEM] * (1 + len(parts)),
        out_specs=VMEM,
        out_shape=jax.ShapeDtypeStruct((NZ, CHUNK + 2 * HALF_TILES, 8, HD), bf16),
        compiler_params=SMALL,
        name="middle",
    )(pieces, *parts)


def close_kernel(counts, parts, cache_out, out):
    pick = selection(counts[0, 0, 0], counts[0, 0, 1]).astype(bf16)
    total = jnp.sum(parts[...].astype(f32), axis=0)
    chunk = total[:CHUNK].astype(bf16)
    for i in range(CHUNKS):
        out[i] = chunk
    sub = lax.broadcasted_iota(jnp.int32, (8, HD), 0)
    top_keys, top_values, rest_keys, rest_values = [], [], [], []
    for h in range(KVH):
        at = CHUNK + h // HEADS * HALF_TILES + h % HEADS
        top_keys.append(total[at])
        top_values.append(total[at + HEADS])
        both = total[at + 2 * HEADS]
        rest_keys.append(jnp.where(sub < 4, both, 0.0))
        rest_values.append(jnp.where(sub < 4, pltpu.roll(both, 4, 0), 0.0))
    compact = jnp.concatenate(
        [
            jnp.concatenate(top_keys + top_values, axis=1),
            jnp.concatenate(rest_keys + rest_values, axis=1),
        ],
        axis=0,
    ).astype(bf16)
    cache_out[...] = dot(pick, compact, ((0,), (0,))).astype(bf16)


def close(counts, parts):
    return pl.pallas_call(
        close_kernel,
        in_specs=[SMEM, VMEM],
        out_specs=[VMEM, VMEM],
        out_shape=[
            jax.ShapeDtypeStruct((16, 2 * KEY_FEATURES), bf16),
            jax.ShapeDtypeStruct((CHUNKS, CHUNK, 8, HD), bf16),
        ],
        compiler_params=SMALL,
        name="close",
    )(counts, parts)


def unpack_kernel(place, mine, other, out):
    lower = place[2] == 0
    for t in range(HALF):
        a = mine[t // CHUNK, t % CHUNK].astype(f32)
        b = other[t // CHUNK, t % CHUNK].astype(f32)
        for at, tile in ((t, jnp.where(lower, a, b)), (t + HALF, jnp.where(lower, b, a))):
            r, c = divmod(at, PER_ROW)
            out[r * 8 : r * 8 + 8, c * HD : (c + 1) * HD] = tile


def unpack(place, mine, other):
    return pl.pallas_call(
        unpack_kernel,
        in_specs=[SMEM] + [VMEM] * 2,
        out_specs=VMEM,
        out_shape=jax.ShapeDtypeStruct((UPDATE_RANK, MODEL_WIDTH + 2 * KEY_FEATURES), f32),
        compiler_params=SMALL,
        name="unpack",
    )(place, mine, other)


def exchange(x, axes):
    return lax.all_to_all(x, axes, 0, 0, tiled=True)


def shift(x, by):
    return lax.ppermute(x, "x", [(i, (i + by) % NX) for i in range(NX)])


def swap(x):
    return lax.ppermute(x, "core", [(0, 1), (1, 0)])


def spread(column):
    return [column, shift(column, 1), shift(column, 2), shift(column, 3)]


def collect(parts):
    parts = [p.reshape(NZ, 2 * HALF_TILES, 8, HD) for p in parts]
    return [parts[0], shift(parts[1], -1), shift(parts[2], -2), shift(parts[3], -3)]


def local(
    query, key, value, beacon_slot_state, frozen_beacon_cache, adapter_down_weight,
    adapter_up_weight, output_cotangent, span_beacon_count, span_document, boundary,
):
    place = jnp.stack([lax.axis_index(axis) for axis in ("z", "x", "core")]).astype(jnp.int32)
    state = beacon_slot_state[0, 0].reshape(2 * MAX_BEACONS, MODEL_WIDTH)
    frozen = frozen_beacon_cache[0, 0].reshape(2 * MAX_BEACONS, 2 * KEY_FEATURES)

    message, state_tiles = project(
        span_beacon_count, span_document, state, adapter_down_weight.T, adapter_up_weight, frozen
    )
    arrays = (query[0, 0], key[0, 0], value[0, 0], output_cotangent[0, 0])
    arrays = [pltpu.with_memory_space_constraint(x, pltpu.HBM) for x in arrays]
    arrays.append(adapter_up_weight)
    column = exchange(message, "z")
    boxes_a = spread(column[:, : LOW_TILE + 1])
    boxes_b = spread(jnp.concatenate([column[:, LOW_TILE + 1 :], state_tiles], axis=1))
    first = attend(0, (place, span_document, boundary), *arrays, boxes_a)
    low_total, bias, low_all = first[10:]
    second = attend(1, (place,), *arrays, boxes_b, (bias, low_all, low_total), first[:8])
    attended, grad_query, grad_key, grad_value = second[:4]
    parts = collect(second[4:8])
    low_parts = exchange(second[10], "z")
    keep, send = factor(place, low_parts, boxes_b, first[8:10] + second[8:10])
    send, parts = lax.optimization_barrier((send, parts))
    pieces = (keep.astype(f32) + swap(send).astype(f32)).astype(bf16)
    both = exchange(middle(exchange(pieces, PLANE), parts), "z")
    cache_gradient, chunk = close(span_beacon_count, both)
    mine = exchange(chunk, PLANE)
    adapter_gradient = unpack(place, mine, swap(mine))
    return (
        attended[None, None],
        grad_query[None, None],
        grad_key[None, None],
        grad_value[None, None],
        cache_gradient.reshape(1, 1, 2, MAX_BEACONS, 2 * KEY_FEATURES),
        adapter_gradient,
    )


def solution(mesh):
    chips = Mesh(mesh.devices.reshape(NZ, NX, NY, NC), ALL_AXES)
    dp, ctx = ("y", "core"), ("z", "x")
    array5 = P(dp, ctx, None, None, None)
    array3 = P(dp, ctx, None)
    return jax.shard_map(
        local,
        mesh=chips,
        in_specs=(array5, array5, array5, array5, array5, P(), P(), array5, array3, array3, array3),
        out_specs=(array5, array5, array5, array5, array5, P()),
        check_vma=False,
    )
```

```python
import jax
import jax.numpy as jnp
from jax import lax
from jax.experimental import pallas as pl
from jax.experimental.pallas import tpu as pltpu
from jax.sharding import Mesh, PartitionSpec as P

MODEL_WIDTH = 4096
KVH = 8
HD = 128
SPAN = 64
MAX_BEACONS = 8
UPDATE_RANK = 64
GROUP = 4
QW = 4096
KEY_FEATURES = 1024
NCH = 64
NZ, NX, NY, NC = 8, 4, 4, 2

bf16 = jnp.bfloat16
f32 = jnp.float32
ALL_AXES = ("z", "x", "y", "core")
PLANE = ("x", "y")

HEADS = 4
STEP = 2
HALF_TILES = 3 * HEADS
LOW_TILE = HALF_TILES
FAR = 384
NEAR = 128
KEYS = FAR + NEAR
ROWS = GROUP * 2 * SPAN
MASKED = -1e30
SCORE_SCALE = HD ** (-0.5)
LOG2E = 1.4426950408889634


def dot(a, b, dims=((1,), (0,))):
    return lax.dot_general(a, b, (dims, ((), ())), preferred_element_type=f32)


def selection(first, second):
    row = lax.broadcasted_iota(jnp.int32, (16, 16), 0)
    slot = lax.broadcasted_iota(jnp.int32, (16, 16), 1)
    source = jnp.where(row < first, row, row - first + MAX_BEACONS)
    return jnp.where((slot == source) & (row < first + second), 1.0, 0.0)


def project_kernel(counts, docs, state, down_t, up, frozen, out):
    first, second = counts[0, 0, 0], counts[0, 0, 1]
    low = dot(state[...], down_t[...], ((1,), (1,))).astype(bf16)
    states = (frozen[...].astype(f32) + dot(low, up[...])).astype(bf16)
    pick = selection(first, second).astype(bf16)
    rows = dot(pick, states)
    low_rows = dot(pick, low).astype(bf16)
    sub = lax.broadcasted_iota(jnp.int32, (8, HD), 0)
    halves = []
    for heads in (range(HEADS), range(HEADS, KVH)):
        tiles = [rows[:8, h * HD : (h + 1) * HD] for h in heads]
        tiles += [rows[:8, (KVH + h) * HD : (KVH + h + 1) * HD] for h in heads]
        for h in heads:
            keys = rows[8:, h * HD : (h + 1) * HD]
            values = rows[8:, (KVH + h) * HD : (KVH + h + 1) * HD]
            tiles.append(jnp.where(sub < 4, keys, pltpu.roll(values, 4, 0)))
        halves.append(tiles)
    put_row = lax.broadcasted_iota(jnp.int32, (UPDATE_RANK, HD), 0)
    put_col = lax.broadcasted_iota(jnp.int32, (UPDATE_RANK, HD), 1)
    left = jnp.where(put_row == put_col, 1.0, 0.0).astype(bf16)
    right = jnp.where(put_row + UPDATE_RANK == put_col, 1.0, 0.0).astype(bf16)
    extra = dot(low_rows, left)[:8] + dot(low_rows, right)[8:]
    side = lax.broadcasted_iota(jnp.int32, (8, HD), 1) >= UPDATE_RANK
    for i, fact in enumerate((first, second, docs[0, 0, 0], docs[0, 0, 1])):
        extra = jnp.where(side & (sub == 4 + i), fact.astype(f32), extra)
    halves[0].append(extra)
    for t, tile in enumerate(halves[0] + halves[1]):
        packed = tile.astype(bf16)
        for z in range(NZ):
            out[z, t] = packed


VMEM = pl.BlockSpec(memory_space=pltpu.VMEM)
SMEM = pl.BlockSpec(memory_space=pltpu.SMEM)
SMALL = pltpu.CompilerParams(vmem_limit_bytes=8 * 1024 * 1024)


def project(counts, docs, state, down_t, up, frozen):
    return pl.pallas_call(
        project_kernel,
        in_specs=[SMEM] * 2 + [VMEM] * 4,
        out_specs=VMEM,
        out_shape=jax.ShapeDtypeStruct((NZ, LOW_TILE + 1 + HALF_TILES, 8, HD), bf16),
        name="project",
    )(counts, docs, state, down_t, up, frozen)


def fill_bias(place, docs, ends, boxes, bias):
    z_own, x_own = place[0], place[1]
    pair = z_own * NX + x_own
    lane = lax.broadcasted_iota(jnp.int32, (8, NEAR), 1)
    sub = lax.broadcasted_iota(jnp.int32, (8, NEAR), 0)
    side = lane // SPAN
    offset = lane % SPAN
    own_span = jnp.where(side == 0, pair, NCH - 1 - pair).astype(f32)
    own_doc = jnp.where(side == 0, docs[0, 0, 0], docs[0, 0, 1]).astype(f32)
    live = offset < jnp.where(side == 0, ends[0, 0, 0], ends[0, 0, 1])
    for block in range(NEAR // 8):
        key_side = block * 8 // SPAN
        key_offset = sub + (block * 8) % SPAN
        key_live = key_offset < ends[0, 0, key_side]
        seen = (side == key_side) & (key_offset <= offset) & (key_live == live)
        bias[block * 8 : block * 8 + 8, :] = jnp.where(seen, 0.0, MASKED)

    def facts(box, z, slot):
        tile = boxes[box][z, LOW_TILE].astype(f32)
        tile = jnp.where(lane < UPDATE_RANK, pltpu.roll(tile, UPDATE_RANK, 1), tile)
        first, second = tile[4:5], tile[5:6]
        first_doc, second_doc = tile[6:7], tile[7:8]
        source = z * NX + lax.rem(x_own - box + NX, NX)
        low = slot < first
        high = slot < first + second
        span = jnp.where(low, source, NCH - 1 - source).astype(f32)
        doc = jnp.where(low, first_doc, second_doc)
        return jnp.where(high, span, 2.0 * NCH), doc

    def write(at, span, doc):
        seen = live & (span < own_span) & (doc == own_doc)
        bias[at : at + 8, :] = jnp.where(seen, 0.0, MASKED)

    slot = sub.astype(f32)
    for box in range(NX):
        for z in range(NZ):
            write(NEAR + box * 64 + z * 8, *facts(box, z, slot))
        for z in range(0, NZ, 2):
            span_a, doc_a = facts(box, z, slot + 8.0)
            span_b, doc_b = facts(box, z + 1, slot + 4.0)
            write(
                NEAR + 256 + box * 32 + z * 4,
                jnp.where(sub < 4, span_a, span_b),
                jnp.where(sub < 4, doc_a, doc_b),
            )


def gather_low(boxes, low_all):
    rows = [None] * (2 * NX)
    lane = lax.broadcasted_iota(jnp.int32, (NZ, 8, HD), 2)
    sub = lax.broadcasted_iota(jnp.int32, (NZ // 2, 8, HD), 1)
    for b, box in enumerate(boxes):
        tile = box[:, LOW_TILE].astype(f32)
        head = jnp.where(lane < UPDATE_RANK, tile, 0.0)
        rows[b] = head.reshape(64, HD)
        tail = jnp.where(lane < UPDATE_RANK, pltpu.roll(tile, UPDATE_RANK, 2), 0.0)
        tail = tail.reshape(NZ // 2, 2, 8, HD)
        tail = jnp.where(sub < 4, tail[:, 0], pltpu.roll(tail[:, 1], 4, 1))
        rows[NX + b] = tail.reshape(32, HD)
    low_all[...] = jnp.concatenate(rows, axis=0).T[:UPDATE_RANK].astype(bf16)


def attend_kernel(
    place, docs, ends, query, key, value, grad, up_key, up_value, box0, box1, box2, box3,
    bias, low_all, low_before,
    attended, grad_query, grad_key, grad_value, out0, out1, out2, out3, up_key_part,
    up_value_part, low_part, low_total, last,
):
    boxes = (box0, box1, box2, box3)
    outs = (out0, out1, out2, out3)
    g = pl.program_id(0)

    @pl.when(g == 0)
    def _():
        if low_before is None:
            fill_bias(place, docs, ends, boxes, bias)
            gather_low(boxes, low_all)
            low_total[...] = jnp.zeros_like(low_total)
        else:
            low_total[...] = low_before[...]

    sub = lax.broadcasted_iota(jnp.int32, (NZ // 2, 8, HD), 1)

    def stack(ref, n):
        whole = ref[:, :, n * GROUP * HD : (n + 1) * GROUP * HD].reshape(2 * SPAN, GROUP * HD)
        return jnp.concatenate(
            [whole[:, m * HD : (m + 1) * HD] for m in range(GROUP)], axis=0
        )

    def far_rows(tile):
        return [box[:, tile].astype(f32).reshape(8 * NZ, HD) for box in boxes]

    def own(ref, n):
        return ref[:, :, n * HD : (n + 1) * HD].reshape(NEAR, HD).astype(f32)

    def load(n):
        h = g * STEP + n
        extra_keys, extra_values = [], []
        for box in boxes:
            both = box[:, 2 * HEADS + h].astype(f32).reshape(NZ // 2, 2, 8, HD)
            even, odd = both[:, 0], both[:, 1]
            extra_keys.append(jnp.where(sub < 4, even, pltpu.roll(odd, 4, 1)).reshape(4 * NZ, HD))
            extra_values.append(
                jnp.where(sub < 4, pltpu.roll(even, 4, 1), odd).reshape(4 * NZ, HD)
            )
        keys = jnp.concatenate([own(key, n)] + far_rows(h) + extra_keys, axis=0)
        values = jnp.concatenate([own(value, n)] + far_rows(HEADS + h) + extra_values, axis=0)
        keys, values = keys.astype(bf16), values.astype(bf16)
        queries, grads = stack(query, n), stack(grad, n)
        return keys, values, queries, grads, grads.T

    def scored(keys, values, queries, grads, grads_t):
        return dot(keys, queries, ((1,), (1,))), dot(values, grads_t)

    def soften(scores):
        scores = scores * (SCORE_SCALE * LOG2E) + jnp.tile(bias[...], (1, GROUP))
        top = jnp.max(scores, axis=0, keepdims=True)
        weights = jnp.exp2(scores - top)
        total = jnp.sum(weights, axis=0, keepdims=True)
        return weights * (1.0 / total)

    def forward(values, exact):
        probs = exact.astype(bf16)
        return probs, dot(values.T, probs).astype(bf16)

    def backward(keys, queries, grads, grads_t, exact, probs, rounded_t, grad_probs):
        delta = jnp.sum(grads_t.astype(f32) * rounded_t.astype(f32), axis=0, keepdims=True)
        grad_scores = (exact * (grad_probs - delta)).astype(bf16)
        query_grad = (dot(keys.T, grad_scores) * SCORE_SCALE).astype(bf16).T
        key_grad = dot(grad_scores, queries) * SCORE_SCALE
        value_grad = dot(probs, grads)
        return rounded_t.T, query_grad, key_grad, value_grad

    def emit(n, summed, query_grad, key_grad, value_grad):
        for m in range(GROUP):
            at = slice(m * 2 * SPAN, (m + 1) * 2 * SPAN)
            cols = slice((n * GROUP + m) * HD, (n * GROUP + m + 1) * HD)
            attended[:, :, cols] = summed[at].reshape(2, SPAN, HD)
            grad_query[:, :, cols] = query_grad[at].reshape(2, SPAN, HD)
        cols = slice(n * HD, (n + 1) * HD)
        grad_key[:, :, cols] = key_grad[:NEAR].astype(bf16).reshape(2, SPAN, HD)
        grad_value[:, :, cols] = value_grad[:NEAR].astype(bf16).reshape(2, SPAN, HD)
        for b, out in enumerate(outs):
            at = NEAR + b * 64
            out[:, 0, n] = key_grad[at : at + 64].reshape(NZ, 8, HD).astype(bf16)
            out[:, 1, n] = value_grad[at : at + 64].reshape(NZ, 8, HD).astype(bf16)
            at = NEAR + 256 + b * 32
            k = key_grad[at : at + 32].reshape(NZ // 2, 8, HD)
            v = value_grad[at : at + 32].reshape(NZ // 2, 8, HD)
            even = jnp.where(sub < 4, k, pltpu.roll(v, 4, 1)).astype(bf16)
            odd = jnp.where(sub < 4, pltpu.roll(k, 4, 1), v).astype(bf16)
            for i in range(NZ // 2):
                out[2 * i, 2, n] = even[i]
                out[2 * i + 1, 2, n] = odd[i]
        far_keys = key_grad[NEAR:].astype(bf16)
        far_values = value_grad[NEAR:].astype(bf16)
        far = jnp.concatenate([far_keys, far_values], axis=1)
        up_part = dot(low_all[...], far)
        up_key_part[:, cols] = up_part[:, :HD]
        up_value_part[:, cols] = up_part[:, HD:]
        up_both = jnp.concatenate([up_key[:, cols], up_value[:, cols]], axis=1)
        low_total[...] += dot(far, jnp.concatenate([up_both, up_both], axis=0), ((1,), (1,)))

    ns = range(STEP)
    loaded = [load(n) for n in ns]
    raw = [scored(*loaded[n]) for n in ns]
    exact, ahead = [], []
    for n in ns:
        exact.append(soften(raw[n][0]))
        ahead.append(forward(loaded[n][1], exact[n]))
    for n in ns:
        keys, values, queries, grads, grads_t = loaded[n]
        emit(n, *backward(keys, queries, grads, grads_t, exact[n], *ahead[n], raw[n][1]))

    if not last:
        return

    @pl.when(g == HEADS // STEP - 1)
    def _():
        lane = lax.broadcasted_iota(jnp.int32, (8, HD), 1)
        for b in range(NX):
            x = lax.rem(place[1] - b + NX, NX)
            for z in range(NZ):
                at = b * 64 + z * 8
                head = low_total[at : at + 8, :]
                at = 256 + b * 32 + z // 2 * 8
                tail = low_total[at : at + 8, :]
                if z % 2:
                    tail = pltpu.roll(tail, 4, 0)
                low_part[z, x] = jnp.where(lane < UPDATE_RANK, head, tail).astype(bf16)


def first_kernel(*refs):
    (place, docs, ends, query, key, value, grad, up_key, up_value, *boxes) = refs[:13]
    (attended, grad_query, grad_key, grad_value, *rest) = refs[13:]
    outs, (up_k, up_v, low_total, bias, low_all) = rest[:4], rest[4:]
    attend_kernel(
        place, docs, ends, query, key, value, grad, up_key, up_value, *boxes,
        bias, low_all, None,
        attended, grad_query, grad_key, grad_value, *outs, up_k, up_v, None, low_total, False,
    )


def second_kernel(*refs):
    (place, query, key, value, grad, up_key, up_value, *boxes) = refs[:11]
    bias, low_all, low_before = refs[11:14]
    (attended, grad_query, grad_key, grad_value, *rest) = refs[22:]
    outs, (up_k, up_v, low_part, low_total) = rest[:4], rest[4:]
    attend_kernel(
        place, None, None, query, key, value, grad, up_key, up_value, *boxes,
        bias, low_all, low_before,
        attended, grad_query, grad_key, grad_value, *outs, up_k, up_v, low_part, low_total, True,
    )


def attend(half, small, query, key, value, grad, up, boxes, carried=(), filled=()):
    at = half * HEADS // STEP
    wide = pl.BlockSpec((2, SPAN, STEP * GROUP * HD), lambda g: (0, 0, g + at))
    narrow = pl.BlockSpec((2, SPAN, STEP * HD), lambda g: (0, 0, g + at))
    whole = pl.BlockSpec(boxes[0].shape, lambda g: (0, 0, 0, 0))
    part = pl.BlockSpec((NZ, 3, STEP, 8, HD), lambda g: (0, half, g, 0, 0))
    up_key = pl.BlockSpec((UPDATE_RANK, STEP * HD), lambda g: (0, g + at))
    up_value = pl.BlockSpec((UPDATE_RANK, STEP * HD), lambda g: (0, KVH // STEP + g + at))
    up_part = pl.BlockSpec((UPDATE_RANK, STEP * HD), lambda g: (0, g))
    low_part = pl.BlockSpec((NZ, NX, 8, HD), lambda g: (0, 0, 0, 0))
    wide_shape = jax.ShapeDtypeStruct((2, SPAN, QW), bf16)
    narrow_shape = jax.ShapeDtypeStruct((2, SPAN, KEY_FEATURES), bf16)
    part_shape = jax.ShapeDtypeStruct((NZ, 2 * 3, HEADS, 8, HD), bf16)
    up_shape = jax.ShapeDtypeStruct((UPDATE_RANK, HEADS * HD), f32)
    kept = [
        jax.ShapeDtypeStruct((FAR, HD), f32),
        jax.ShapeDtypeStruct((KEYS, NEAR), f32),
        jax.ShapeDtypeStruct((UPDATE_RANK, FAR), bf16),
    ]
    kept_specs = [pl.BlockSpec(k.shape, lambda g: (0, 0)) for k in kept]
    in_specs = [SMEM] * len(small) + [wide, narrow, narrow, wide, up_key, up_value] + [whole] * NX
    out_specs = [wide, wide, narrow, narrow] + [part] * NX + [up_part] * 2
    out_shape = [wide_shape] * 2 + [narrow_shape] * 2
    out_shape += [part_shape] * NX + [up_shape] * 2
    scratch, aliases = [], {}
    if half == 0:
        out_specs += kept_specs
        out_shape += kept
    else:
        in_specs += kept_specs[1:] + kept_specs[:1] + [pl.BlockSpec(memory_space=pl.ANY)] * 8
        out_specs.append(low_part)
        out_shape.append(jax.ShapeDtypeStruct((NZ, NX, 8, HD), bf16))
        scratch = [pltpu.VMEM((FAR, HD), f32)]
        aliases = {len(in_specs) - 8 + i: i for i in range(8)}
    return pl.pallas_call(
        (first_kernel, second_kernel)[half],
        grid=(HEADS // STEP,),
        in_specs=in_specs,
        out_specs=out_specs,
        out_shape=out_shape,
        scratch_shapes=scratch,
        input_output_aliases=aliases,
        compiler_params=pltpu.CompilerParams(vmem_limit_bytes=28 * 1024 * 1024),
        cost_estimate=pl.CostEstimate(
            flops=6 * 10**9, bytes_accessed=4 * 2**20, transcendentals=HEADS * KEYS * ROWS
        ),
        name=("attend_first", "attend_second")[half],
    )(*small, query, key, value, grad, up, up, *boxes, *carried, *filled)


PER_ROW = (MODEL_WIDTH + 2 * KEY_FEATURES) // HD
CHUNK = 12
CHUNKS = NX * NY
HALF = CHUNKS * CHUNK


def factor_kernel(place, counts, low_parts, state, key_a, value_a, key_b, value_b, keep, send):
    pick = selection(counts[0, 0, 0], counts[0, 0, 1])
    total = jnp.sum(low_parts[...].astype(f32), axis=0)
    compact = jnp.concatenate([total, pltpu.roll(total, UPDATE_RANK, 1)], axis=0).astype(bf16)
    low_grad = dot(pick.astype(bf16), compact, ((0,), (0,))).astype(bf16)
    down_piece = dot(low_grad, state[...], ((0,), (0,)))
    wide = MODEL_WIDTH // HD
    ups = (key_a, key_b, value_a, value_b)

    def tile(t):
        r, c = divmod(t, PER_ROW)
        rows = slice(r * 8, r * 8 + 8)
        if c < wide:
            return down_piece[rows, c * HD : (c + 1) * HD]
        which, c = divmod(c - wide, HEADS)
        return ups[which][rows, c * HD : (c + 1) * HD]

    lower = place[2] == 0
    for t in range(HALF):
        a, b = tile(t), tile(HALF + t)
        keep[t // CHUNK, t % CHUNK] = jnp.where(lower, a, b).astype(bf16)
        send[t // CHUNK, t % CHUNK] = jnp.where(lower, b, a).astype(bf16)


def factor(place, counts, low_parts, state, ups):
    return pl.pallas_call(
        factor_kernel,
        in_specs=[SMEM] * 2 + [VMEM] * 6,
        out_specs=[VMEM] * 2,
        out_shape=[jax.ShapeDtypeStruct((CHUNKS, CHUNK, 8, HD), bf16)] * 2,
        compiler_params=SMALL,
        name="factor",
    )(place, counts, low_parts, state, *ups)


def middle_kernel(pieces, *refs):
    out = refs[-1]
    chunk = jnp.sum(pieces[...].astype(f32), axis=0).astype(bf16)
    a, b, c, d = refs[:-1]
    for z in range(NZ):
        out[z, :CHUNK] = chunk
        out[z, CHUNK:] = (
            (a[z].astype(f32) + b[z].astype(f32)) + (c[z].astype(f32) + d[z].astype(f32))
        ).astype(bf16)


def middle(pieces, parts):
    return pl.pallas_call(
        middle_kernel,
        in_specs=[VMEM] * (1 + len(parts)),
        out_specs=VMEM,
        out_shape=jax.ShapeDtypeStruct((NZ, CHUNK + 2 * HALF_TILES, 8, HD), bf16),
        compiler_params=SMALL,
        name="middle",
    )(pieces, *parts)


def close_kernel(counts, parts, cache_out, out):
    pick = selection(counts[0, 0, 0], counts[0, 0, 1]).astype(bf16)
    total = jnp.sum(parts[...].astype(f32), axis=0)
    chunk = total[:CHUNK].astype(bf16)
    for i in range(CHUNKS):
        out[i] = chunk
    sub = lax.broadcasted_iota(jnp.int32, (8, HD), 0)
    top_keys, top_values, rest_keys, rest_values = [], [], [], []
    for h in range(KVH):
        at = CHUNK + h // HEADS * HALF_TILES + h % HEADS
        top_keys.append(total[at])
        top_values.append(total[at + HEADS])
        both = total[at + 2 * HEADS]
        rest_keys.append(jnp.where(sub < 4, both, 0.0))
        rest_values.append(jnp.where(sub < 4, pltpu.roll(both, 4, 0), 0.0))
    compact = jnp.concatenate(
        [
            jnp.concatenate(top_keys + top_values, axis=1),
            jnp.concatenate(rest_keys + rest_values, axis=1),
        ],
        axis=0,
    ).astype(bf16)
    cache_out[...] = dot(pick, compact, ((0,), (0,))).astype(bf16)


def close(counts, parts):
    return pl.pallas_call(
        close_kernel,
        in_specs=[SMEM, VMEM],
        out_specs=[VMEM, VMEM],
        out_shape=[
            jax.ShapeDtypeStruct((16, 2 * KEY_FEATURES), bf16),
            jax.ShapeDtypeStruct((CHUNKS, CHUNK, 8, HD), bf16),
        ],
        compiler_params=SMALL,
        name="close",
    )(counts, parts)


def unpack_kernel(place, mine, other, out):
    lower = place[2] == 0
    for t in range(HALF):
        a = mine[t // CHUNK, t % CHUNK].astype(f32)
        b = other[t // CHUNK, t % CHUNK].astype(f32)
        for at, tile in ((t, jnp.where(lower, a, b)), (t + HALF, jnp.where(lower, b, a))):
            r, c = divmod(at, PER_ROW)
            out[r * 8 : r * 8 + 8, c * HD : (c + 1) * HD] = tile


def unpack(place, mine, other):
    return pl.pallas_call(
        unpack_kernel,
        in_specs=[SMEM] + [VMEM] * 2,
        out_specs=VMEM,
        out_shape=jax.ShapeDtypeStruct((UPDATE_RANK, MODEL_WIDTH + 2 * KEY_FEATURES), f32),
        compiler_params=SMALL,
        name="unpack",
    )(place, mine, other)


def exchange(x, axes):
    return lax.all_to_all(x, axes, 0, 0, tiled=True)


def shift(x, by):
    return lax.ppermute(x, "x", [(i, (i + by) % NX) for i in range(NX)])


def swap(x):
    return lax.ppermute(x, "core", [(0, 1), (1, 0)])


def spread(column):
    return [column, shift(column, 1), shift(column, 2), shift(column, 3)]


def collect(parts):
    parts = [p.reshape(NZ, 2 * HALF_TILES, 8, HD) for p in parts]
    return [parts[0], shift(parts[1], -1), shift(parts[2], -2), shift(parts[3], -3)]


def local(
    query, key, value, beacon_slot_state, frozen_beacon_cache, adapter_down_weight,
    adapter_up_weight, output_cotangent, span_beacon_count, span_document, boundary,
):
    place = jnp.stack([lax.axis_index(axis) for axis in ("z", "x", "core")]).astype(jnp.int32)
    state = beacon_slot_state[0, 0].reshape(2 * MAX_BEACONS, MODEL_WIDTH)
    frozen = frozen_beacon_cache[0, 0].reshape(2 * MAX_BEACONS, 2 * KEY_FEATURES)

    message = project(
        span_beacon_count, span_document, state, adapter_down_weight.T, adapter_up_weight, frozen
    )
    arrays = (query[0, 0], key[0, 0], value[0, 0], output_cotangent[0, 0])
    arrays = [pltpu.with_memory_space_constraint(x, pltpu.HBM) for x in arrays]
    arrays.append(adapter_up_weight)
    column = exchange(message, "z")
    boxes_a = spread(column[:, : LOW_TILE + 1])
    boxes_b = spread(column[:, LOW_TILE + 1 :])
    first = attend(0, (place, span_document, boundary), *arrays, boxes_a)
    low_total, bias, low_all = first[10:]
    second = attend(1, (place,), *arrays, boxes_b, (bias, low_all, low_total), first[:8])
    attended, grad_query, grad_key, grad_value = second[:4]
    parts = collect(second[4:8])
    low_parts = exchange(second[10].reshape(NZ * NX, 8, HD), ("z", "x"))
    keep, send = factor(place, span_beacon_count, low_parts, state, first[8:10] + second[8:10])
    send, parts = lax.optimization_barrier((send, parts))
    pieces = (keep.astype(f32) + swap(send).astype(f32)).astype(bf16)
    both = exchange(middle(exchange(pieces, PLANE), parts), "z")
    cache_gradient, chunk = close(span_beacon_count, both)
    mine = exchange(chunk, PLANE)
    adapter_gradient = unpack(place, mine, swap(mine))
    return (
        attended[None, None],
        grad_query[None, None],
        grad_key[None, None],
        grad_value[None, None],
        cache_gradient.reshape(1, 1, 2, MAX_BEACONS, 2 * KEY_FEATURES),
        adapter_gradient,
    )


def solution(mesh):
    chips = Mesh(mesh.devices.reshape(NZ, NX, NY, NC), ALL_AXES)
    dp, ctx = ("y", "core"), ("z", "x")
    array5 = P(dp, ctx, None, None, None)
    array3 = P(dp, ctx, None)
    return jax.shard_map(
        local,
        mesh=chips,
        in_specs=(array5, array5, array5, array5, array5, P(), P(), array5, array3, array3, array3),
        out_specs=(array5, array5, array5, array5, array5, P()),
        check_vma=False,
    )
```

```python
import jax
import jax.numpy as jnp
from jax import lax
from jax.experimental import pallas as pl
from jax.experimental.pallas import tpu as pltpu
from jax.sharding import Mesh, PartitionSpec as P

MODEL_WIDTH = 4096
KVH = 8
HD = 128
SPAN = 64
MAX_BEACONS = 8
UPDATE_RANK = 64
GROUP = 4
QW = 4096
KEY_FEATURES = 1024
NCH = 64
NZ, NX, NY, NC = 8, 4, 4, 2

bf16 = jnp.bfloat16
f32 = jnp.float32
ALL_AXES = ("z", "x", "y", "core")
PLANE = ("x", "y")

HEADS = 4
STEP = 2
HALF_TILES = 3 * HEADS
LOW_TILE = HALF_TILES
FAR = 384
NEAR = 128
KEYS = FAR + NEAR
ROWS = GROUP * 2 * SPAN
MASKED = -1e30
SCORE_SCALE = HD ** (-0.5)
LOG2E = 1.4426950408889634


def dot(a, b, dims=((1,), (0,))):
    return lax.dot_general(a, b, (dims, ((), ())), preferred_element_type=f32)


def selection(first, second):
    row = lax.broadcasted_iota(jnp.int32, (16, 16), 0)
    slot = lax.broadcasted_iota(jnp.int32, (16, 16), 1)
    source = jnp.where(row < first, row, row - first + MAX_BEACONS)
    return jnp.where((slot == source) & (row < first + second), 1.0, 0.0)


def project_kernel(counts, docs, state, down_t, up, frozen, out):
    first, second = counts[0, 0, 0], counts[0, 0, 1]
    low = dot(state[...], down_t[...], ((1,), (1,))).astype(bf16)
    states = (frozen[...].astype(f32) + dot(low, up[...])).astype(bf16)
    pick = selection(first, second).astype(bf16)
    rows = dot(pick, states)
    low_rows = dot(pick, low).astype(bf16)
    sub = lax.broadcasted_iota(jnp.int32, (8, HD), 0)
    halves = []
    for heads in (range(HEADS), range(HEADS, KVH)):
        tiles = [rows[:8, h * HD : (h + 1) * HD] for h in heads]
        tiles += [rows[:8, (KVH + h) * HD : (KVH + h + 1) * HD] for h in heads]
        for h in heads:
            keys = rows[8:, h * HD : (h + 1) * HD]
            values = rows[8:, (KVH + h) * HD : (KVH + h + 1) * HD]
            tiles.append(jnp.where(sub < 4, keys, pltpu.roll(values, 4, 0)))
        halves.append(tiles)
    put_row = lax.broadcasted_iota(jnp.int32, (UPDATE_RANK, HD), 0)
    put_col = lax.broadcasted_iota(jnp.int32, (UPDATE_RANK, HD), 1)
    left = jnp.where(put_row == put_col, 1.0, 0.0).astype(bf16)
    right = jnp.where(put_row + UPDATE_RANK == put_col, 1.0, 0.0).astype(bf16)
    extra = dot(low_rows, left)[:8] + dot(low_rows, right)[8:]
    side = lax.broadcasted_iota(jnp.int32, (8, HD), 1) >= UPDATE_RANK
    for i, fact in enumerate((first, second, docs[0, 0, 0], docs[0, 0, 1])):
        extra = jnp.where(side & (sub == 4 + i), fact.astype(f32), extra)
    halves[0].append(extra)
    for t, tile in enumerate(halves[0] + halves[1]):
        packed = tile.astype(bf16)
        for z in range(NZ):
            out[z, t] = packed


VMEM = pl.BlockSpec(memory_space=pltpu.VMEM)
SMEM = pl.BlockSpec(memory_space=pltpu.SMEM)
SMALL = pltpu.CompilerParams(vmem_limit_bytes=8 * 1024 * 1024)


def project(counts, docs, state, down_t, up, frozen):
    return pl.pallas_call(
        project_kernel,
        in_specs=[SMEM] * 2 + [VMEM] * 4,
        out_specs=VMEM,
        out_shape=jax.ShapeDtypeStruct((NZ, LOW_TILE + 1 + HALF_TILES, 8, HD), bf16),
        name="project",
    )(counts, docs, state, down_t, up, frozen)


def fill_bias(place, docs, ends, boxes, bias):
    z_own, x_own = place[0], place[1]
    pair = z_own * NX + x_own
    lane = lax.broadcasted_iota(jnp.int32, (8, NEAR), 1)
    sub = lax.broadcasted_iota(jnp.int32, (8, NEAR), 0)
    side = lane // SPAN
    offset = lane % SPAN
    own_span = jnp.where(side == 0, pair, NCH - 1 - pair).astype(f32)
    own_doc = jnp.where(side == 0, docs[0, 0, 0], docs[0, 0, 1]).astype(f32)
    live = offset < jnp.where(side == 0, ends[0, 0, 0], ends[0, 0, 1])
    for block in range(NEAR // 8):
        key_side = block * 8 // SPAN
        key_offset = sub + (block * 8) % SPAN
        key_live = key_offset < ends[0, 0, key_side]
        seen = (side == key_side) & (key_offset <= offset) & (key_live == live)
        bias[block * 8 : block * 8 + 8, :] = jnp.where(seen, 0.0, MASKED)

    def facts(box, z, slot):
        tile = boxes[box][z, LOW_TILE].astype(f32)
        tile = jnp.where(lane < UPDATE_RANK, pltpu.roll(tile, UPDATE_RANK, 1), tile)
        first, second = tile[4:5], tile[5:6]
        first_doc, second_doc = tile[6:7], tile[7:8]
        source = z * NX + lax.rem(x_own - box + NX, NX)
        low = slot < first
        high = slot < first + second
        span = jnp.where(low, source, NCH - 1 - source).astype(f32)
        doc = jnp.where(low, first_doc, second_doc)
        return jnp.where(high, span, 2.0 * NCH), doc

    def write(at, span, doc):
        seen = live & (span < own_span) & (doc == own_doc)
        bias[at : at + 8, :] = jnp.where(seen, 0.0, MASKED)

    slot = sub.astype(f32)
    for box in range(NX):
        for z in range(NZ):
            write(NEAR + box * 64 + z * 8, *facts(box, z, slot))
        for z in range(0, NZ, 2):
            span_a, doc_a = facts(box, z, slot + 8.0)
            span_b, doc_b = facts(box, z + 1, slot + 4.0)
            write(
                NEAR + 256 + box * 32 + z * 4,
                jnp.where(sub < 4, span_a, span_b),
                jnp.where(sub < 4, doc_a, doc_b),
            )


def gather_low(boxes, low_all):
    rows = [None] * (2 * NX)
    lane = lax.broadcasted_iota(jnp.int32, (NZ, 8, HD), 2)
    sub = lax.broadcasted_iota(jnp.int32, (NZ // 2, 8, HD), 1)
    for b, box in enumerate(boxes):
        tile = box[:, LOW_TILE].astype(f32)
        head = jnp.where(lane < UPDATE_RANK, tile, 0.0)
        rows[b] = head.reshape(64, HD)
        tail = jnp.where(lane < UPDATE_RANK, pltpu.roll(tile, UPDATE_RANK, 2), 0.0)
        tail = tail.reshape(NZ // 2, 2, 8, HD)
        tail = jnp.where(sub < 4, tail[:, 0], pltpu.roll(tail[:, 1], 4, 1))
        rows[NX + b] = tail.reshape(32, HD)
    low_all[...] = jnp.concatenate(rows, axis=0).T[:UPDATE_RANK].astype(bf16)


def attend_kernel(
    place, docs, ends, query, key, value, grad, up_key, up_value, box0, box1, box2, box3,
    bias, low_all, low_before,
    attended, grad_query, grad_key, grad_value, out0, out1, out2, out3, up_key_part,
    up_value_part, low_part, low_total, last,
):
    boxes = (box0, box1, box2, box3)
    outs = (out0, out1, out2, out3)
    g = pl.program_id(0)

    @pl.when(g == 0)
    def _():
        if low_before is None:
            fill_bias(place, docs, ends, boxes, bias)
            gather_low(boxes, low_all)
            low_total[...] = jnp.zeros_like(low_total)
        else:
            low_total[...] = low_before[...]

    sub = lax.broadcasted_iota(jnp.int32, (NZ // 2, 8, HD), 1)

    def stack(ref, n):
        whole = ref[:, :, n * GROUP * HD : (n + 1) * GROUP * HD].reshape(2 * SPAN, GROUP * HD)
        return jnp.concatenate(
            [whole[:, m * HD : (m + 1) * HD] for m in range(GROUP)], axis=0
        )

    def far_rows(tile):
        return [box[:, tile].astype(f32).reshape(8 * NZ, HD) for box in boxes]

    def own(ref, n):
        return ref[:, :, n * HD : (n + 1) * HD].reshape(NEAR, HD).astype(f32)

    def load(n):
        h = g * STEP + n
        extra_keys, extra_values = [], []
        for box in boxes:
            both = box[:, 2 * HEADS + h].astype(f32).reshape(NZ // 2, 2, 8, HD)
            even, odd = both[:, 0], both[:, 1]
            extra_keys.append(jnp.where(sub < 4, even, pltpu.roll(odd, 4, 1)).reshape(4 * NZ, HD))
            extra_values.append(
                jnp.where(sub < 4, pltpu.roll(even, 4, 1), odd).reshape(4 * NZ, HD)
            )
        keys = jnp.concatenate([own(key, n)] + far_rows(h) + extra_keys, axis=0)
        values = jnp.concatenate([own(value, n)] + far_rows(HEADS + h) + extra_values, axis=0)
        keys, values = keys.astype(bf16), values.astype(bf16)
        queries, grads = stack(query, n), stack(grad, n)
        return keys, values, queries, grads, grads.T

    def scored(keys, values, queries, grads, grads_t):
        return dot(keys, queries, ((1,), (1,))), dot(values, grads_t)

    def soften(scores):
        scores = scores * (SCORE_SCALE * LOG2E) + jnp.tile(bias[...], (1, GROUP))
        top = jnp.max(scores, axis=0, keepdims=True)
        weights = jnp.exp2(scores - top)
        total = jnp.sum(weights, axis=0, keepdims=True)
        return weights * (1.0 / total)

    def forward(values, exact):
        probs = exact.astype(bf16)
        return probs, dot(values.T, probs).astype(bf16)

    def backward(keys, queries, grads, grads_t, exact, probs, rounded_t, grad_probs):
        delta = jnp.sum(grads_t.astype(f32) * rounded_t.astype(f32), axis=0, keepdims=True)
        grad_scores = (exact * (grad_probs - delta)).astype(bf16)
        query_grad = (dot(keys.T, grad_scores) * SCORE_SCALE).astype(bf16).T
        key_grad = dot(grad_scores, queries) * SCORE_SCALE
        value_grad = dot(probs, grads)
        return rounded_t.T, query_grad, key_grad, value_grad

    def emit(n, summed, query_grad, key_grad, value_grad):
        for m in range(GROUP):
            at = slice(m * 2 * SPAN, (m + 1) * 2 * SPAN)
            cols = slice((n * GROUP + m) * HD, (n * GROUP + m + 1) * HD)
            attended[:, :, cols] = summed[at].reshape(2, SPAN, HD)
            grad_query[:, :, cols] = query_grad[at].reshape(2, SPAN, HD)
        cols = slice(n * HD, (n + 1) * HD)
        grad_key[:, :, cols] = key_grad[:NEAR].astype(bf16).reshape(2, SPAN, HD)
        grad_value[:, :, cols] = value_grad[:NEAR].astype(bf16).reshape(2, SPAN, HD)
        for b, out in enumerate(outs):
            at = NEAR + b * 64
            out[:, 0, n] = key_grad[at : at + 64].reshape(NZ, 8, HD).astype(bf16)
            out[:, 1, n] = value_grad[at : at + 64].reshape(NZ, 8, HD).astype(bf16)
            at = NEAR + 256 + b * 32
            k = key_grad[at : at + 32].reshape(NZ // 2, 8, HD)
            v = value_grad[at : at + 32].reshape(NZ // 2, 8, HD)
            even = jnp.where(sub < 4, k, pltpu.roll(v, 4, 1)).astype(bf16)
            odd = jnp.where(sub < 4, pltpu.roll(k, 4, 1), v).astype(bf16)
            for i in range(NZ // 2):
                out[2 * i, 2, n] = even[i]
                out[2 * i + 1, 2, n] = odd[i]
        far_keys = key_grad[NEAR:].astype(bf16)
        far_values = value_grad[NEAR:].astype(bf16)
        far = jnp.concatenate([far_keys, far_values], axis=1)
        up_part = dot(low_all[...], far)
        up_key_part[:, cols] = up_part[:, :HD]
        up_value_part[:, cols] = up_part[:, HD:]
        up_both = jnp.concatenate([up_key[:, cols], up_value[:, cols]], axis=1)
        low_total[...] += dot(far, jnp.concatenate([up_both, up_both], axis=0), ((1,), (1,)))

    ns = range(STEP)
    loaded = [load(n) for n in ns]
    raw = [scored(*loaded[n]) for n in ns]
    exact, ahead = [], []
    for n in ns:
        exact.append(soften(raw[n][0]))
        ahead.append(forward(loaded[n][1], exact[n]))
    for n in ns:
        keys, values, queries, grads, grads_t = loaded[n]
        emit(n, *backward(keys, queries, grads, grads_t, exact[n], *ahead[n], raw[n][1]))

    if not last:
        return

    @pl.when(g == HEADS // STEP - 1)
    def _():
        lane = lax.broadcasted_iota(jnp.int32, (8, HD), 1)
        for b in range(NX):
            x = lax.rem(place[1] - b + NX, NX)
            for z in range(NZ):
                at = b * 64 + z * 8
                head = low_total[at : at + 8, :]
                at = 256 + b * 32 + z // 2 * 8
                tail = low_total[at : at + 8, :]
                if z % 2:
                    tail = pltpu.roll(tail, 4, 0)
                low_part[z, x] = jnp.where(lane < UPDATE_RANK, head, tail).astype(bf16)


def first_kernel(*refs):
    (place, docs, ends, query, key, value, grad, up_key, up_value, *boxes) = refs[:13]
    (attended, grad_query, grad_key, grad_value, *rest) = refs[13:]
    outs, (up_k, up_v, low_total, bias, low_all) = rest[:4], rest[4:]
    attend_kernel(
        place, docs, ends, query, key, value, grad, up_key, up_value, *boxes,
        bias, low_all, None,
        attended, grad_query, grad_key, grad_value, *outs, up_k, up_v, None, low_total, False,
    )


def second_kernel(*refs):
    (place, query, key, value, grad, up_key, up_value, *boxes) = refs[:11]
    bias, low_all, low_before = refs[11:14]
    (attended, grad_query, grad_key, grad_value, *rest) = refs[22:]
    outs, (up_k, up_v, low_part, low_total) = rest[:4], rest[4:]
    attend_kernel(
        place, None, None, query, key, value, grad, up_key, up_value, *boxes,
        bias, low_all, low_before,
        attended, grad_query, grad_key, grad_value, *outs, up_k, up_v, low_part, low_total, True,
    )


def attend(half, small, query, key, value, grad, up, boxes, carried=(), filled=()):
    at = half * HEADS // STEP
    wide = pl.BlockSpec((2, SPAN, STEP * GROUP * HD), lambda g: (0, 0, g + at))
    narrow = pl.BlockSpec((2, SPAN, STEP * HD), lambda g: (0, 0, g + at))
    whole = pl.BlockSpec(boxes[0].shape, lambda g: (0, 0, 0, 0))
    part = pl.BlockSpec((NZ, 3, STEP, 8, HD), lambda g: (0, half, g, 0, 0))
    up_key = pl.BlockSpec((UPDATE_RANK, STEP * HD), lambda g: (0, g + at))
    up_value = pl.BlockSpec((UPDATE_RANK, STEP * HD), lambda g: (0, KVH // STEP + g + at))
    up_part = pl.BlockSpec((UPDATE_RANK, STEP * HD), lambda g: (0, g))
    low_part = pl.BlockSpec((NZ, NX, 8, HD), lambda g: (0, 0, 0, 0))
    wide_shape = jax.ShapeDtypeStruct((2, SPAN, QW), bf16)
    narrow_shape = jax.ShapeDtypeStruct((2, SPAN, KEY_FEATURES), bf16)
    part_shape = jax.ShapeDtypeStruct((NZ, 2 * 3, HEADS, 8, HD), bf16)
    up_shape = jax.ShapeDtypeStruct((UPDATE_RANK, HEADS * HD), f32)
    kept = [
        jax.ShapeDtypeStruct((FAR, HD), f32),
        jax.ShapeDtypeStruct((KEYS, NEAR), f32),
        jax.ShapeDtypeStruct((UPDATE_RANK, FAR), bf16),
    ]
    kept_specs = [pl.BlockSpec(k.shape, lambda g: (0, 0)) for k in kept]
    in_specs = [SMEM] * len(small) + [wide, narrow, narrow, wide, up_key, up_value] + [whole] * NX
    out_specs = [wide, wide, narrow, narrow] + [part] * NX + [up_part] * 2
    out_shape = [wide_shape] * 2 + [narrow_shape] * 2
    out_shape += [part_shape] * NX + [up_shape] * 2
    scratch, aliases = [], {}
    if half == 0:
        out_specs += kept_specs
        out_shape += kept
    else:
        in_specs += kept_specs[1:] + kept_specs[:1] + [pl.BlockSpec(memory_space=pl.ANY)] * 8
        out_specs.append(low_part)
        out_shape.append(jax.ShapeDtypeStruct((NZ, NX, 8, HD), bf16))
        scratch = [pltpu.VMEM((FAR, HD), f32)]
        aliases = {len(in_specs) - 8 + i: i for i in range(8)}
    return pl.pallas_call(
        (first_kernel, second_kernel)[half],
        grid=(HEADS // STEP,),
        in_specs=in_specs,
        out_specs=out_specs,
        out_shape=out_shape,
        scratch_shapes=scratch,
        input_output_aliases=aliases,
        compiler_params=pltpu.CompilerParams(vmem_limit_bytes=28 * 1024 * 1024),
        cost_estimate=pl.CostEstimate(
            flops=6 * 10**9, bytes_accessed=4 * 2**20, transcendentals=HEADS * KEYS * ROWS
        ),
        name=("attend_first", "attend_second")[half],
    )(*small, query, key, value, grad, up, up, *boxes, *carried, *filled)


PER_ROW = (MODEL_WIDTH + 2 * KEY_FEATURES) // HD
CHUNK = 12
CHUNKS = NX * NY
HALF = CHUNKS * CHUNK


def factor_kernel(place, counts, low_parts, state, key_a, value_a, key_b, value_b, keep, send):
    pick = selection(counts[0, 0, 0], counts[0, 0, 1])
    total = jnp.sum(low_parts[...].astype(f32), axis=0)
    compact = jnp.concatenate([total, pltpu.roll(total, UPDATE_RANK, 1)], axis=0).astype(bf16)
    low_grad = dot(pick.astype(bf16), compact, ((0,), (0,))).astype(bf16)
    down_piece = dot(low_grad, state[...], ((0,), (0,)))
    wide = MODEL_WIDTH // HD
    ups = (key_a, key_b, value_a, value_b)

    def tile(t):
        r, c = divmod(t, PER_ROW)
        rows = slice(r * 8, r * 8 + 8)
        if c < wide:
            return down_piece[rows, c * HD : (c + 1) * HD]
        which, c = divmod(c - wide, HEADS)
        return ups[which][rows, c * HD : (c + 1) * HD]

    lower = place[2] == 0
    for t in range(HALF):
        a, b = tile(t), tile(HALF + t)
        keep[t // CHUNK, t % CHUNK] = jnp.where(lower, a, b).astype(bf16)
        send[t // CHUNK, t % CHUNK] = jnp.where(lower, b, a).astype(bf16)


def factor(place, counts, low_parts, state, ups):
    return pl.pallas_call(
        factor_kernel,
        in_specs=[SMEM] * 2 + [VMEM] * 6,
        out_specs=[VMEM] * 2,
        out_shape=[jax.ShapeDtypeStruct((CHUNKS, CHUNK, 8, HD), bf16)] * 2,
        compiler_params=SMALL,
        name="factor",
    )(place, counts, low_parts, state, *ups)


def middle_kernel(pieces, *refs):
    out = refs[-1]
    chunk = jnp.sum(pieces[...].astype(f32), axis=0).astype(bf16)
    a, b, c, d = refs[:-1]
    for z in range(NZ):
        out[z, :CHUNK] = chunk
        out[z, CHUNK:] = (
            (a[z].astype(f32) + b[z].astype(f32)) + (c[z].astype(f32) + d[z].astype(f32))
        ).astype(bf16)


def middle(pieces, parts):
    return pl.pallas_call(
        middle_kernel,
        in_specs=[VMEM] * (1 + len(parts)),
        out_specs=VMEM,
        out_shape=jax.ShapeDtypeStruct((NZ, CHUNK + 2 * HALF_TILES, 8, HD), bf16),
        compiler_params=SMALL,
        name="middle",
    )(pieces, *parts)


def spread_kernel(parts, out):
    chunk = jnp.sum(parts[:, :CHUNK].astype(f32), axis=0).astype(bf16)
    for i in range(CHUNKS):
        out[i] = chunk


def spread_chunk(parts):
    return pl.pallas_call(
        spread_kernel,
        in_specs=[VMEM],
        out_specs=VMEM,
        out_shape=jax.ShapeDtypeStruct((CHUNKS, CHUNK, 8, HD), bf16),
        compiler_params=SMALL,
        name="spread_chunk",
    )(parts)


def cache_kernel(counts, parts, cache_out):
    pick = selection(counts[0, 0, 0], counts[0, 0, 1]).astype(bf16)
    total = jnp.sum(parts[:, CHUNK:].astype(f32), axis=0)
    sub = lax.broadcasted_iota(jnp.int32, (8, HD), 0)
    top_keys, top_values, rest_keys, rest_values = [], [], [], []
    for h in range(KVH):
        at = h // HEADS * HALF_TILES + h % HEADS
        top_keys.append(total[at])
        top_values.append(total[at + HEADS])
        both = total[at + 2 * HEADS]
        rest_keys.append(jnp.where(sub < 4, both, 0.0))
        rest_values.append(jnp.where(sub < 4, pltpu.roll(both, 4, 0), 0.0))
    compact = jnp.concatenate(
        [
            jnp.concatenate(top_keys + top_values, axis=1),
            jnp.concatenate(rest_keys + rest_values, axis=1),
        ],
        axis=0,
    ).astype(bf16)
    cache_out[...] = dot(pick, compact, ((0,), (0,))).astype(bf16)


def cache(counts, parts):
    return pl.pallas_call(
        cache_kernel,
        in_specs=[SMEM, VMEM],
        out_specs=VMEM,
        out_shape=jax.ShapeDtypeStruct((16, 2 * KEY_FEATURES), bf16),
        compiler_params=SMALL,
        name="cache",
    )(counts, parts)


def unpack_kernel(place, mine, other, out):
    lower = place[2] == 0
    for t in range(HALF):
        a = mine[t // CHUNK, t % CHUNK].astype(f32)
        b = other[t // CHUNK, t % CHUNK].astype(f32)
        for at, tile in ((t, jnp.where(lower, a, b)), (t + HALF, jnp.where(lower, b, a))):
            r, c = divmod(at, PER_ROW)
            out[r * 8 : r * 8 + 8, c * HD : (c + 1) * HD] = tile


def unpack(place, mine, other):
    return pl.pallas_call(
        unpack_kernel,
        in_specs=[SMEM] + [VMEM] * 2,
        out_specs=VMEM,
        out_shape=jax.ShapeDtypeStruct((UPDATE_RANK, MODEL_WIDTH + 2 * KEY_FEATURES), f32),
        compiler_params=SMALL,
        name="unpack",
    )(place, mine, other)


def exchange(x, axes):
    return lax.all_to_all(x, axes, 0, 0, tiled=True)


def shift(x, by):
    return lax.ppermute(x, "x", [(i, (i + by) % NX) for i in range(NX)])


def swap(x):
    return lax.ppermute(x, "core", [(0, 1), (1, 0)])


def spread(column):
    return [column, shift(column, 1), shift(column, 2), shift(column, 3)]


def collect(parts):
    parts = [p.reshape(NZ, 2 * HALF_TILES, 8, HD) for p in parts]
    return [parts[0], shift(parts[1], -1), shift(parts[2], -2), shift(parts[3], -3)]


def local(
    query, key, value, beacon_slot_state, frozen_beacon_cache, adapter_down_weight,
    adapter_up_weight, output_cotangent, span_beacon_count, span_document, boundary,
):
    place = jnp.stack([lax.axis_index(axis) for axis in ("z", "x", "core")]).astype(jnp.int32)
    state = beacon_slot_state[0, 0].reshape(2 * MAX_BEACONS, MODEL_WIDTH)
    frozen = frozen_beacon_cache[0, 0].reshape(2 * MAX_BEACONS, 2 * KEY_FEATURES)

    message = project(
        span_beacon_count, span_document, state, adapter_down_weight.T, adapter_up_weight, frozen
    )
    arrays = (query[0, 0], key[0, 0], value[0, 0], output_cotangent[0, 0])
    arrays = [pltpu.with_memory_space_constraint(x, pltpu.HBM) for x in arrays]
    arrays.append(adapter_up_weight)
    column = exchange(message, "z")
    boxes_a = spread(column[:, : LOW_TILE + 1])
    boxes_b = spread(column[:, LOW_TILE + 1 :])
    first = attend(0, (place, span_document, boundary), *arrays, boxes_a)
    low_total, bias, low_all = first[10:]
    second = attend(1, (place,), *arrays, boxes_b, (bias, low_all, low_total), first[:8])
    attended, grad_query, grad_key, grad_value = second[:4]
    parts = collect(second[4:8])
    low_parts = exchange(second[10].reshape(NZ * NX, 8, HD), ("z", "x"))
    keep, send = factor(place, span_beacon_count, low_parts, state, first[8:10] + second[8:10])
    send, parts = lax.optimization_barrier((send, parts))
    pieces = (keep.astype(f32) + swap(send).astype(f32)).astype(bf16)
    both = exchange(middle(exchange(pieces, PLANE), parts), "z")
    mine = exchange(spread_chunk(both), PLANE)
    cache_gradient = cache(span_beacon_count, both)
    adapter_gradient = unpack(place, mine, swap(mine))
    return (
        attended[None, None],
        grad_query[None, None],
        grad_key[None, None],
        grad_value[None, None],
        cache_gradient.reshape(1, 1, 2, MAX_BEACONS, 2 * KEY_FEATURES),
        adapter_gradient,
    )


def solution(mesh):
    chips = Mesh(mesh.devices.reshape(NZ, NX, NY, NC), ALL_AXES)
    dp, ctx = ("y", "core"), ("z", "x")
    array5 = P(dp, ctx, None, None, None)
    array3 = P(dp, ctx, None)
    return jax.shard_map(
        local,
        mesh=chips,
        in_specs=(array5, array5, array5, array5, array5, P(), P(), array5, array3, array3, array3),
        out_specs=(array5, array5, array5, array5, array5, P()),
        check_vma=False,
    )
```

```python
import jax
import jax.numpy as jnp
from jax import lax
from jax.experimental import pallas as pl
from jax.experimental.pallas import tpu as pltpu
from jax.sharding import Mesh, PartitionSpec as P

MODEL_WIDTH = 4096
KVH = 8
HD = 128
SPAN = 64
MAX_BEACONS = 8
UPDATE_RANK = 64
GROUP = 4
QW = 4096
KEY_FEATURES = 1024
NCH = 64
NZ, NX, NY, NC = 8, 4, 4, 2

bf16 = jnp.bfloat16
f32 = jnp.float32
ALL_AXES = ("z", "x", "y", "core")
PLANE = ("x", "y")

HEADS = 4
STEP = 2
HALF_TILES = 3 * HEADS
LOW_TILE = HALF_TILES
FAR = 384
NEAR = 128
KEYS = FAR + NEAR
ROWS = GROUP * 2 * SPAN
MASKED = -1e30
SCORE_SCALE = HD ** (-0.5)
LOG2E = 1.4426950408889634


def dot(a, b, dims=((1,), (0,))):
    return lax.dot_general(a, b, (dims, ((), ())), preferred_element_type=f32)


def selection(first, second):
    row = lax.broadcasted_iota(jnp.int32, (16, 16), 0)
    slot = lax.broadcasted_iota(jnp.int32, (16, 16), 1)
    source = jnp.where(row < first, row, row - first + MAX_BEACONS)
    return jnp.where((slot == source) & (row < first + second), 1.0, 0.0)


def project_kernel(counts, docs, state, down_t, up, frozen, out):
    first, second = counts[0, 0, 0], counts[0, 0, 1]
    low = dot(state[...], down_t[...], ((1,), (1,))).astype(bf16)
    states = (frozen[...].astype(f32) + dot(low, up[...])).astype(bf16)
    pick = selection(first, second).astype(bf16)
    rows = dot(pick, states)
    low_rows = dot(pick, low).astype(bf16)
    sub = lax.broadcasted_iota(jnp.int32, (8, HD), 0)
    halves = []
    for heads in (range(HEADS), range(HEADS, KVH)):
        tiles = [rows[:8, h * HD : (h + 1) * HD] for h in heads]
        tiles += [rows[:8, (KVH + h) * HD : (KVH + h + 1) * HD] for h in heads]
        for h in heads:
            keys = rows[8:, h * HD : (h + 1) * HD]
            values = rows[8:, (KVH + h) * HD : (KVH + h + 1) * HD]
            tiles.append(jnp.where(sub < 4, keys, pltpu.roll(values, 4, 0)))
        halves.append(tiles)
    put_row = lax.broadcasted_iota(jnp.int32, (UPDATE_RANK, HD), 0)
    put_col = lax.broadcasted_iota(jnp.int32, (UPDATE_RANK, HD), 1)
    left = jnp.where(put_row == put_col, 1.0, 0.0).astype(bf16)
    right = jnp.where(put_row + UPDATE_RANK == put_col, 1.0, 0.0).astype(bf16)
    extra = dot(low_rows, left)[:8] + dot(low_rows, right)[8:]
    side = lax.broadcasted_iota(jnp.int32, (8, HD), 1) >= UPDATE_RANK
    for i, fact in enumerate((first, second, docs[0, 0, 0], docs[0, 0, 1])):
        extra = jnp.where(side & (sub == 4 + i), fact.astype(f32), extra)
    halves[0].append(extra)
    for t, tile in enumerate(halves[0] + halves[1]):
        packed = tile.astype(bf16)
        for z in range(NZ):
            out[z, t] = packed


VMEM = pl.BlockSpec(memory_space=pltpu.VMEM)
SMEM = pl.BlockSpec(memory_space=pltpu.SMEM)
SMALL = pltpu.CompilerParams(vmem_limit_bytes=8 * 1024 * 1024)


def project(counts, docs, state, down_t, up, frozen):
    return pl.pallas_call(
        project_kernel,
        in_specs=[SMEM] * 2 + [VMEM] * 4,
        out_specs=VMEM,
        out_shape=jax.ShapeDtypeStruct((NZ, LOW_TILE + 1 + HALF_TILES, 8, HD), bf16),
        name="project",
    )(counts, docs, state, down_t, up, frozen)


def fill_bias(place, docs, ends, boxes, bias):
    z_own, x_own = place[0], place[1]
    pair = z_own * NX + x_own
    lane = lax.broadcasted_iota(jnp.int32, (8, NEAR), 1)
    sub = lax.broadcasted_iota(jnp.int32, (8, NEAR), 0)
    side = lane // SPAN
    offset = lane % SPAN
    own_span = jnp.where(side == 0, pair, NCH - 1 - pair).astype(f32)
    own_doc = jnp.where(side == 0, docs[0, 0, 0], docs[0, 0, 1]).astype(f32)
    live = offset < jnp.where(side == 0, ends[0, 0, 0], ends[0, 0, 1])
    for block in range(NEAR // 8):
        key_side = block * 8 // SPAN
        key_offset = sub + (block * 8) % SPAN
        key_live = key_offset < ends[0, 0, key_side]
        seen = (side == key_side) & (key_offset <= offset) & (key_live == live)
        bias[block * 8 : block * 8 + 8, :] = jnp.where(seen, 0.0, MASKED)

    def facts(box, z, slot):
        tile = boxes[box][z, LOW_TILE].astype(f32)
        tile = jnp.where(lane < UPDATE_RANK, pltpu.roll(tile, UPDATE_RANK, 1), tile)
        first, second = tile[4:5], tile[5:6]
        first_doc, second_doc = tile[6:7], tile[7:8]
        source = z * NX + lax.rem(x_own - box + NX, NX)
        low = slot < first
        high = slot < first + second
        span = jnp.where(low, source, NCH - 1 - source).astype(f32)
        doc = jnp.where(low, first_doc, second_doc)
        return jnp.where(high, span, 2.0 * NCH), doc

    def write(at, span, doc):
        seen = live & (span < own_span) & (doc == own_doc)
        bias[at : at + 8, :] = jnp.where(seen, 0.0, MASKED)

    slot = sub.astype(f32)
    for box in range(NX):
        for z in range(NZ):
            write(NEAR + box * 64 + z * 8, *facts(box, z, slot))
        for z in range(0, NZ, 2):
            span_a, doc_a = facts(box, z, slot + 8.0)
            span_b, doc_b = facts(box, z + 1, slot + 4.0)
            write(
                NEAR + 256 + box * 32 + z * 4,
                jnp.where(sub < 4, span_a, span_b),
                jnp.where(sub < 4, doc_a, doc_b),
            )


def gather_low(boxes, low_all):
    rows = [None] * (2 * NX)
    lane = lax.broadcasted_iota(jnp.int32, (NZ, 8, HD), 2)
    sub = lax.broadcasted_iota(jnp.int32, (NZ // 2, 8, HD), 1)
    for b, box in enumerate(boxes):
        tile = box[:, LOW_TILE].astype(f32)
        head = jnp.where(lane < UPDATE_RANK, tile, 0.0)
        rows[b] = head.reshape(64, HD)
        tail = jnp.where(lane < UPDATE_RANK, pltpu.roll(tile, UPDATE_RANK, 2), 0.0)
        tail = tail.reshape(NZ // 2, 2, 8, HD)
        tail = jnp.where(sub < 4, tail[:, 0], pltpu.roll(tail[:, 1], 4, 1))
        rows[NX + b] = tail.reshape(32, HD)
    low_all[...] = jnp.concatenate(rows, axis=0).T[:UPDATE_RANK].astype(bf16)


def attend_kernel(
    place, docs, ends, query, key, value, grad, up_key, up_value, box0, box1, box2, box3,
    bias, low_all, low_before,
    attended, grad_query, grad_key, grad_value, out0, out1, out2, out3, up_key_part,
    up_value_part, low_part, low_total, last,
):
    boxes = (box0, box1, box2, box3)
    outs = (out0, out1, out2, out3)
    g = pl.program_id(0)

    @pl.when(g == 0)
    def _():
        if low_before is None:
            fill_bias(place, docs, ends, boxes, bias)
            gather_low(boxes, low_all)
            low_total[...] = jnp.zeros_like(low_total)
        else:
            low_total[...] = low_before[...]

    sub = lax.broadcasted_iota(jnp.int32, (NZ // 2, 8, HD), 1)

    def stack(ref, n):
        whole = ref[:, :, n * GROUP * HD : (n + 1) * GROUP * HD].reshape(2 * SPAN, GROUP * HD)
        return jnp.concatenate(
            [whole[:, m * HD : (m + 1) * HD] for m in range(GROUP)], axis=0
        )

    def far_rows(tile):
        return [box[:, tile].astype(f32).reshape(8 * NZ, HD) for box in boxes]

    def own(ref, n):
        return ref[:, :, n * HD : (n + 1) * HD].reshape(NEAR, HD).astype(f32)

    def load(n):
        h = g * STEP + n
        extra_keys, extra_values = [], []
        for box in boxes:
            both = box[:, 2 * HEADS + h].astype(f32).reshape(NZ // 2, 2, 8, HD)
            even, odd = both[:, 0], both[:, 1]
            extra_keys.append(jnp.where(sub < 4, even, pltpu.roll(odd, 4, 1)).reshape(4 * NZ, HD))
            extra_values.append(
                jnp.where(sub < 4, pltpu.roll(even, 4, 1), odd).reshape(4 * NZ, HD)
            )
        keys = jnp.concatenate([own(key, n)] + far_rows(h) + extra_keys, axis=0)
        values = jnp.concatenate([own(value, n)] + far_rows(HEADS + h) + extra_values, axis=0)
        keys, values = keys.astype(bf16), values.astype(bf16)
        queries, grads = stack(query, n), stack(grad, n)
        return keys, values, queries, grads, grads.T

    def scored(keys, values, queries, grads, grads_t):
        return dot(keys, queries, ((1,), (1,))), dot(values, grads_t)

    def soften(scores):
        scores = scores * (SCORE_SCALE * LOG2E) + jnp.tile(bias[...], (1, GROUP))
        top = jnp.max(scores, axis=0, keepdims=True)
        weights = jnp.exp2(scores - top)
        total = jnp.sum(weights, axis=0, keepdims=True)
        return weights * (1.0 / total)

    def forward(values, exact):
        probs = exact.astype(bf16)
        return probs, dot(values.T, probs).astype(bf16)

    def backward(keys, queries, grads, grads_t, exact, probs, rounded_t, grad_probs):
        delta = jnp.sum(grads_t.astype(f32) * rounded_t.astype(f32), axis=0, keepdims=True)
        grad_scores = (exact * (grad_probs - delta)).astype(bf16)
        query_grad = (dot(keys.T, grad_scores) * SCORE_SCALE).astype(bf16).T
        key_grad = dot(grad_scores, queries) * SCORE_SCALE
        value_grad = dot(probs, grads)
        return rounded_t.T, query_grad, key_grad, value_grad

    def emit(n, summed, query_grad, key_grad, value_grad):
        for m in range(GROUP):
            at = slice(m * 2 * SPAN, (m + 1) * 2 * SPAN)
            cols = slice((n * GROUP + m) * HD, (n * GROUP + m + 1) * HD)
            attended[:, :, cols] = summed[at].reshape(2, SPAN, HD)
            grad_query[:, :, cols] = query_grad[at].reshape(2, SPAN, HD)
        cols = slice(n * HD, (n + 1) * HD)
        grad_key[:, :, cols] = key_grad[:NEAR].astype(bf16).reshape(2, SPAN, HD)
        grad_value[:, :, cols] = value_grad[:NEAR].astype(bf16).reshape(2, SPAN, HD)
        first, h = (3 if last else 0), g * STEP + n
        for b, out in enumerate(outs):
            at = NEAR + b * 64
            out[:, first, h] = key_grad[at : at + 64].reshape(NZ, 8, HD).astype(bf16)
            out[:, first + 1, h] = value_grad[at : at + 64].reshape(NZ, 8, HD).astype(bf16)
            at = NEAR + 256 + b * 32
            k = key_grad[at : at + 32].reshape(NZ // 2, 8, HD)
            v = value_grad[at : at + 32].reshape(NZ // 2, 8, HD)
            even = jnp.where(sub < 4, k, pltpu.roll(v, 4, 1)).astype(bf16)
            odd = jnp.where(sub < 4, pltpu.roll(k, 4, 1), v).astype(bf16)
            for i in range(NZ // 2):
                out[2 * i, first + 2, h] = even[i]
                out[2 * i + 1, first + 2, h] = odd[i]
        far_keys = key_grad[NEAR:].astype(bf16)
        far_values = value_grad[NEAR:].astype(bf16)
        far = jnp.concatenate([far_keys, far_values], axis=1)
        up_part = dot(low_all[...], far)
        up_key_part[:, cols] = up_part[:, :HD]
        up_value_part[:, cols] = up_part[:, HD:]
        up_both = jnp.concatenate([up_key[:, cols], up_value[:, cols]], axis=1)
        low_total[...] += dot(far, jnp.concatenate([up_both, up_both], axis=0), ((1,), (1,)))

    ns = range(STEP)
    loaded = [load(n) for n in ns]
    raw = [scored(*loaded[n]) for n in ns]
    exact, ahead = [], []
    for n in ns:
        exact.append(soften(raw[n][0]))
        ahead.append(forward(loaded[n][1], exact[n]))
    for n in ns:
        keys, values, queries, grads, grads_t = loaded[n]
        emit(n, *backward(keys, queries, grads, grads_t, exact[n], *ahead[n], raw[n][1]))

    if not last:
        return

    @pl.when(g == HEADS // STEP - 1)
    def _():
        lane = lax.broadcasted_iota(jnp.int32, (8, HD), 1)
        for b in range(NX):
            x = lax.rem(place[1] - b + NX, NX)
            for z in range(NZ):
                at = b * 64 + z * 8
                head = low_total[at : at + 8, :]
                at = 256 + b * 32 + z // 2 * 8
                tail = low_total[at : at + 8, :]
                if z % 2:
                    tail = pltpu.roll(tail, 4, 0)
                low_part[z, x] = jnp.where(lane < UPDATE_RANK, head, tail).astype(bf16)


def first_kernel(*refs):
    (place, docs, ends, query, key, value, grad, up_key, up_value, *boxes) = refs[:13]
    (attended, grad_query, grad_key, grad_value, *rest) = refs[13:]
    outs, (up_k, up_v, low_total, bias, low_all) = rest[:4], rest[4:]
    attend_kernel(
        place, docs, ends, query, key, value, grad, up_key, up_value, *boxes,
        bias, low_all, None,
        attended, grad_query, grad_key, grad_value, *outs, up_k, up_v, None, low_total, False,
    )


def second_kernel(*refs):
    (place, query, key, value, grad, up_key, up_value, *boxes) = refs[:11]
    bias, low_all, low_before = refs[11:14]
    (attended, grad_query, grad_key, grad_value, *rest) = refs[22:]
    outs, (up_k, up_v, low_part, low_total) = rest[:4], rest[4:]
    attend_kernel(
        place, None, None, query, key, value, grad, up_key, up_value, *boxes,
        bias, low_all, low_before,
        attended, grad_query, grad_key, grad_value, *outs, up_k, up_v, low_part, low_total, True,
    )


def attend(half, small, query, key, value, grad, up, boxes, carried=(), filled=()):
    at = half * HEADS // STEP
    wide = pl.BlockSpec((2, SPAN, STEP * GROUP * HD), lambda g: (0, 0, g + at))
    narrow = pl.BlockSpec((2, SPAN, STEP * HD), lambda g: (0, 0, g + at))
    whole = VMEM
    part = VMEM
    up_key = pl.BlockSpec((UPDATE_RANK, STEP * HD), lambda g: (0, g + at))
    up_value = pl.BlockSpec((UPDATE_RANK, STEP * HD), lambda g: (0, KVH // STEP + g + at))
    up_part = pl.BlockSpec((UPDATE_RANK, STEP * HD), lambda g: (0, g))
    low_part = pl.BlockSpec((NZ, NX, 8, HD), lambda g: (0, 0, 0, 0))
    wide_shape = jax.ShapeDtypeStruct((2, SPAN, QW), bf16)
    narrow_shape = jax.ShapeDtypeStruct((2, SPAN, KEY_FEATURES), bf16)
    part_shape = jax.ShapeDtypeStruct((NZ, 2 * 3, HEADS, 8, HD), bf16)
    up_shape = jax.ShapeDtypeStruct((UPDATE_RANK, HEADS * HD), f32)
    kept = [
        jax.ShapeDtypeStruct((FAR, HD), f32),
        jax.ShapeDtypeStruct((KEYS, NEAR), f32),
        jax.ShapeDtypeStruct((UPDATE_RANK, FAR), bf16),
    ]
    in_specs = [SMEM] * len(small) + [wide, narrow, narrow, wide, up_key, up_value] + [whole] * NX
    out_specs = [wide, wide, narrow, narrow] + [part] * NX + [up_part] * 2
    out_shape = [wide_shape] * 2 + [narrow_shape] * 2
    out_shape += [part_shape] * NX + [up_shape] * 2
    scratch, aliases = [], {}
    if half == 0:
        out_specs += [VMEM] * 3
        out_shape += kept
    else:
        in_specs += [VMEM] * 3 + [pl.BlockSpec(memory_space=pl.ANY)] * 4 + [VMEM] * 4
        out_specs.append(low_part)
        out_shape.append(jax.ShapeDtypeStruct((NZ, NX, 8, HD), bf16))
        scratch = [pltpu.VMEM((FAR, HD), f32)]
        aliases = {len(in_specs) - 8 + i: i for i in range(8)}
    return pl.pallas_call(
        (first_kernel, second_kernel)[half],
        grid=(HEADS // STEP,),
        in_specs=in_specs,
        out_specs=out_specs,
        out_shape=out_shape,
        scratch_shapes=scratch,
        input_output_aliases=aliases,
        compiler_params=pltpu.CompilerParams(vmem_limit_bytes=28 * 1024 * 1024),
        cost_estimate=pl.CostEstimate(
            flops=6 * 10**9, bytes_accessed=4 * 2**20, transcendentals=HEADS * KEYS * ROWS
        ),
        name=("attend_first", "attend_second")[half],
    )(*small, query, key, value, grad, up, up, *boxes, *carried, *filled)


PER_ROW = (MODEL_WIDTH + 2 * KEY_FEATURES) // HD
CHUNK = 12
CHUNKS = NX * NY
HALF = CHUNKS * CHUNK


def factor_kernel(place, counts, low_parts, state, key_a, value_a, key_b, value_b, keep, send):
    pick = selection(counts[0, 0, 0], counts[0, 0, 1])
    total = jnp.sum(low_parts[...].astype(f32), axis=0)
    compact = jnp.concatenate([total, pltpu.roll(total, UPDATE_RANK, 1)], axis=0).astype(bf16)
    low_grad = dot(pick.astype(bf16), compact, ((0,), (0,))).astype(bf16)
    down_piece = dot(low_grad, state[...], ((0,), (0,)))
    wide = MODEL_WIDTH // HD
    ups = (key_a, key_b, value_a, value_b)

    def tile(t):
        r, c = divmod(t, PER_ROW)
        rows = slice(r * 8, r * 8 + 8)
        if c < wide:
            return down_piece[rows, c * HD : (c + 1) * HD]
        which, c = divmod(c - wide, HEADS)
        return ups[which][rows, c * HD : (c + 1) * HD]

    lower = place[2] == 0
    for t in range(HALF):
        a, b = tile(t), tile(HALF + t)
        keep[t // CHUNK, t % CHUNK] = jnp.where(lower, a, b).astype(bf16)
        send[t // CHUNK, t % CHUNK] = jnp.where(lower, b, a).astype(bf16)


def factor(place, counts, low_parts, state, ups):
    return pl.pallas_call(
        factor_kernel,
        in_specs=[SMEM] * 2 + [VMEM] * 6,
        out_specs=[VMEM] * 2,
        out_shape=[jax.ShapeDtypeStruct((CHUNKS, CHUNK, 8, HD), bf16)] * 2,
        compiler_params=SMALL,
        name="factor",
    )(place, counts, low_parts, state, *ups)


def middle_kernel(pieces, *refs):
    out = refs[-1]
    chunk = jnp.sum(pieces[...].astype(f32), axis=0).astype(bf16)
    a, b, c, d = refs[:-1]
    for z in range(NZ):
        out[z, :CHUNK] = chunk
        out[z, CHUNK:] = (
            (a[z].astype(f32) + b[z].astype(f32)) + (c[z].astype(f32) + d[z].astype(f32))
        ).astype(bf16)


def middle(pieces, parts):
    return pl.pallas_call(
        middle_kernel,
        in_specs=[VMEM] * (1 + len(parts)),
        out_specs=VMEM,
        out_shape=jax.ShapeDtypeStruct((NZ, CHUNK + 2 * HALF_TILES, 8, HD), bf16),
        compiler_params=SMALL,
        name="middle",
    )(pieces, *parts)


def spread_kernel(parts, out):
    chunk = jnp.sum(parts[:, :CHUNK].astype(f32), axis=0).astype(bf16)
    for i in range(CHUNKS):
        out[i] = chunk


def spread_chunk(parts):
    return pl.pallas_call(
        spread_kernel,
        in_specs=[VMEM],
        out_specs=VMEM,
        out_shape=jax.ShapeDtypeStruct((CHUNKS, CHUNK, 8, HD), bf16),
        compiler_params=SMALL,
        name="spread_chunk",
    )(parts)


def cache_kernel(counts, parts, cache_out):
    pick = selection(counts[0, 0, 0], counts[0, 0, 1]).astype(bf16)
    total = jnp.sum(parts[:, CHUNK:].astype(f32), axis=0)
    sub = lax.broadcasted_iota(jnp.int32, (8, HD), 0)
    top_keys, top_values, rest_keys, rest_values = [], [], [], []
    for h in range(KVH):
        at = h // HEADS * HALF_TILES + h % HEADS
        top_keys.append(total[at])
        top_values.append(total[at + HEADS])
        both = total[at + 2 * HEADS]
        rest_keys.append(jnp.where(sub < 4, both, 0.0))
        rest_values.append(jnp.where(sub < 4, pltpu.roll(both, 4, 0), 0.0))
    compact = jnp.concatenate(
        [
            jnp.concatenate(top_keys + top_values, axis=1),
            jnp.concatenate(rest_keys + rest_values, axis=1),
        ],
        axis=0,
    ).astype(bf16)
    cache_out[...] = dot(pick, compact, ((0,), (0,))).astype(bf16)


def cache(counts, parts):
    return pl.pallas_call(
        cache_kernel,
        in_specs=[SMEM, VMEM],
        out_specs=VMEM,
        out_shape=jax.ShapeDtypeStruct((16, 2 * KEY_FEATURES), bf16),
        compiler_params=SMALL,
        name="cache",
    )(counts, parts)


def unpack_kernel(place, mine, other, out):
    own = pl.program_id(0) == place[2]
    for t in range(HALF):
        r, c = divmod(t, PER_ROW)
        at = t // CHUNK, t % CHUNK
        tile = jnp.where(own, mine[at].astype(f32), other[at].astype(f32))
        out[r * 8 : r * 8 + 8, c * HD : (c + 1) * HD] = tile


def unpack(place, mine, other):
    wide = MODEL_WIDTH + 2 * KEY_FEATURES
    return pl.pallas_call(
        unpack_kernel,
        grid=(NC,),
        in_specs=[SMEM] + [VMEM] * 2,
        out_specs=pl.BlockSpec((UPDATE_RANK // NC, wide), lambda half: (half, 0)),
        out_shape=jax.ShapeDtypeStruct((UPDATE_RANK, wide), f32),
        compiler_params=SMALL,
        name="unpack",
    )(place, mine, other)


def exchange(x, axes):
    return lax.all_to_all(x, axes, 0, 0, tiled=True)


def shift(x, by):
    return lax.ppermute(x, "x", [(i, (i + by) % NX) for i in range(NX)])


def swap(x):
    return lax.ppermute(x, "core", [(0, 1), (1, 0)])


def spread(column):
    return [column, shift(column, 1), shift(column, 2), shift(column, 3)]


def collect(parts):
    parts = [p.reshape(NZ, 2 * HALF_TILES, 8, HD) for p in parts]
    return [parts[0], shift(parts[1], -1), shift(parts[2], -2), shift(parts[3], -3)]


def local(
    query, key, value, beacon_slot_state, frozen_beacon_cache, adapter_down_weight,
    adapter_up_weight, output_cotangent, span_beacon_count, span_document, boundary,
):
    place = jnp.stack([lax.axis_index(axis) for axis in ("z", "x", "core")]).astype(jnp.int32)
    state = beacon_slot_state[0, 0].reshape(2 * MAX_BEACONS, MODEL_WIDTH)
    frozen = frozen_beacon_cache[0, 0].reshape(2 * MAX_BEACONS, 2 * KEY_FEATURES)

    message = project(
        span_beacon_count, span_document, state, adapter_down_weight.T, adapter_up_weight, frozen
    )
    arrays = (query[0, 0], key[0, 0], value[0, 0], output_cotangent[0, 0])
    arrays = [pltpu.with_memory_space_constraint(x, pltpu.HBM) for x in arrays]
    arrays.append(adapter_up_weight)
    column = exchange(message, "z")
    boxes_a = spread(column[:, : LOW_TILE + 1])
    boxes_b = spread(column[:, LOW_TILE + 1 :])
    first = attend(0, (place, span_document, boundary), *arrays, boxes_a)
    low_total, bias, low_all = first[10:]
    second = attend(1, (place,), *arrays, boxes_b, (bias, low_all, low_total), first[:8])
    attended, grad_query, grad_key, grad_value = second[:4]
    parts = collect(second[4:8])
    low_parts = exchange(second[10].reshape(NZ * NX, 8, HD), ("z", "x"))
    keep, send = factor(place, span_beacon_count, low_parts, state, first[8:10] + second[8:10])
    send, parts = lax.optimization_barrier((send, parts))
    pieces = (keep.astype(f32) + swap(send).astype(f32)).astype(bf16)
    both = exchange(middle(exchange(pieces, PLANE), parts), "z")
    mine = exchange(spread_chunk(both), PLANE)
    cache_gradient = cache(span_beacon_count, both)
    adapter_gradient = unpack(place, mine, swap(mine))
    return (
        attended[None, None],
        grad_query[None, None],
        grad_key[None, None],
        grad_value[None, None],
        cache_gradient.reshape(1, 1, 2, MAX_BEACONS, 2 * KEY_FEATURES),
        adapter_gradient,
    )


def solution(mesh):
    chips = Mesh(mesh.devices.reshape(NZ, NX, NY, NC), ALL_AXES)
    dp, ctx = ("y", "core"), ("z", "x")
    array5 = P(dp, ctx, None, None, None)
    array3 = P(dp, ctx, None)
    return jax.shard_map(
        local,
        mesh=chips,
        in_specs=(array5, array5, array5, array5, array5, P(), P(), array5, array3, array3, array3),
        out_specs=(array5, array5, array5, array5, array5, P()),
        check_vma=False,
    )
```
